128 devices in a mesh: row: 4 (over x), col: 32 (over y, z, core).
Axes of the slice: x: 4, y: 4, z: 4, core: 2. Of those that a mesh axis runs over, the one named last changes fastest.
Arguments:
- node_states: bfloat16 [12288, 512], P(('row', 'col')), may hold values from -6 to 6
- walk_nodes: int32 [1024, 64], P(('row', 'col')), may hold values from 0 to 12287, as said below
- walk_lengths: int32 [1024], P(('row', 'col')), may hold values from 16 to 64
- adjacency: int32 [12288, 12288], P('col', 'row'), may hold values 0 or 1
- w_xz: bfloat16 [2, 512, 2048], replicated, may hold values from -0.25 to 0.25
- w_bc: bfloat16 [2, 512, 256], replicated, may hold values from -0.25 to 0.25
- w_dt: bfloat16 [2, 512, 16], replicated, may hold values from -0.25 to 0.25
- decay_rate: float32 [2, 16], replicated, may hold values from 0.01 to 1
- w_out: bfloat16 [2, 1024, 512], replicated, may hold values from -0.1875 to 0.1875
- w_up: bfloat16 [512, 1024], replicated, may hold values from -0.25 to 0.25
- w_down: bfloat16 [1024, 512], replicated, may hold values from -0.1875 to 0.1875
Outputs:
- refreshed: bfloat16 [12288, 512], P('col')
The draws below stay inside these ranges and needn't reach their ends.
Inputs may be any that keep to these rules, and one draw needn't show every extreme that they name: `walk_nodes`: among the 8 walks of one device (aligned blocks of walks), at most 8 positions, live or not, fall on the 96 nodes held by any one device (nodes n with the same n // 96).
All inputs are finite; a program needn't handle non-finite values. No bound on the sum of `adjacency` on one device may be relied on, other than what follows from the above.
Results may differ from the reference program's by a relative error of at most 0.018.
Values may be sent and summed in bfloat16 or wider, within the bound.
No kernel may reach another device: no remote copies, remote signals or barrier semaphores. Data moves between devices by JAX's collectives and lax.ppermute only.
A program may use at most 128 MiB of HBM per device.

```python
import math
import jax
import jax.numpy as jnp
from jax import lax

D = 512
INNER = 1024
HEADS = 16
STATE = 128
GIN_HIDDEN = 1024
WALK_LEN = 64
LAYERS = 2
NODE_DEV = 96
WALK_DEV = 8
NODES = 12288
NWALKS = 1024
CAP = 8


def draw_walk_nodes(key, part):
    block_count = NWALKS // WALK_DEV
    tok_count = WALK_DEV * WALK_LEN
    owner_count = NODES // NODE_DEV
    slot_count = owner_count * CAP
    hub_owner = jax.random.randint(jax.random.fold_in(key, 7), (), 0, owner_count)

    def one_block(block_key):
        key_scores, key_order, key_local = jax.random.split(block_key, 3)
        slot_index = jnp.arange(slot_count, dtype=jnp.int32)
        owner_of = slot_index // CAP
        scores = jax.random.randint(key_scores, (slot_count,), 0, 65536) * slot_count + slot_index
        scores = jnp.where(owner_of == hub_owner, slot_index - slot_count, scores)
        chosen = jnp.argsort(scores)[:tok_count]
        owner_ids = (chosen // CAP).astype(jnp.int32)
        owner_ids = owner_ids[jax.random.permutation(key_order, tok_count)]
        local_ids = jax.random.randint(key_local, (tok_count,), 0, NODE_DEV)
        return (owner_ids * NODE_DEV + local_ids).reshape(WALK_DEV, WALK_LEN)
    block_keys = jax.random.split(jax.random.fold_in(key, 11), block_count)
    return jax.vmap(one_block)(block_keys).reshape(NWALKS, WALK_LEN).astype(jnp.int32)


def set_ends(drawn, key, low, top_value):
    extent = drawn.shape
    spot = [jax.random.randint(jax.random.fold_in(key, axis), (), 0, extent[axis]) for axis in range(len(extent))]
    drawn = drawn.at[tuple(spot)].set(low)
    longest = extent.index(max(extent))
    spot[longest] = (spot[longest] + 1) % extent[longest]
    return drawn.at[tuple(spot)].set(top_value)


def levels(rng, shape, cuts, low, top_value):
    gain, own = 1.0, jax.random.fold_in(rng, 6)
    for dim, shards_of in cuts:
        heights = jnp.exp(jax.random.uniform(jax.random.fold_in(own, dim), (shards_of,), jnp.float32, low / len(cuts), top_value / len(cuts)))
        gain = gain * jnp.repeat(heights, shape[dim] // shards_of).reshape([-1 if axis == dim else 1 for axis in range(len(shape))])
    return gain


def bell_draw(own_key, shape, scale, most, cuts=(), held_as=jnp.bfloat16):
    values = jax.random.normal(own_key, shape, jnp.float32) * scale
    if len(cuts) > 0:
        values = levels(own_key, shape, cuts, -0.22, 0.18) * values
    return jnp.clip(values, min=-most, max=most).astype(held_as)


def setup_inputs(seed: int = 0) -> dict:
    key_list = jax.random.split(jax.random.key(seed), 12)
    node_states = bell_draw(key_list[0], (NODES, D), 1.0, 6.0, ((0, 128),))
    walk_nodes = draw_walk_nodes(jax.random.fold_in(key_list[11], 71), 0)
    walk_lengths = set_ends(jax.random.randint(key_list[2], (NWALKS,), WALK_LEN // 4, WALK_LEN + 1), jax.random.fold_in(key_list[2], 1), WALK_LEN // 4, WALK_LEN).astype(jnp.int32)
    adjacency = set_ends((jax.random.randint(key_list[3], (NODES, NODES), 0, NODES) < 16).astype(jnp.int32), jax.random.fold_in(key_list[3], 1), 0, 1)
    w_xz = bell_draw(key_list[4], (LAYERS, D, 2 * INNER), D ** -0.5, 0.25)
    w_bc = bell_draw(key_list[5], (LAYERS, D, 2 * STATE), D ** -0.5, 0.25)
    w_dt = bell_draw(key_list[6], (LAYERS, D, HEADS), D ** -0.5, 0.25)
    decay_rate = jnp.clip(jnp.exp(jax.random.uniform(key_list[7], (LAYERS, HEADS), jnp.float32, math.log(0.01), math.log(1.0))), 0.01, 1.0)
    w_out = bell_draw(key_list[8], (LAYERS, INNER, D), INNER ** -0.5, 0.1875)
    w_up = bell_draw(key_list[9], (D, GIN_HIDDEN), D ** -0.5, 0.25)
    w_down = bell_draw(key_list[10], (GIN_HIDDEN, D), GIN_HIDDEN ** -0.5, 0.1875)
    return {"node_states": node_states, "walk_nodes": walk_nodes, "walk_lengths": walk_lengths, "adjacency": adjacency, "w_xz": w_xz, "w_bc": w_bc, "w_dt": w_dt, "decay_rate": decay_rate, "w_out": w_out, "w_up": w_up, "w_down": w_down}


def encode_walks(first, live, w_xz, w_bc, w_dt, decay_rate, w_out):
    walk_count, walk_len, width = first.shape
    inner_width = w_out.shape[1]
    heads = w_dt.shape[2]
    state_width = w_bc.shape[2] // 2
    head_width = inner_width // heads
    live_mask = live.astype(jnp.float32)
    position_ids = jnp.arange(walk_len, dtype=jnp.int32)
    forward_tri = position_ids[:, None] >= position_ids[None, :]
    backward_tri = position_ids[:, None] <= position_ids[None, :]
    stream = first.reshape(walk_count * walk_len, width)
    for layer_index in range(w_xz.shape[0]):
        widened = stream.astype(jnp.float32)
        normed = (widened * lax.rsqrt(lax.optimization_barrier(jnp.mean(widened * widened, axis=-1, keepdims=True)) + 1e-05)).astype(jnp.bfloat16)
        both = jnp.dot(normed, w_xz[layer_index], preferred_element_type=jnp.float32)
        inner = both[:, :inner_width].astype(jnp.bfloat16).reshape(walk_count, walk_len, heads, head_width)
        gate = both[:, inner_width:]
        proj = jnp.dot(normed, w_bc[layer_index], preferred_element_type=jnp.float32).astype(jnp.bfloat16)
        proj = proj.reshape(walk_count, walk_len, 2 * state_width)
        b_input = proj[..., :state_width]
        c_output = proj[..., state_width:]
        step_size = jax.nn.softplus(jnp.dot(normed, w_dt[layer_index], preferred_element_type=jnp.float32))
        step_size = step_size.reshape(walk_count, walk_len, heads)
        log_decay = -decay_rate[layer_index][None, None, :] * step_size
        running = jnp.transpose(jnp.cumsum(log_decay, axis=1), (0, 2, 1))
        before = running - jnp.transpose(log_decay, (0, 2, 1))
        forward_gap = running[:, :, :, None] - running[:, :, None, :]
        backward_gap = before[:, :, None, :] - before[:, :, :, None]
        decay_mat = jnp.where(forward_tri, jnp.exp(jnp.minimum(forward_gap, 0.0)), 0.0)
        decay_mat = decay_mat + jnp.where(backward_tri, jnp.exp(jnp.minimum(backward_gap, 0.0)), 0.0)
        scores = jnp.einsum('wtk,wsk->wts', c_output.astype(jnp.float32), b_input.astype(jnp.float32)) * state_width ** (-0.5)
        source = jnp.transpose(step_size * live_mask[:, :, None], (0, 2, 1))
        mix = (scores[:, None, :, :] * decay_mat * source[:, :, None, :]).astype(jnp.bfloat16)
        mixed = jnp.einsum('whts,wshp->wthp', mix.astype(jnp.float32), inner.astype(jnp.float32))
        mixed = mixed.reshape(walk_count * walk_len, inner_width)
        gated = (mixed * jax.nn.silu(gate)).astype(jnp.bfloat16)
        stream = (widened + jnp.dot(gated, w_out[layer_index], preferred_element_type=jnp.float32)).astype(jnp.bfloat16)
    return stream

def finish_nodes(combined, w_up, w_down):
    centred = combined - lax.optimization_barrier(jnp.mean(combined, axis=-1, keepdims=True))
    normal = centred * lax.rsqrt(lax.optimization_barrier(jnp.mean(centred * centred, axis=-1, keepdims=True)) + 1e-05)
    hidden = jax.nn.gelu(jnp.dot(normal.astype(jnp.bfloat16), w_up, preferred_element_type=jnp.float32)).astype(jnp.bfloat16)
    return (normal + jnp.dot(hidden, w_down, preferred_element_type=jnp.float32)).astype(jnp.bfloat16)

def reference(node_states, walk_nodes, walk_lengths, adjacency, w_xz, w_bc, w_dt, decay_rate, w_out, w_up, w_down):
    position_ids = jnp.arange(WALK_LEN, dtype=jnp.int32)
    live = position_ids[None, :] < walk_lengths[:, None]
    first = jnp.where(live[:, :, None], node_states[walk_nodes], jnp.zeros((), jnp.bfloat16)).astype(jnp.bfloat16)
    block_count = NWALKS // WALK_DEV

    def encode_block(pair):
        return encode_walks(pair[0], pair[1], w_xz, w_bc, w_dt, decay_rate, w_out)
    encoded = lax.map(encode_block, (first.reshape(block_count, WALK_DEV, WALK_LEN, D), live.reshape(block_count, WALK_DEV, WALK_LEN)))
    encoded = encoded.reshape(NWALKS * WALK_LEN, D)
    flat_nodes = walk_nodes.reshape(-1)
    flat_live = live.reshape(-1)
    values = jnp.where(flat_live[:, None], encoded.astype(jnp.float32), 0.0)
    visit_sum = jax.ops.segment_sum(values, flat_nodes, num_segments=NODES)
    visit_count = jax.ops.segment_sum(flat_live.astype(jnp.float32), flat_nodes, num_segments=NODES)
    update = (node_states.astype(jnp.float32) + visit_sum / (1.0 + visit_count)[:, None]).astype(jnp.bfloat16)

    def neighbour_block(rows):
        return jnp.dot(rows.astype(jnp.bfloat16), update, preferred_element_type=jnp.float32)
    neighbours = lax.map(neighbour_block, adjacency.reshape(NODES // NODE_DEV, NODE_DEV, NODES)).reshape(NODES, D)
    combined = update.astype(jnp.float32) + neighbours
    return finish_nodes(combined, w_up, w_down)
```

```python
import functools

import jax
import jax.numpy as jnp
from jax import lax
from jax.experimental import pallas as pl
from jax.experimental.pallas import tpu as pltpu
from jax.sharding import PartitionSpec as P

F32 = jnp.float32
BF16 = jnp.bfloat16
I32 = jnp.int32
VMEM_SPEC = pl.BlockSpec(memory_space=pltpu.VMEM)
SMEM_SPEC = pl.BlockSpec(memory_space=pltpu.SMEM)
CAP = 8
EPS = 1e-05


def iota(shape, dim):
    return lax.broadcasted_iota(I32, shape, dim)


def mm(a, b):
    return jnp.dot(a, b, preferred_element_type=F32)


def mm_nt(a, b):
    return lax.dot_general(a, b, (((1,), (1,)), ((), ())), preferred_element_type=F32)


def onehot(cond):
    return cond.astype(F32).astype(BF16)


def as_column(row):
    return jnp.transpose(jnp.broadcast_to(row, (8, row.shape[1])))[:, 0:1]


def route_kernel(nodes_ref, lengths_ref, wanted_ref, slots_ref, *, node_count, owners):
    walk_count, walk_len = nodes_ref.shape
    tok = walk_count * walk_len
    place = iota((1, walk_len), 1)
    pieces = []
    for w in range(walk_count):
        live = place < lengths_ref[w]
        pieces.append(jnp.where(live, nodes_ref[w : w + 1, :], -1))
    node_row = jnp.concatenate(pieces, axis=1)
    live_row = node_row >= 0
    owner_row = ((node_row.astype(F32) + 0.5) * (1.0 / node_count)).astype(I32)
    local_row = node_row - owner_row * node_count
    owner_row = jnp.where(live_row, owner_row, -1)
    local_row = jnp.where(live_row, local_row + 1, 0)
    owner_col = as_column(owner_row)
    local_col = as_column(local_row)
    same = owner_col == owner_row
    first_i = iota((tok, tok), 0)
    second_i = iota((tok, tok), 1)
    rank_row = jnp.sum(jnp.where(same & (first_i < second_i), 1.0, 0.0), axis=0, keepdims=True)
    rank_row = rank_row.astype(I32)
    rank_col = as_column(rank_row)
    slot_row = jnp.where(live_row, owner_row * CAP + rank_row, -1)
    slots_ref[...] = jnp.broadcast_to(slot_row, slots_ref.shape)
    by_owner = onehot(iota((owners, tok), 0) == owner_row)
    by_rank = jnp.where(iota((tok, 128), 1) == rank_col, local_col.astype(F32), 0.0).astype(BF16)
    wanted = mm(by_owner, by_rank).astype(I32) - 1
    wanted_ref[...] = wanted[:, :CAP]


def route(walk_nodes, walk_lengths, node_count, owners):
    tok = walk_nodes.shape[0] * walk_nodes.shape[1]
    return pl.pallas_call(
        functools.partial(route_kernel, node_count=node_count, owners=owners),
        out_shape=(
            jax.ShapeDtypeStruct((owners, CAP), I32),
            jax.ShapeDtypeStruct((8, tok), I32),
        ),
        in_specs=[VMEM_SPEC, SMEM_SPEC],
        out_specs=(VMEM_SPEC, VMEM_SPEC),
        name="route",
    )(walk_nodes, walk_lengths)


def pick_kernel(requests_ref, states_ref, picked_ref, reqrow_ref):
    owners = requests_ref.shape[0]
    node_count = states_ref.shape[0]
    total = owners * CAP
    spread = onehot(iota((total, owners), 0) // CAP == iota((total, owners), 1))
    wide = mm(spread, requests_ref[...].astype(F32).astype(BF16))
    mine = iota((total, CAP), 1) == iota((total, CAP), 0) % CAP
    col = jnp.sum(jnp.where(mine, wide, 0.0), axis=1, keepdims=True).astype(I32)
    chosen = onehot(iota((total, node_count), 1) == col)
    picked_ref[...] = mm(chosen, states_ref[...]).astype(BF16)
    reqrow_ref[...] = jnp.transpose(jnp.broadcast_to(col, (total, 8)))


def pick(requests, node_states):
    total = requests.shape[0] * CAP
    return pl.pallas_call(
        pick_kernel,
        out_shape=(
            jax.ShapeDtypeStruct((total, node_states.shape[1]), BF16),
            jax.ShapeDtypeStruct((8, total), I32),
        ),
        in_specs=[VMEM_SPEC, VMEM_SPEC],
        out_specs=(VMEM_SPEC, VMEM_SPEC),
        name="pick",
    )(requests, node_states)


def encode_kernel(
    arrived_ref,
    slots_ref,
    w_xz_ref,
    w_bc_ref,
    w_dt_ref,
    rate_ref,
    w_out_ref,
    out_ref,
    stream_ref,
    inner_ref,
    gate_ref,
    proj_ref,
    gated_ref,
    cum_ref,
    before_ref,
    rows_ref,
    *,
    walk_len,
):
    layers, inner_width, width = w_out_ref.shape
    heads = w_dt_ref.shape[2]
    head_width = inner_width // heads
    state_width = w_bc_ref.shape[2] // 2
    total = arrived_ref.shape[0]
    tok = slots_ref.shape[1]
    pairs = inner_width // 128
    walk_pairs = tok // (2 * walk_len)
    copies = 128 // heads

    slot_row = slots_ref[0:1, :]
    slot_col = as_column(slot_row)
    take = onehot(iota((tok, total), 1) == slot_col)
    stream_ref[...] = mm(take, arrived_ref[...])

    live_col = slot_col >= 0
    place = iota((tok, 128), 0) % walk_len
    part = iota((tok, 128), 1) // heads
    spread_heads = onehot(iota((128, inner_width), 0) % heads == iota((128, inner_width), 1) // head_width)
    tile_heads = iota((heads, 128), 0) == iota((heads, 128), 1) % heads
    lane = iota((walk_len, 128), 1)
    left = lane < walk_len
    left_row = iota((1, 128), 1) < walk_len
    t_of = iota((walk_len, 128), 0)
    s_of = lane % walk_len
    earlier = s_of < t_of
    diagonal = jnp.where(s_of == t_of, 1.0, 0.0)
    left_bf = jnp.where(left, 1.0, 0.0).astype(BF16)
    right_bf = jnp.where(left, 0.0, 1.0).astype(BF16)

    def split3(v):
        high = v.astype(BF16).astype(F32)
        rest = v - high
        middle = rest.astype(BF16).astype(F32)
        low = rest - middle
        return jnp.where(part == 0, high, jnp.where(part == 1, middle, jnp.where(part == 2, low, 0.0))).astype(BF16)

    for layer in range(layers):
        x = stream_ref[...]
        normed = (x * lax.rsqrt(jnp.mean(x * x, axis=-1, keepdims=True) + EPS)).astype(BF16)
        inner_ref[...] = mm(normed, w_xz_ref[layer, :, :inner_width]).astype(BF16)
        gate_ref[...] = mm(normed, w_xz_ref[layer, :, inner_width:])
        proj_ref[...] = mm(normed, w_bc_ref[layer]).astype(BF16)
        w_dt_tiled = mm(w_dt_ref[layer], onehot(tile_heads)).astype(BF16)
        raw = mm(normed, w_dt_tiled)
        step = jnp.maximum(raw, 0.0) + jnp.log1p(jnp.exp(-jnp.abs(raw)))
        rate = jnp.dot(
            rate_ref[layer : layer + 1, :],
            tile_heads.astype(F32),
            precision=lax.Precision.HIGHEST,
            preferred_element_type=F32,
        )
        cum = -rate * step
        shift = 1
        while shift < walk_len:
            cum = cum + jnp.where(place >= shift, pltpu.roll(cum, shift, 0), 0.0)
            shift *= 2
        before = jnp.where(place >= 1, pltpu.roll(cum, 1, 0), 0.0)
        source = jnp.where(live_col, step, 0.0)
        cum_ref[...] = mm(split3(cum), spread_heads)
        before_ref[...] = mm(split3(before), spread_heads)
        for q, v in enumerate((cum, before, source)):
            flipped = jnp.transpose(v)[:heads, :]
            rows_ref[2 * q] = flipped
            for j in range(walk_pairs):
                rows_ref[2 * q + 1, :, 128 * j : 128 * (j + 1)] = pltpu.roll(
                    flipped[:, 128 * j : 128 * (j + 1)], walk_len, 1
                )

        def pair_body(j, carry):
            lanes = pl.ds(pl.multiple_of(j * 128, 128), 128)
            for odd in range(2):
                rows = pl.ds(pl.multiple_of((2 * j + odd) * walk_len, walk_len), walk_len)
                both = proj_ref[rows, :]
                b_in = both[:, :state_width]
                c_out = both[:, state_width:]
                scores = mm_nt(c_out, jnp.concatenate([b_in, b_in], axis=0)) * state_width ** (-0.5)
                for p in range(pairs):
                    cols = slice(128 * p, 128 * (p + 1))

                    def row_of(q):
                        a = rows_ref[2 * q + odd, 2 * p : 2 * p + 1, lanes]
                        b = rows_ref[2 * q + 1 - odd, 2 * p + 1 : 2 * p + 2, lanes]
                        return jnp.where(left_row, a, b)

                    gap = jnp.where(
                        earlier, cum_ref[rows, cols] - row_of(0), row_of(1) - before_ref[rows, cols]
                    )
                    decay = jnp.exp(jnp.minimum(gap, 0.0)) + diagonal
                    mix = (scores * decay * row_of(2)).astype(BF16)
                    inner = inner_ref[rows, cols]
                    split = jnp.concatenate([inner * left_bf, inner * right_bf], axis=0)
                    mixed = mm(mix, split)
                    gate = gate_ref[rows, cols]
                    gated_ref[rows, cols] = (mixed * (gate * jax.nn.sigmoid(gate))).astype(BF16)
            return carry

        lax.fori_loop(0, walk_pairs, pair_body, 0)
        stream = x + mm(gated_ref[...], w_out_ref[layer])
        stream_ref[...] = stream.astype(BF16).astype(F32)

    put = onehot(iota((total, tok), 0) == slot_row)
    out_ref[...] = mm(put, stream_ref[...].astype(BF16)).astype(BF16)


def encode(arrived, slots, w_xz, w_bc, w_dt, decay_rate, w_out, walk_len):
    total, width = arrived.shape
    tok = slots.shape[1]
    inner_width = w_out.shape[1]
    heads = w_dt.shape[2]
    return pl.pallas_call(
        functools.partial(encode_kernel, walk_len=walk_len),
        out_shape=jax.ShapeDtypeStruct((total, width), BF16),
        in_specs=[VMEM_SPEC] * 7,
        out_specs=VMEM_SPEC,
        scratch_shapes=[
            pltpu.VMEM((tok, width), F32),
            pltpu.VMEM((tok, inner_width), BF16),
            pltpu.VMEM((tok, inner_width), F32),
            pltpu.VMEM((tok, w_bc.shape[2]), BF16),
            pltpu.VMEM((tok, inner_width), BF16),
            pltpu.VMEM((tok, inner_width), F32),
            pltpu.VMEM((tok, inner_width), F32),
            pltpu.VMEM((6, heads, tok), F32),
        ],
        name="encode",
    )(arrived, slots, w_xz, w_bc, w_dt, decay_rate, w_out)


def update_kernel(returned_ref, reqrow_ref, states_ref, out_ref):
    node_count = states_ref.shape[0]
    total = returned_ref.shape[0]
    member = jnp.where(iota((node_count, total), 0) == reqrow_ref[0:1, :], 1.0, 0.0)
    visits = jnp.sum(member, axis=1, keepdims=True)
    summed = mm(member.astype(BF16), returned_ref[...])
    out_ref[...] = (states_ref[...].astype(F32) + summed / (1.0 + visits)).astype(BF16)


def update_nodes(returned, reqrow, node_states):
    return pl.pallas_call(
        update_kernel,
        out_shape=jax.ShapeDtypeStruct(node_states.shape, BF16),
        in_specs=[VMEM_SPEC] * 3,
        out_specs=VMEM_SPEC,
        name="update",
    )(returned, reqrow, node_states)


def finish_kernel(own_ref, one_ref, two_ref, three_ref, w_up_ref, w_down_ref, out_ref):
    combined = (own_ref[...] + one_ref[...].astype(F32)) + (
        two_ref[...].astype(F32) + three_ref[...].astype(F32)
    )
    centred = combined - jnp.mean(combined, axis=-1, keepdims=True)
    normal = centred * lax.rsqrt(jnp.mean(centred * centred, axis=-1, keepdims=True) + EPS)
    hidden = jax.nn.gelu(mm(normal.astype(BF16), w_up_ref[...])).astype(BF16)
    out_ref[...] = (normal + mm(hidden, w_down_ref[...])).astype(BF16)


def finish(own, parts, w_up, w_down):
    return pl.pallas_call(
        finish_kernel,
        out_shape=jax.ShapeDtypeStruct(own.shape, BF16),
        in_specs=[VMEM_SPEC] * 6,
        out_specs=VMEM_SPEC,
        name="finish",
    )(own, *parts, w_up, w_down)


def ring(size, distance):
    return [(i, (i + distance) % size) for i in range(size)]


def per_device(
    node_states,
    walk_nodes,
    walk_lengths,
    adjacency,
    w_xz,
    w_bc,
    w_dt,
    decay_rate,
    w_out,
    w_up,
    w_down,
):
    node_count, width = node_states.shape
    walk_count, walk_len = walk_nodes.shape
    everyone = ("row", "col")
    owners = lax.axis_size(everyone)
    row_size = lax.axis_size("row")
    row_block = adjacency.shape[0]

    wanted, slots = route(walk_nodes, walk_lengths, node_count, owners)
    requests = lax.all_to_all(wanted, everyone, split_axis=0, concat_axis=0, tiled=True)
    picked, reqrow = pick(requests, node_states)
    arrived = lax.all_to_all(
        picked.reshape(owners, CAP, width), everyone, split_axis=0, concat_axis=0, tiled=True
    )
    outgoing = encode(
        arrived.reshape(owners * CAP, width), slots, w_xz, w_bc, w_dt, decay_rate, w_out, walk_len
    )
    returned = lax.all_to_all(
        outgoing.reshape(owners, CAP, width), everyone, split_axis=0, concat_axis=0, tiled=True
    )
    update = update_nodes(returned.reshape(owners * CAP, width), reqrow, node_states)

    my_row = lax.axis_index("row")
    row_global = lax.axis_index("col") * row_block + jnp.arange(row_block, dtype=I32)
    col_global = my_row * adjacency.shape[1] + jnp.arange(adjacency.shape[1], dtype=I32)
    self_link = (row_global[:, None] == col_global[None, :]).astype(I32)
    links = (adjacency + self_link).astype(BF16)
    piece = lax.all_gather(update, "col", axis=0, tiled=True)
    sums = jnp.dot(links, piece, preferred_element_type=F32)

    part = row_block // row_size

    def block_for(distance):
        return lax.dynamic_slice_in_dim(sums, ((my_row + distance) % row_size) * part, part, axis=0)

    parts = [
        lax.ppermute(block_for(d).astype(BF16), "row", ring(row_size, d)) for d in range(1, row_size)
    ]
    done = finish(block_for(0), parts, w_up, w_down)
    result = jnp.zeros((row_block, width), BF16)
    result = lax.dynamic_update_slice_in_dim(result, done, my_row * part, axis=0)
    for d in range(1, row_size):
        moved = lax.ppermute(done, "row", ring(row_size, d))
        result = lax.dynamic_update_slice_in_dim(
            result, moved, ((my_row - d) % row_size) * part, axis=0
        )
    return result


def solution(mesh):
    return jax.shard_map(
        per_device,
        mesh=mesh,
        in_specs=(
            P(("row", "col"), None),
            P(("row", "col"), None),
            P(("row", "col")),
            P("col", "row"),
            P(),
            P(),
            P(),
            P(),
            P(),
            P(),
            P(),
        ),
        out_specs=P("col", None),
        check_vma=False,
    )
```

```python
import functools

import jax
import jax.numpy as jnp
from jax import lax
from jax.experimental import pallas as pl
from jax.experimental.pallas import tpu as pltpu
from jax.sharding import PartitionSpec as P

F32 = jnp.float32
BF16 = jnp.bfloat16
I32 = jnp.int32
VMEM_SPEC = pl.BlockSpec(memory_space=pltpu.VMEM)
SMEM_SPEC = pl.BlockSpec(memory_space=pltpu.SMEM)
CAP = 8
EPS = 1e-05
SIDE = 4
CORES = 2


def iota(shape, dim):
    return lax.broadcasted_iota(I32, shape, dim)


def mm(a, b):
    return jnp.dot(a, b, preferred_element_type=F32)


def mm_nt(a, b):
    return lax.dot_general(a, b, (((1,), (1,)), ((), ())), preferred_element_type=F32)


def onehot(cond):
    return cond.astype(F32).astype(BF16)


def as_column(row):
    return jnp.transpose(jnp.broadcast_to(row, (8, row.shape[1])))[:, 0:1]


def route_kernel(nodes_ref, lengths_ref, wanted_ref, slots_ref, *, node_count, owners):
    walk_count, walk_len = nodes_ref.shape
    tok = walk_count * walk_len
    place = iota((1, walk_len), 1)
    pieces = []
    for w in range(walk_count):
        live = place < lengths_ref[w]
        pieces.append(jnp.where(live, nodes_ref[w : w + 1, :], -1))
    node_row = jnp.concatenate(pieces, axis=1)
    live_row = node_row >= 0
    owner_row = ((node_row.astype(F32) + 0.5) * (1.0 / node_count)).astype(I32)
    local_row = node_row - owner_row * node_count
    owner_row = jnp.where(live_row, owner_row, -1)
    local_row = jnp.where(live_row, local_row + 1, 0)
    owner_col = as_column(owner_row)
    local_col = as_column(local_row)
    same = owner_col == owner_row
    first_i = iota((tok, tok), 0)
    second_i = iota((tok, tok), 1)
    rank_row = jnp.sum(jnp.where(same & (first_i < second_i), 1.0, 0.0), axis=0, keepdims=True)
    rank_row = rank_row.astype(I32)
    rank_col = as_column(rank_row)
    slot_row = jnp.where(live_row, owner_row * CAP + rank_row, -1)
    slots_ref[...] = jnp.broadcast_to(slot_row, slots_ref.shape)
    by_owner = onehot(iota((owners, tok), 0) == owner_row)
    by_rank = jnp.where(iota((tok, 128), 1) == rank_col, local_col.astype(F32), 0.0).astype(BF16)
    wanted = mm(by_owner, by_rank).astype(I32) - 1
    wanted_ref[...] = wanted[:, :CAP]


def route(walk_nodes, walk_lengths, node_count, owners):
    tok = walk_nodes.shape[0] * walk_nodes.shape[1]
    return pl.pallas_call(
        functools.partial(route_kernel, node_count=node_count, owners=owners),
        out_shape=(
            jax.ShapeDtypeStruct((owners, CAP), I32),
            jax.ShapeDtypeStruct((8, tok), I32),
        ),
        in_specs=[VMEM_SPEC, SMEM_SPEC],
        out_specs=(VMEM_SPEC, VMEM_SPEC),
        name="route",
    )(walk_nodes, walk_lengths)


def pick_kernel(requests_ref, states_ref, picked_ref, reqrow_ref):
    owners = requests_ref.shape[0]
    node_count = states_ref.shape[0]
    total = owners * CAP
    spread = onehot(iota((total, owners), 0) // CAP == iota((total, owners), 1))
    wide = mm(spread, requests_ref[...].astype(F32).astype(BF16))
    mine = iota((total, CAP), 1) == iota((total, CAP), 0) % CAP
    col = jnp.sum(jnp.where(mine, wide, 0.0), axis=1, keepdims=True).astype(I32)
    chosen = onehot(iota((total, node_count), 1) == col)
    picked_ref[...] = mm(chosen, states_ref[...]).astype(BF16)
    reqrow_ref[...] = jnp.transpose(jnp.broadcast_to(col, (total, 8)))


def pick(requests, node_states):
    total = requests.shape[0] * CAP
    return pl.pallas_call(
        pick_kernel,
        out_shape=(
            jax.ShapeDtypeStruct((total, node_states.shape[1]), BF16),
            jax.ShapeDtypeStruct((8, total), I32),
        ),
        in_specs=[VMEM_SPEC, VMEM_SPEC],
        out_specs=(VMEM_SPEC, VMEM_SPEC),
        name="pick",
    )(requests, node_states)


def encode_kernel(
    arrived_ref,
    slots_ref,
    w_xz_ref,
    w_bc_ref,
    w_dt_ref,
    rate_ref,
    w_out_ref,
    out_ref,
    stream_ref,
    inner_ref,
    gate_ref,
    proj_ref,
    gated_ref,
    cum_ref,
    before_ref,
    rows_ref,
    *,
    walk_len,
):
    layers, inner_width, width = w_out_ref.shape
    heads = w_dt_ref.shape[2]
    head_width = inner_width // heads
    state_width = w_bc_ref.shape[2] // 2
    total = arrived_ref.shape[0]
    tok = slots_ref.shape[1]
    pairs = inner_width // 128
    walk_pairs = tok // (2 * walk_len)
    copies = 128 // heads

    slot_row = slots_ref[0:1, :]
    slot_col = as_column(slot_row)
    take = onehot(iota((tok, total), 1) == slot_col)
    stream_ref[...] = mm(take, arrived_ref[...])

    live_col = slot_col >= 0
    place = iota((tok, 128), 0) % walk_len
    part = iota((tok, 128), 1) // heads
    spread_heads = onehot(iota((128, inner_width), 0) % heads == iota((128, inner_width), 1) // head_width)
    tile_heads = iota((heads, 128), 0) == iota((heads, 128), 1) % heads
    lane = iota((walk_len, 128), 1)
    left = lane < walk_len
    left_row = iota((1, 128), 1) < walk_len
    t_of = iota((walk_len, 128), 0)
    s_of = lane % walk_len
    earlier = s_of < t_of
    diagonal = jnp.where(s_of == t_of, 1.0, 0.0)
    left_bf = jnp.where(left, 1.0, 0.0).astype(BF16)
    right_bf = jnp.where(left, 0.0, 1.0).astype(BF16)

    def split3(v):
        high = v.astype(BF16).astype(F32)
        rest = v - high
        middle = rest.astype(BF16).astype(F32)
        low = rest - middle
        return jnp.where(part == 0, high, jnp.where(part == 1, middle, jnp.where(part == 2, low, 0.0))).astype(BF16)

    for layer in range(layers):
        x = stream_ref[...]
        normed = (x * lax.rsqrt(jnp.mean(x * x, axis=-1, keepdims=True) + EPS)).astype(BF16)
        inner_ref[...] = mm(normed, w_xz_ref[layer, :, :inner_width]).astype(BF16)
        gate_ref[...] = mm(normed, w_xz_ref[layer, :, inner_width:])
        proj_ref[...] = mm(normed, w_bc_ref[layer]).astype(BF16)
        w_dt_tiled = mm(w_dt_ref[layer], onehot(tile_heads)).astype(BF16)
        raw = mm(normed, w_dt_tiled)
        step = jnp.maximum(raw, 0.0) + jnp.log1p(jnp.exp(-jnp.abs(raw)))
        rate = jnp.dot(
            rate_ref[layer : layer + 1, :],
            tile_heads.astype(F32),
            precision=lax.Precision.HIGHEST,
            preferred_element_type=F32,
        )
        cum = -rate * step
        shift = 1
        while shift < walk_len:
            cum = cum + jnp.where(place >= shift, pltpu.roll(cum, shift, 0), 0.0)
            shift *= 2
        before = jnp.where(place >= 1, pltpu.roll(cum, 1, 0), 0.0)
        source = jnp.where(live_col, step, 0.0)
        cum_ref[...] = mm(split3(cum), spread_heads)
        before_ref[...] = mm(split3(before), spread_heads)
        for q, v in enumerate((cum, before, source)):
            flipped = jnp.transpose(v)[:heads, :]
            rows_ref[2 * q] = flipped
            for j in range(walk_pairs):
                rows_ref[2 * q + 1, :, 128 * j : 128 * (j + 1)] = pltpu.roll(
                    flipped[:, 128 * j : 128 * (j + 1)], walk_len, 1
                )

        def pair_body(j, carry):
            lanes = pl.ds(pl.multiple_of(j * 128, 128), 128)
            for odd in range(2):
                rows = pl.ds(pl.multiple_of((2 * j + odd) * walk_len, walk_len), walk_len)
                both = proj_ref[rows, :]
                b_in = both[:, :state_width]
                c_out = both[:, state_width:]
                scores = mm_nt(c_out, jnp.concatenate([b_in, b_in], axis=0)) * state_width ** (-0.5)
                for p in range(pairs):
                    cols = slice(128 * p, 128 * (p + 1))

                    def row_of(q):
                        a = rows_ref[2 * q + odd, 2 * p : 2 * p + 1, lanes]
                        b = rows_ref[2 * q + 1 - odd, 2 * p + 1 : 2 * p + 2, lanes]
                        return jnp.where(left_row, a, b)

                    gap = jnp.where(
                        earlier, cum_ref[rows, cols] - row_of(0), row_of(1) - before_ref[rows, cols]
                    )
                    decay = jnp.exp(jnp.minimum(gap, 0.0)) + diagonal
                    mix = (scores * decay * row_of(2)).astype(BF16)
                    inner = inner_ref[rows, cols]
                    split = jnp.concatenate([inner * left_bf, inner * right_bf], axis=0)
                    mixed = mm(mix, split)
                    gate = gate_ref[rows, cols]
                    gated_ref[rows, cols] = (mixed * (gate * jax.nn.sigmoid(gate))).astype(BF16)
            return carry

        lax.fori_loop(0, walk_pairs, pair_body, 0)
        stream = x + mm(gated_ref[...], w_out_ref[layer])
        stream_ref[...] = stream.astype(BF16).astype(F32)

    put = onehot(iota((total, tok), 0) == slot_row)
    out_ref[...] = mm(put, stream_ref[...].astype(BF16)).astype(BF16)


def encode(arrived, slots, w_xz, w_bc, w_dt, decay_rate, w_out, walk_len):
    total, width = arrived.shape
    tok = slots.shape[1]
    inner_width = w_out.shape[1]
    heads = w_dt.shape[2]
    return pl.pallas_call(
        functools.partial(encode_kernel, walk_len=walk_len),
        out_shape=jax.ShapeDtypeStruct((total, width), BF16),
        in_specs=[VMEM_SPEC] * 7,
        out_specs=VMEM_SPEC,
        scratch_shapes=[
            pltpu.VMEM((tok, width), F32),
            pltpu.VMEM((tok, inner_width), BF16),
            pltpu.VMEM((tok, inner_width), F32),
            pltpu.VMEM((tok, w_bc.shape[2]), BF16),
            pltpu.VMEM((tok, inner_width), BF16),
            pltpu.VMEM((tok, inner_width), F32),
            pltpu.VMEM((tok, inner_width), F32),
            pltpu.VMEM((6, heads, tok), F32),
        ],
        name="encode",
    )(arrived, slots, w_xz, w_bc, w_dt, decay_rate, w_out)


def update_kernel(returned_ref, reqrow_ref, states_ref, out_ref):
    node_count = states_ref.shape[0]
    total = returned_ref.shape[0]
    member = jnp.where(iota((node_count, total), 0) == reqrow_ref[0:1, :], 1.0, 0.0)
    visits = jnp.sum(member, axis=1, keepdims=True)
    summed = mm(member.astype(BF16), returned_ref[...])
    out_ref[...] = (states_ref[...].astype(F32) + summed / (1.0 + visits)).astype(BF16)


def update_nodes(returned, reqrow, node_states):
    return pl.pallas_call(
        update_kernel,
        out_shape=jax.ShapeDtypeStruct(node_states.shape, BF16),
        in_specs=[VMEM_SPEC] * 3,
        out_specs=VMEM_SPEC,
        name="update",
    )(returned, reqrow, node_states)


def finish_kernel(own_ref, one_ref, two_ref, three_ref, w_up_ref, w_down_ref, out_ref):
    combined = (own_ref[...] + one_ref[...].astype(F32)) + (
        two_ref[...].astype(F32) + three_ref[...].astype(F32)
    )
    centred = combined - jnp.mean(combined, axis=-1, keepdims=True)
    normal = centred * lax.rsqrt(jnp.mean(centred * centred, axis=-1, keepdims=True) + EPS)
    hidden = jax.nn.gelu(mm(normal.astype(BF16), w_up_ref[...])).astype(BF16)
    out_ref[...] = (normal + mm(hidden, w_down_ref[...])).astype(BF16)


def finish(own, parts, w_up, w_down):
    return pl.pallas_call(
        finish_kernel,
        out_shape=jax.ShapeDtypeStruct(own.shape, BF16),
        in_specs=[VMEM_SPEC] * 6,
        out_specs=VMEM_SPEC,
        name="finish",
    )(own, *parts, w_up, w_down)


def neighbour_kernel(
    place_ref, links_ref, mine_ref, other_ref, own_ref, one_ref, two_ref, three_ref, piece_ref, sums_ref
):
    my_row, y, z, core = place_ref[0], place_ref[1], place_ref[2], place_ref[3]
    half_rows = mine_ref.shape[0] // (2 * SIDE * SIDE)
    for half in range(2):
        for e in range(SIDE):
            for d in range(SIDE):
                dy, dz = (d, e) if half == 0 else (e, d)
                source = ((half * SIDE + e) * SIDE + d) * half_rows
                device = ((y + SIDE - dy) % SIDE * SIDE + (z + SIDE - dz) % SIDE) * CORES
                for ref, who in ((mine_ref, core), (other_ref, 1 - core)):
                    target = pl.multiple_of(((device + who) * 2 + half) * half_rows, half_rows)
                    piece_ref[pl.ds(target, half_rows), :] = ref[source : source + half_rows, :]
    sums_ref[...] = mm(links_ref[...], piece_ref[...])
    part = own_ref.shape[0]

    def block(distance):
        start = pl.multiple_of((my_row + distance) % SIDE * part, part)
        return sums_ref[pl.ds(start, part), :]

    own_ref[...] = block(0)
    one_ref[...] = block(1).astype(BF16)
    two_ref[...] = block(2).astype(BF16)
    three_ref[...] = block(3).astype(BF16)


def neighbour_sums(place, links, mine, other):
    row_block, width = links.shape[0], mine.shape[1]
    part = row_block // SIDE
    sent = jax.ShapeDtypeStruct((part, width), BF16)
    return pl.pallas_call(
        neighbour_kernel,
        out_shape=(jax.ShapeDtypeStruct((part, width), F32), sent, sent, sent),
        in_specs=[SMEM_SPEC] + [VMEM_SPEC] * 3,
        out_specs=(VMEM_SPEC,) * 4,
        scratch_shapes=[
            pltpu.VMEM((links.shape[1], width), BF16),
            pltpu.VMEM((row_block, width), F32),
        ],
        name="neighbours",
    )(place, links, mine, other)


def along(value, dy=0, dz=0, dc=0):
    pairs = []
    for y in range(SIDE):
        for z in range(SIDE):
            for c in range(CORES):
                to = ((y + dy) % SIDE * SIDE + (z + dz) % SIDE) * CORES + (c + dc) % CORES
                pairs.append(((y * SIDE + z) * CORES + c, to))
    return lax.ppermute(value, "col", pairs)


def gather_half(value, axis):
    moved = [along(value, **{axis: d}) for d in range(1, SIDE)]
    return jnp.concatenate([value] + moved, axis=0)


def gather_blocks(update):
    half = update.shape[0] // 2
    first = gather_half(update[:half], "dy")
    second = gather_half(update[half:], "dz")
    first = gather_half(first, "dz")
    second = gather_half(second, "dy")
    mine = jnp.concatenate([first, second], axis=0)
    return mine, along(mine, dc=1)


def ring(size, distance):
    return [(i, (i + distance) % size) for i in range(size)]


def per_device(
    node_states,
    walk_nodes,
    walk_lengths,
    adjacency,
    w_xz,
    w_bc,
    w_dt,
    decay_rate,
    w_out,
    w_up,
    w_down,
):
    node_count, width = node_states.shape
    walk_count, walk_len = walk_nodes.shape
    everyone = ("row", "col")
    owners = lax.axis_size(everyone)
    row_size = lax.axis_size("row")
    row_block = adjacency.shape[0]

    wanted, slots = route(walk_nodes, walk_lengths, node_count, owners)
    requests = lax.all_to_all(wanted, everyone, split_axis=0, concat_axis=0, tiled=True)
    picked, reqrow = pick(requests, node_states)
    arrived = lax.all_to_all(
        picked.reshape(owners, CAP, width), everyone, split_axis=0, concat_axis=0, tiled=True
    )
    outgoing = encode(
        arrived.reshape(owners * CAP, width), slots, w_xz, w_bc, w_dt, decay_rate, w_out, walk_len
    )
    returned = lax.all_to_all(
        outgoing.reshape(owners, CAP, width), everyone, split_axis=0, concat_axis=0, tiled=True
    )
    update = update_nodes(returned.reshape(owners * CAP, width), reqrow, node_states)

    my_row = lax.axis_index("row")
    row_global = lax.axis_index("col") * row_block + jnp.arange(row_block, dtype=I32)
    col_global = my_row * adjacency.shape[1] + jnp.arange(adjacency.shape[1], dtype=I32)
    self_link = (row_global[:, None] == col_global[None, :]).astype(I32)
    links = (adjacency + self_link).astype(BF16)
    mine, other = gather_blocks(update)
    my_col = lax.axis_index("col")
    place = jnp.stack([my_row, my_col // (SIDE * CORES), my_col // CORES % SIDE, my_col % CORES])
    own, *sent = neighbour_sums(place.astype(I32), links, mine, other)
    parts = [lax.ppermute(block, "row", ring(row_size, d)) for d, block in enumerate(sent, 1)]
    part = row_block // row_size
    done = finish(own, parts, w_up, w_down)
    result = jnp.zeros((row_block, width), BF16)
    result = lax.dynamic_update_slice_in_dim(result, done, my_row * part, axis=0)
    for d in range(1, row_size):
        moved = lax.ppermute(done, "row", ring(row_size, d))
        result = lax.dynamic_update_slice_in_dim(
            result, moved, ((my_row - d) % row_size) * part, axis=0
        )
    return result


def solution(mesh):
    return jax.shard_map(
        per_device,
        mesh=mesh,
        in_specs=(
            P(("row", "col"), None),
            P(("row", "col"), None),
            P(("row", "col")),
            P("col", "row"),
            P(),
            P(),
            P(),
            P(),
            P(),
            P(),
            P(),
        ),
        out_specs=P("col", None),
        check_vma=False,
    )
```

```python
import functools

import jax
import jax.numpy as jnp
from jax import lax
from jax.experimental import pallas as pl
from jax.experimental.pallas import tpu as pltpu
from jax.sharding import PartitionSpec as P

F32 = jnp.float32
BF16 = jnp.bfloat16
I32 = jnp.int32
VMEM_SPEC = pl.BlockSpec(memory_space=pltpu.VMEM)
HBM_SPEC = pl.BlockSpec(memory_space=pltpu.HBM)
SMEM_SPEC = pl.BlockSpec(memory_space=pltpu.SMEM)
CAP = 8
EPS = 1e-05
SIDE = 4
CORES = 2


def iota(shape, dim):
    return lax.broadcasted_iota(I32, shape, dim)


def mm(a, b):
    return jnp.dot(a, b, preferred_element_type=F32)


def mm_nt(a, b):
    return lax.dot_general(a, b, (((1,), (1,)), ((), ())), preferred_element_type=F32)


def near_core(*arrays):
    return [pltpu.with_memory_space_constraint(a, pltpu.VMEM) for a in arrays]


def in_hbm(*arrays):
    return [pltpu.with_memory_space_constraint(a, pltpu.HBM) for a in arrays]


def onehot(cond):
    return cond.astype(F32).astype(BF16)


def as_column(row):
    return jnp.transpose(jnp.broadcast_to(row, (8, row.shape[1])))[:, 0:1]


def route_kernel(nodes_ref, lengths_ref, wanted_ref, slots_ref, *, node_count, owners):
    walk_count, walk_len = nodes_ref.shape
    tok = walk_count * walk_len
    place = iota((1, walk_len), 1)
    pieces = []
    for w in range(walk_count):
        live = place < lengths_ref[w]
        pieces.append(jnp.where(live, nodes_ref[w : w + 1, :], -1))
    node_row = jnp.concatenate(pieces, axis=1)
    live_row = node_row >= 0
    owner_row = ((node_row.astype(F32) + 0.5) * (1.0 / node_count)).astype(I32)
    local_row = node_row - owner_row * node_count
    owner_row = jnp.where(live_row, owner_row, -1)
    local_row = jnp.where(live_row, local_row + 1, 0)
    owner_col = as_column(owner_row)
    local_col = as_column(local_row)
    same = owner_col == owner_row
    first_i = iota((tok, tok), 0)
    second_i = iota((tok, tok), 1)
    rank_row = jnp.sum(jnp.where(same & (first_i < second_i), 1.0, 0.0), axis=0, keepdims=True)
    rank_row = rank_row.astype(I32)
    rank_col = as_column(rank_row)
    slot_row = jnp.where(live_row, owner_row * CAP + rank_row, -1)
    slots_ref[...] = jnp.broadcast_to(slot_row, slots_ref.shape)
    by_owner = onehot(iota((owners, tok), 0) == owner_row)
    by_rank = jnp.where(iota((tok, 128), 1) == rank_col, local_col.astype(F32), 0.0).astype(BF16)
    wanted = mm(by_owner, by_rank).astype(I32) - 1
    wanted_ref[...] = wanted[:, :CAP]


def route(walk_nodes, walk_lengths, node_count, owners):
    tok = walk_nodes.shape[0] * walk_nodes.shape[1]
    return pl.pallas_call(
        functools.partial(route_kernel, node_count=node_count, owners=owners),
        out_shape=(
            jax.ShapeDtypeStruct((owners, CAP), I32),
            jax.ShapeDtypeStruct((8, tok), I32),
        ),
        in_specs=[VMEM_SPEC, SMEM_SPEC],
        out_specs=(VMEM_SPEC, VMEM_SPEC),
        name="route",
        compiler_params=pltpu.CompilerParams(vmem_limit_bytes=12 << 20),
    )(walk_nodes, walk_lengths)


def pick_kernel(requests_ref, states_ref, picked_ref, reqrow_ref):
    owners = requests_ref.shape[0]
    node_count = states_ref.shape[0]
    total = owners * CAP
    spread = onehot(iota((total, owners), 0) // CAP == iota((total, owners), 1))
    wide = mm(spread, requests_ref[...].astype(F32).astype(BF16))
    mine = iota((total, CAP), 1) == iota((total, CAP), 0) % CAP
    col = jnp.sum(jnp.where(mine, wide, 0.0), axis=1, keepdims=True).astype(I32)
    chosen = onehot(iota((total, node_count), 1) == col)
    picked_ref[...] = mm(chosen, states_ref[...]).astype(BF16)
    reqrow_ref[...] = jnp.transpose(jnp.broadcast_to(col, (total, 8)))


def pick(requests, node_states):
    total = requests.shape[0] * CAP
    return pl.pallas_call(
        pick_kernel,
        out_shape=(
            jax.ShapeDtypeStruct((total, node_states.shape[1]), BF16),
            jax.ShapeDtypeStruct((8, total), I32),
        ),
        in_specs=[VMEM_SPEC, VMEM_SPEC],
        out_specs=(VMEM_SPEC, VMEM_SPEC),
        name="pick",
        compiler_params=pltpu.CompilerParams(vmem_limit_bytes=12 << 20),
    )(*near_core(requests, node_states))


def encode_kernel(
    arrived_ref,
    slots_ref,
    w_dt_ref,
    rate_ref,
    w_xz_hbm,
    w_bc_hbm,
    w_out_hbm,
    out_ref,
    w_xz_ref,
    w_bc_ref,
    w_out_ref,
    weights_sem,
    stream_ref,
    inner_ref,
    gate_ref,
    proj_ref,
    gated_ref,
    cum_ref,
    before_ref,
    rows_ref,
    *,
    walk_len,
):
    layers, inner_width, width = w_out_ref.shape
    heads = w_dt_ref.shape[2]
    head_width = inner_width // heads
    state_width = w_bc_ref.shape[2] // 2
    total = arrived_ref.shape[0]
    tok = slots_ref.shape[1]
    pairs = inner_width // 128
    walk_pairs = tok // (2 * walk_len)
    loads = []
    for layer in range(layers):
        for q, (source, target) in enumerate(
            ((w_xz_hbm, w_xz_ref), (w_bc_hbm, w_bc_ref), (w_out_hbm, w_out_ref))
        ):
            load = pltpu.make_async_copy(source.at[layer], target.at[layer], weights_sem.at[layer, q])
            load.start()
            loads.append(load)

    slot_row = slots_ref[0:1, :]
    slot_col = as_column(slot_row)
    take = onehot(iota((tok, total), 1) == slot_col)
    stream_ref[...] = mm(take, arrived_ref[...])

    live_col = slot_col >= 0
    place = iota((tok, 128), 0) % walk_len
    part = iota((tok, 128), 1) // heads
    spread_heads = onehot(iota((128, inner_width), 0) % heads == iota((128, inner_width), 1) // head_width)
    tile_heads = iota((heads, 128), 0) == iota((heads, 128), 1) % heads
    lane = iota((walk_len, 128), 1)
    left = lane < walk_len
    left_row = iota((1, 128), 1) < walk_len
    t_of = iota((walk_len, 128), 0)
    s_of = lane % walk_len
    earlier = s_of < t_of
    diagonal = jnp.where(s_of == t_of, 1.0, 0.0)
    left_bf = jnp.where(left, 1.0, 0.0).astype(BF16)
    right_bf = jnp.where(left, 0.0, 1.0).astype(BF16)

    def split3(v):
        high = v.astype(BF16).astype(F32)
        rest = v - high
        middle = rest.astype(BF16).astype(F32)
        low = rest - middle
        return jnp.where(part == 0, high, jnp.where(part == 1, middle, jnp.where(part == 2, low, 0.0))).astype(BF16)

    for layer in range(layers):
        x = stream_ref[...]
        normed = (x * lax.rsqrt(jnp.mean(x * x, axis=-1, keepdims=True) + EPS)).astype(BF16)
        loads[3 * layer].wait()
        inner_ref[...] = mm(normed, w_xz_ref[layer, :, :inner_width]).astype(BF16)
        gate_ref[...] = mm(normed, w_xz_ref[layer, :, inner_width:])
        loads[3 * layer + 1].wait()
        proj_ref[...] = mm(normed, w_bc_ref[layer]).astype(BF16)
        w_dt_tiled = mm(w_dt_ref[layer], onehot(tile_heads)).astype(BF16)
        raw = mm(normed, w_dt_tiled)
        step = jnp.maximum(raw, 0.0) + jnp.log1p(jnp.exp(-jnp.abs(raw)))
        rate = jnp.dot(
            rate_ref[layer : layer + 1, :],
            tile_heads.astype(F32),
            precision=lax.Precision.HIGHEST,
            preferred_element_type=F32,
        )
        cum = -rate * step
        shift = 1
        while shift < walk_len:
            cum = cum + jnp.where(place >= shift, pltpu.roll(cum, shift, 0), 0.0)
            shift *= 2
        before = jnp.where(place >= 1, pltpu.roll(cum, 1, 0), 0.0)
        source = jnp.where(live_col, step, 0.0)
        cum_ref[...] = mm(split3(cum), spread_heads)
        before_ref[...] = mm(split3(before), spread_heads)
        for q, v in enumerate((cum, before, source)):
            flipped = jnp.transpose(v)[:heads, :]
            rows_ref[2 * q] = flipped
            for j in range(walk_pairs):
                rows_ref[2 * q + 1, :, 128 * j : 128 * (j + 1)] = pltpu.roll(
                    flipped[:, 128 * j : 128 * (j + 1)], walk_len, 1
                )

        def pair_body(j, carry):
            lanes = pl.ds(pl.multiple_of(j * 128, 128), 128)
            for odd in range(2):
                rows = pl.ds(pl.multiple_of((2 * j + odd) * walk_len, walk_len), walk_len)
                both = proj_ref[rows, :]
                b_in = both[:, :state_width]
                c_out = both[:, state_width:]
                scores = mm_nt(c_out, jnp.concatenate([b_in, b_in], axis=0)) * state_width ** (-0.5)
                for p in range(pairs):
                    cols = slice(128 * p, 128 * (p + 1))

                    def row_of(q):
                        a = rows_ref[2 * q + odd, 2 * p : 2 * p + 1, lanes]
                        b = rows_ref[2 * q + 1 - odd, 2 * p + 1 : 2 * p + 2, lanes]
                        return jnp.where(left_row, a, b)

                    gap = jnp.where(
                        earlier, cum_ref[rows, cols] - row_of(0), row_of(1) - before_ref[rows, cols]
                    )
                    decay = jnp.exp(jnp.minimum(gap, 0.0)) + diagonal
                    mix = (scores * decay * row_of(2)).astype(BF16)
                    inner = inner_ref[rows, cols]
                    split = jnp.concatenate([inner * left_bf, inner * right_bf], axis=0)
                    mixed = mm(mix, split)
                    gate = gate_ref[rows, cols]
                    gated_ref[rows, cols] = (mixed * (gate * jax.nn.sigmoid(gate))).astype(BF16)
            return carry

        lax.fori_loop(0, walk_pairs, pair_body, 0)
        loads[3 * layer + 2].wait()
        stream = x + mm(gated_ref[...], w_out_ref[layer])
        stream_ref[...] = stream.astype(BF16).astype(F32)

    put = onehot(iota((total, tok), 0) == slot_row)
    out_ref[...] = mm(put, stream_ref[...].astype(BF16)).astype(BF16)


def encode(arrived, slots, w_xz, w_bc, w_dt, decay_rate, w_out, walk_len):
    total, width = arrived.shape
    tok = slots.shape[1]
    inner_width = w_out.shape[1]
    heads = w_dt.shape[2]
    return pl.pallas_call(
        functools.partial(encode_kernel, walk_len=walk_len),
        out_shape=jax.ShapeDtypeStruct((total, width), BF16),
        in_specs=[VMEM_SPEC] * 4 + [HBM_SPEC] * 3,
        out_specs=VMEM_SPEC,
        scratch_shapes=[
            pltpu.VMEM(w_xz.shape, BF16),
            pltpu.VMEM(w_bc.shape, BF16),
            pltpu.VMEM(w_out.shape, BF16),
            pltpu.SemaphoreType.DMA((w_out.shape[0], 3)),
            pltpu.VMEM((tok, width), F32),
            pltpu.VMEM((tok, inner_width), BF16),
            pltpu.VMEM((tok, inner_width), F32),
            pltpu.VMEM((tok, w_bc.shape[2]), BF16),
            pltpu.VMEM((tok, inner_width), BF16),
            pltpu.VMEM((tok, inner_width), F32),
            pltpu.VMEM((tok, inner_width), F32),
            pltpu.VMEM((6, heads, tok), F32),
        ],
        name="encode",
        compiler_params=pltpu.CompilerParams(vmem_limit_bytes=40 << 20),
    )(*near_core(arrived, slots, w_dt, decay_rate), *in_hbm(w_xz, w_bc, w_out))


def update_kernel(returned_ref, reqrow_ref, states_ref, out_ref):
    node_count = states_ref.shape[0]
    total = returned_ref.shape[0]
    member = jnp.where(iota((node_count, total), 0) == reqrow_ref[0:1, :], 1.0, 0.0)
    visits = jnp.sum(member, axis=1, keepdims=True)
    summed = mm(member.astype(BF16), returned_ref[...])
    out_ref[...] = (states_ref[...].astype(F32) + summed / (1.0 + visits)).astype(BF16)


def update_nodes(returned, reqrow, node_states):
    return pl.pallas_call(
        update_kernel,
        out_shape=jax.ShapeDtypeStruct(node_states.shape, BF16),
        in_specs=[VMEM_SPEC] * 3,
        out_specs=VMEM_SPEC,
        name="update",
        compiler_params=pltpu.CompilerParams(vmem_limit_bytes=12 << 20),
    )(*near_core(returned, reqrow, node_states))


def finish_kernel(
    own_ref, one_ref, two_ref, three_ref, w_up_hbm, w_down_hbm, out_ref, w_up_ref, w_down_ref, weights_sem
):
    up = pltpu.make_async_copy(w_up_hbm, w_up_ref, weights_sem.at[0])
    down = pltpu.make_async_copy(w_down_hbm, w_down_ref, weights_sem.at[1])
    up.start()
    down.start()
    combined = (own_ref[...] + one_ref[...].astype(F32)) + (
        two_ref[...].astype(F32) + three_ref[...].astype(F32)
    )
    centred = combined - jnp.mean(combined, axis=-1, keepdims=True)
    normal = centred * lax.rsqrt(jnp.mean(centred * centred, axis=-1, keepdims=True) + EPS)
    up.wait()
    hidden = jax.nn.gelu(mm(normal.astype(BF16), w_up_ref[...])).astype(BF16)
    down.wait()
    out_ref[...] = (normal + mm(hidden, w_down_ref[...])).astype(BF16)


def finish(own, parts, w_up, w_down):
    return pl.pallas_call(
        finish_kernel,
        out_shape=jax.ShapeDtypeStruct(own.shape, BF16),
        in_specs=[VMEM_SPEC] * 4 + [HBM_SPEC] * 2,
        out_specs=VMEM_SPEC,
        scratch_shapes=[
            pltpu.VMEM(w_up.shape, BF16),
            pltpu.VMEM(w_down.shape, BF16),
            pltpu.SemaphoreType.DMA((2,)),
        ],
        name="finish",
        compiler_params=pltpu.CompilerParams(vmem_limit_bytes=12 << 20),
    )(own, *near_core(*parts), *in_hbm(w_up, w_down))


def neighbour_kernel(place_ref, links_ref, *refs):
    mine, other = refs[:SIDE], refs[SIDE : 2 * SIDE]
    own_ref, one_ref, two_ref, three_ref, piece_ref, sums_ref = refs[2 * SIDE :]
    my_row, y, z, core = place_ref[0], place_ref[1], place_ref[2], place_ref[3]
    rows = mine[0].shape[0] // SIDE
    for e in range(SIDE):
        for d in range(SIDE):
            for ref, who in ((mine[e], core), (other[e], 1 - core)):
                dy = d + who * (e - d)
                dz = e + who * (d - e)
                device = ((y + SIDE - dy) % SIDE * SIDE + (z + SIDE - dz) % SIDE) * CORES + who
                target = pl.multiple_of(device * rows, rows)
                piece_ref[pl.ds(target, rows), :] = ref[d * rows : (d + 1) * rows, :]
    sums_ref[...] = mm(links_ref[...], piece_ref[...])
    part = own_ref.shape[0]

    def block(distance):
        start = pl.multiple_of((my_row + distance) % SIDE * part, part)
        return sums_ref[pl.ds(start, part), :]

    own_ref[...] = block(0)
    one_ref[...] = block(1).astype(BF16)
    two_ref[...] = block(2).astype(BF16)
    three_ref[...] = block(3).astype(BF16)


def neighbour_sums(place, links, mine, other):
    row_block, width = links.shape[0], mine[0].shape[1]
    part = row_block // SIDE
    sent = jax.ShapeDtypeStruct((part, width), BF16)
    return pl.pallas_call(
        neighbour_kernel,
        out_shape=(jax.ShapeDtypeStruct((part, width), F32), sent, sent, sent),
        in_specs=[SMEM_SPEC] + [VMEM_SPEC] * (1 + 2 * SIDE),
        out_specs=(VMEM_SPEC,) * 4,
        scratch_shapes=[
            pltpu.VMEM((links.shape[1], width), BF16),
            pltpu.VMEM((row_block, width), F32),
        ],
        name="neighbours",
        compiler_params=pltpu.CompilerParams(vmem_limit_bytes=16 << 20),
    )(place, *near_core(links, *mine, *other))


def shifted(value, first, second, swap=0):
    pairs = []
    for y in range(SIDE):
        for z in range(SIDE):
            for c in range(CORES):
                dy, dz = (first, second) if c == 0 else (second, first)
                to = ((y + dy) % SIDE * SIDE + (z + dz) % SIDE) * CORES + (c + swap) % CORES
                pairs.append(((y * SIDE + z) * CORES + c, to))
    return lax.ppermute(value, "col", pairs)


def gather_blocks(update):
    near = [update] + [shifted(update, d, 0) for d in range(1, SIDE)]
    near = jnp.concatenate(near, axis=0)
    far = [near] + [shifted(near, 0, d) for d in range(1, SIDE)]
    return far, [shifted(block, 0, 0, swap=1) for block in far]


def assemble_kernel(place_ref, *refs):
    blocks, out_ref = refs[:-1], refs[-1]
    part = blocks[0].shape[0]
    for d, block_ref in enumerate(blocks):
        start = pl.multiple_of((place_ref[0] + len(blocks) - d) % len(blocks) * part, part)
        out_ref[pl.ds(start, part), :] = block_ref[...]


def assemble(place, done, moved):
    rows, width = done.shape
    return pl.pallas_call(
        assemble_kernel,
        out_shape=jax.ShapeDtypeStruct((rows * (1 + len(moved)), width), BF16),
        in_specs=[SMEM_SPEC] + [VMEM_SPEC] * (1 + len(moved)),
        out_specs=VMEM_SPEC,
        name="assemble",
        compiler_params=pltpu.CompilerParams(vmem_limit_bytes=8 << 20),
    )(place, *near_core(done, *moved))


def ring(size, distance):
    return [(i, (i + distance) % size) for i in range(size)]


def per_device(
    node_states,
    walk_nodes,
    walk_lengths,
    adjacency,
    w_xz,
    w_bc,
    w_dt,
    decay_rate,
    w_out,
    w_up,
    w_down,
):
    node_count, width = node_states.shape
    walk_count, walk_len = walk_nodes.shape
    everyone = ("row", "col")
    owners = lax.axis_size(everyone)
    row_size = lax.axis_size("row")
    row_block = adjacency.shape[0]

    my_row = lax.axis_index("row")
    row_global = lax.axis_index("col") * row_block + jnp.arange(row_block, dtype=I32)
    col_global = my_row * adjacency.shape[1] + jnp.arange(adjacency.shape[1], dtype=I32)
    self_link = (row_global[:, None] == col_global[None, :]).astype(I32)
    links = (adjacency + self_link).astype(BF16)
    wanted, slots = route(walk_nodes, walk_lengths, node_count, owners)
    requests = lax.all_to_all(wanted, everyone, split_axis=0, concat_axis=0, tiled=True)
    picked, reqrow = pick(requests, node_states)
    arrived = lax.all_to_all(
        picked.reshape(owners, CAP, width), everyone, split_axis=0, concat_axis=0, tiled=True
    )
    arrived, links = lax.optimization_barrier((arrived, links))
    outgoing = encode(
        arrived.reshape(owners * CAP, width), slots, w_xz, w_bc, w_dt, decay_rate, w_out, walk_len
    )
    returned = lax.all_to_all(
        outgoing.reshape(owners, CAP, width), everyone, split_axis=0, concat_axis=0, tiled=True
    )
    update = update_nodes(returned.reshape(owners * CAP, width), reqrow, node_states)

    mine, other = gather_blocks(update)
    my_col = lax.axis_index("col")
    place = jnp.stack([my_row, my_col // (SIDE * CORES), my_col // CORES % SIDE, my_col % CORES]).astype(I32)
    own, *sent = neighbour_sums(place, links, mine, other)
    parts = [lax.ppermute(block, "row", ring(row_size, d)) for d, block in enumerate(sent, 1)]
    done = finish(own, parts, w_up, w_down)
    moved = [lax.ppermute(done, "row", ring(row_size, d)) for d in range(1, row_size)]
    return assemble(place, done, moved)


def solution(mesh):
    return jax.shard_map(
        per_device,
        mesh=mesh,
        in_specs=(
            P(("row", "col"), None),
            P(("row", "col"), None),
            P(("row", "col")),
            P("col", "row"),
            P(),
            P(),
            P(),
            P(),
            P(),
            P(),
            P(),
        ),
        out_specs=P("col", None),
        check_vma=False,
    )
```

```python
import functools

import jax
import jax.numpy as jnp
from jax import lax
from jax.experimental import pallas as pl
from jax.experimental.pallas import tpu as pltpu
from jax.sharding import PartitionSpec as P

F32 = jnp.float32
BF16 = jnp.bfloat16
I32 = jnp.int32
VMEM_SPEC = pl.BlockSpec(memory_space=pltpu.VMEM)
HBM_SPEC = pl.BlockSpec(memory_space=pltpu.HBM)
SMEM_SPEC = pl.BlockSpec(memory_space=pltpu.SMEM)
CAP = 8
EPS = 1e-05
LOG2E = 1.4426950408889634
SIDE = 4
CORES = 2


def iota(shape, dim):
    return lax.broadcasted_iota(I32, shape, dim)


def mm(a, b):
    return jnp.dot(a, b, preferred_element_type=F32)


def mm_nt(a, b):
    return lax.dot_general(a, b, (((1,), (1,)), ((), ())), preferred_element_type=F32)


def near_core(*arrays):
    return [pltpu.with_memory_space_constraint(a, pltpu.VMEM) for a in arrays]


def in_hbm(*arrays):
    return [pltpu.with_memory_space_constraint(a, pltpu.HBM) for a in arrays]


def onehot(cond):
    return cond.astype(F32).astype(BF16)


def as_column(row):
    return jnp.transpose(jnp.broadcast_to(row, (8, row.shape[1])))[:, 0:1]


def route_kernel(
    nodes_hbm, lengths_hbm, wanted_ref, slots_ref, nodes_ref, lengths_ref, load_sem, *, node_count, owners
):
    load_nodes = pltpu.make_async_copy(nodes_hbm, nodes_ref, load_sem.at[0])
    load_lengths = pltpu.make_async_copy(lengths_hbm, lengths_ref, load_sem.at[1])
    load_nodes.start()
    load_lengths.start()
    load_nodes.wait()
    load_lengths.wait()
    walk_count, walk_len = nodes_ref.shape
    tok = walk_count * walk_len
    place = iota((1, walk_len), 1)
    pieces = []
    for w in range(walk_count):
        live = place < lengths_ref[w]
        pieces.append(jnp.where(live, nodes_ref[w : w + 1, :], -1))
    node_row = jnp.concatenate(pieces, axis=1)
    live_row = node_row >= 0
    owner_row = ((node_row.astype(F32) + 0.5) * (1.0 / node_count)).astype(I32)
    local_row = node_row - owner_row * node_count
    owner_row = jnp.where(live_row, owner_row, -1)
    local_row = jnp.where(live_row, local_row + 1, 0)
    owner_col = as_column(owner_row)
    local_col = as_column(local_row)
    same = owner_col == owner_row
    first_i = iota((tok, tok), 0)
    second_i = iota((tok, tok), 1)
    rank_row = jnp.sum(jnp.where(same & (first_i < second_i), 1.0, 0.0), axis=0, keepdims=True)
    rank_row = rank_row.astype(I32)
    rank_col = as_column(rank_row)
    slot_row = jnp.where(live_row, owner_row * CAP + rank_row, -1)
    slots_ref[...] = jnp.broadcast_to(slot_row, slots_ref.shape)
    by_owner = onehot(iota((owners, tok), 0) == owner_row)
    by_rank = jnp.where(iota((tok, 128), 1) == rank_col, local_col.astype(F32), 0.0).astype(BF16)
    wanted = mm(by_owner, by_rank).astype(I32) - 1
    wanted_ref[...] = wanted[:, :CAP]


def route(walk_nodes, walk_lengths, node_count, owners):
    tok = walk_nodes.shape[0] * walk_nodes.shape[1]
    return pl.pallas_call(
        functools.partial(route_kernel, node_count=node_count, owners=owners),
        out_shape=(
            jax.ShapeDtypeStruct((owners, CAP), I32),
            jax.ShapeDtypeStruct((8, tok), I32),
        ),
        in_specs=[HBM_SPEC, HBM_SPEC],
        out_specs=(VMEM_SPEC, VMEM_SPEC),
        scratch_shapes=[
            pltpu.VMEM(walk_nodes.shape, I32),
            pltpu.SMEM(walk_lengths.shape, I32),
            pltpu.SemaphoreType.DMA((2,)),
        ],
        name="route",
        compiler_params=pltpu.CompilerParams(vmem_limit_bytes=12 << 20),
    )(*in_hbm(walk_nodes, walk_lengths))


def pick_kernel(requests_ref, states_hbm, picked_ref, reqrow_ref, states_ref, load_sem):
    load = pltpu.make_async_copy(states_hbm, states_ref, load_sem)
    load.start()
    owners = requests_ref.shape[0]
    node_count = states_ref.shape[0]
    total = owners * CAP
    spread = onehot(iota((total, owners), 0) // CAP == iota((total, owners), 1))
    wide = mm(spread, requests_ref[...].astype(F32).astype(BF16))
    mine = iota((total, CAP), 1) == iota((total, CAP), 0) % CAP
    col = jnp.sum(jnp.where(mine, wide, 0.0), axis=1, keepdims=True).astype(I32)
    chosen = onehot(iota((total, node_count), 1) == col)
    reqrow_ref[...] = jnp.transpose(jnp.broadcast_to(col, (total, 8)))
    load.wait()
    picked_ref[...] = mm(chosen, states_ref[...]).astype(BF16)


def pick(requests, node_states):
    total = requests.shape[0] * CAP
    return pl.pallas_call(
        pick_kernel,
        out_shape=(
            jax.ShapeDtypeStruct((total, node_states.shape[1]), BF16),
            jax.ShapeDtypeStruct((8, total), I32),
        ),
        in_specs=[VMEM_SPEC, HBM_SPEC],
        out_specs=(VMEM_SPEC, VMEM_SPEC),
        scratch_shapes=[pltpu.VMEM(node_states.shape, BF16), pltpu.SemaphoreType.DMA(())],
        name="pick",
        compiler_params=pltpu.CompilerParams(vmem_limit_bytes=12 << 20),
    )(*near_core(requests), *in_hbm(node_states))


def encode_kernel(
    arrived_ref,
    slots_ref,
    w_dt_ref,
    rate_ref,
    w_xz_hbm,
    w_bc_hbm,
    w_out_hbm,
    out_ref,
    w_xz_ref,
    w_bc_ref,
    w_out_ref,
    weights_sem,
    stream_ref,
    inner_ref,
    gate_ref,
    proj_ref,
    gated_ref,
    cum_ref,
    before_ref,
    rows_ref,
    *,
    walk_len,
):
    layers, inner_width, width = w_out_ref.shape
    heads = w_dt_ref.shape[1]
    head_width = inner_width // heads
    state_width = w_bc_ref.shape[2] // 2
    total = arrived_ref.shape[0]
    tok = slots_ref.shape[1]
    quads = inner_width // 256
    walk_pairs = tok // (2 * walk_len)

    loads = []
    for layer in range(layers):
        for q, (source, target) in enumerate(
            ((w_xz_hbm, w_xz_ref), (w_bc_hbm, w_bc_ref), (w_out_hbm, w_out_ref))
        ):
            load = pltpu.make_async_copy(source.at[layer], target.at[layer], weights_sem.at[layer, q])
            load.start()
            loads.append(load)

    slot_row = slots_ref[0:1, :]
    slot_col = as_column(slot_row)
    take = onehot(iota((tok, total), 1) == slot_col)
    stream_ref[...] = mm(take, arrived_ref[...])

    live_row = slot_row >= 0
    place = iota((heads, tok), 1) % walk_len
    spread_in = iota((6 * heads, inner_width), 0)
    spread_out = iota((6 * heads, inner_width), 1)
    same_head = spread_in % heads == spread_out // head_width
    spread_cum = onehot(same_head & (spread_in < 3 * heads))
    spread_before = onehot(same_head & (spread_in >= 3 * heads))
    lane = iota((walk_len, 128), 1)
    left = lane < walk_len
    left_row = iota((1, 128), 1) < walk_len
    t_of = iota((walk_len, 128), 0)
    s_of = lane % walk_len
    earlier = s_of < t_of
    diagonal = jnp.where(s_of == t_of, 1.0, 0.0)
    left_bf = jnp.where(left, 1.0, 0.0).astype(BF16)
    right_bf = jnp.where(left, 0.0, 1.0).astype(BF16)
    nothing = jnp.zeros((walk_len, 128), BF16)

    def split3(v):
        high = v.astype(BF16).astype(F32)
        rest = v - high
        middle = rest.astype(BF16).astype(F32)
        return [high, middle, rest - middle]

    for layer in range(layers):
        x = stream_ref[...]
        normed = (x * lax.rsqrt(jnp.mean(x * x, axis=-1, keepdims=True) + EPS)).astype(BF16)
        raw = mm_nt(w_dt_ref[layer], normed)
        step = jnp.maximum(raw, 0.0) + jnp.log1p(jnp.exp(-jnp.abs(raw)))
        rate = as_column(rate_ref[layer : layer + 1, :])
        cum = (-LOG2E * rate) * step
        shift = 1
        while shift < walk_len:
            cum = cum + jnp.where(place >= shift, pltpu.roll(cum, shift, 1), 0.0)
            shift *= 2
        before = jnp.where(place >= 1, pltpu.roll(cum, 1, 1), 0.0)
        source = jnp.where(live_row, step, 0.0)
        for q, v in enumerate((cum, before, source)):
            rows_ref[2 * q] = v
            for j in range(walk_pairs):
                rows_ref[2 * q + 1, :, 128 * j : 128 * (j + 1)] = pltpu.roll(
                    v[:, 128 * j : 128 * (j + 1)], walk_len, 1
                )
        parts = jnp.concatenate(split3(cum) + split3(before), axis=0)
        parts = jnp.transpose(parts).astype(BF16)
        cum_ref[...] = mm(parts, spread_cum)
        before_ref[...] = mm(parts, spread_before)
        loads[3 * layer].wait()
        for q in range(quads):
            cols = slice(256 * q, 256 * (q + 1))
            inner_ref[:, cols] = mm(normed, w_xz_ref[layer, :, cols]).astype(BF16)
            gate_cols = slice(inner_width + 256 * q, inner_width + 256 * (q + 1))
            half_gate = 0.5 * mm(normed, w_xz_ref[layer, :, gate_cols])
            gate_ref[:, cols] = half_gate + half_gate * jnp.tanh(half_gate)
        loads[3 * layer + 1].wait()
        proj_ref[...] = mm(normed, w_bc_ref[layer]).astype(BF16)

        def pair_body(j, carry):
            lanes = pl.ds(pl.multiple_of(j * 128, 128), 128)
            for odd in range(2):
                rows = pl.ds(pl.multiple_of((2 * j + odd) * walk_len, walk_len), walk_len)
                both = proj_ref[rows, :]
                b_in = both[:, :state_width]
                c_out = both[:, state_width:]
                scores = mm_nt(c_out, jnp.concatenate([b_in, b_in], axis=0)) * state_width ** (-0.5)
                for quad in range(quads):
                    mixes, tops, bottoms = [], [], []
                    for p in (2 * quad, 2 * quad + 1):
                        cols = slice(128 * p, 128 * (p + 1))

                        def row_of(q):
                            a = rows_ref[2 * q + odd, 2 * p : 2 * p + 1, lanes]
                            b = rows_ref[2 * q + 1 - odd, 2 * p + 1 : 2 * p + 2, lanes]
                            return jnp.where(left_row, a, b)

                        gap = jnp.where(
                            earlier, cum_ref[rows, cols] - row_of(0), row_of(1) - before_ref[rows, cols]
                        )
                        decay = jnp.exp2(gap) + diagonal
                        mixes.append((scores * decay * row_of(2)).astype(BF16))
                        inner = inner_ref[rows, cols]
                        tops.append(inner * left_bf)
                        bottoms.append(inner * right_bf)
                    blocks = jnp.concatenate(
                        [
                            jnp.concatenate([tops[0], nothing], axis=1),
                            jnp.concatenate([bottoms[0], nothing], axis=1),
                            jnp.concatenate([nothing, tops[1]], axis=1),
                            jnp.concatenate([nothing, bottoms[1]], axis=1),
                        ],
                        axis=0,
                    )
                    mixed = mm(jnp.concatenate(mixes, axis=1), blocks)
                    cols = slice(256 * quad, 256 * (quad + 1))
                    gated_ref[rows, cols] = (mixed * gate_ref[rows, cols]).astype(BF16)
            return carry

        lax.fori_loop(0, walk_pairs, pair_body, 0)
        loads[3 * layer + 2].wait()
        stream = x + mm(gated_ref[...], w_out_ref[layer])
        stream_ref[...] = stream.astype(BF16).astype(F32)

    put = onehot(iota((total, tok), 0) == slot_row)
    out_ref[...] = mm(put, stream_ref[...].astype(BF16)).astype(BF16)


def encode(arrived, slots, w_xz, w_bc, w_dt, decay_rate, w_out, walk_len):
    total, width = arrived.shape
    tok = slots.shape[1]
    inner_width = w_out.shape[1]
    heads = w_dt.shape[2]
    return pl.pallas_call(
        functools.partial(encode_kernel, walk_len=walk_len),
        out_shape=jax.ShapeDtypeStruct((total, width), BF16),
        in_specs=[VMEM_SPEC] * 4 + [HBM_SPEC] * 3,
        out_specs=VMEM_SPEC,
        scratch_shapes=[
            pltpu.VMEM(w_xz.shape, BF16),
            pltpu.VMEM(w_bc.shape, BF16),
            pltpu.VMEM(w_out.shape, BF16),
            pltpu.SemaphoreType.DMA((w_out.shape[0], 3)),
            pltpu.VMEM((tok, width), F32),
            pltpu.VMEM((tok, inner_width), BF16),
            pltpu.VMEM((tok, inner_width), F32),
            pltpu.VMEM((tok, w_bc.shape[2]), BF16),
            pltpu.VMEM((tok, inner_width), BF16),
            pltpu.VMEM((tok, inner_width), F32),
            pltpu.VMEM((tok, inner_width), F32),
            pltpu.VMEM((6, heads, tok), F32),
        ],
        name="encode",
        compiler_params=pltpu.CompilerParams(vmem_limit_bytes=40 << 20),
    )(*near_core(arrived, slots, jnp.swapaxes(w_dt, 1, 2), decay_rate), *in_hbm(w_xz, w_bc, w_out))


def update_kernel(returned_ref, reqrow_ref, states_ref, out_ref):
    node_count = states_ref.shape[0]
    total = returned_ref.shape[0]
    member = jnp.where(iota((node_count, total), 0) == reqrow_ref[0:1, :], 1.0, 0.0)
    visits = jnp.sum(member, axis=1, keepdims=True)
    summed = mm(member.astype(BF16), returned_ref[...])
    out_ref[...] = (states_ref[...].astype(F32) + summed / (1.0 + visits)).astype(BF16)


def update_nodes(returned, reqrow, node_states):
    return pl.pallas_call(
        update_kernel,
        out_shape=jax.ShapeDtypeStruct(node_states.shape, BF16),
        in_specs=[VMEM_SPEC] * 3,
        out_specs=VMEM_SPEC,
        name="update",
        compiler_params=pltpu.CompilerParams(vmem_limit_bytes=12 << 20),
    )(*near_core(returned, reqrow, node_states))


def finish_kernel(
    own_ref, one_ref, two_ref, three_ref, w_up_hbm, w_down_hbm, out_ref, w_up_ref, w_down_ref, weights_sem
):
    up = pltpu.make_async_copy(w_up_hbm, w_up_ref, weights_sem.at[0])
    down = pltpu.make_async_copy(w_down_hbm, w_down_ref, weights_sem.at[1])
    up.start()
    down.start()
    combined = (own_ref[...] + one_ref[...].astype(F32)) + (
        two_ref[...].astype(F32) + three_ref[...].astype(F32)
    )
    centred = combined - jnp.mean(combined, axis=-1, keepdims=True)
    normal = centred * lax.rsqrt(jnp.mean(centred * centred, axis=-1, keepdims=True) + EPS)
    up.wait()
    hidden = jax.nn.gelu(mm(normal.astype(BF16), w_up_ref[...])).astype(BF16)
    down.wait()
    out_ref[...] = (normal + mm(hidden, w_down_ref[...])).astype(BF16)


def finish(own, parts, w_up, w_down):
    return pl.pallas_call(
        finish_kernel,
        out_shape=jax.ShapeDtypeStruct(own.shape, BF16),
        in_specs=[VMEM_SPEC] * 4 + [HBM_SPEC] * 2,
        out_specs=VMEM_SPEC,
        scratch_shapes=[
            pltpu.VMEM(w_up.shape, BF16),
            pltpu.VMEM(w_down.shape, BF16),
            pltpu.SemaphoreType.DMA((2,)),
        ],
        name="finish",
        compiler_params=pltpu.CompilerParams(vmem_limit_bytes=12 << 20),
    )(own, *near_core(*parts), *in_hbm(w_up, w_down))


def neighbour_kernel(place_ref, links_ref, *refs):
    mine, other = refs[:SIDE], refs[SIDE : 2 * SIDE]
    own_ref, one_ref, two_ref, three_ref, piece_ref, sums_ref = refs[2 * SIDE :]
    my_row, y, z, core = place_ref[0], place_ref[1], place_ref[2], place_ref[3]
    rows = mine[0].shape[0] // SIDE
    for e in range(SIDE):
        for d in range(SIDE):
            for ref, who in ((mine[e], core), (other[e], 1 - core)):
                dy = d + who * (e - d)
                dz = e + who * (d - e)
                device = ((y + SIDE - dy) % SIDE * SIDE + (z + SIDE - dz) % SIDE) * CORES + who
                target = pl.multiple_of(device * rows, rows)
                piece_ref[pl.ds(target, rows), :] = ref[d * rows : (d + 1) * rows, :]
    sums_ref[...] = mm(links_ref[...], piece_ref[...])
    part = own_ref.shape[0]

    def block(distance):
        start = pl.multiple_of((my_row + distance) % SIDE * part, part)
        return sums_ref[pl.ds(start, part), :]

    own_ref[...] = block(0)
    one_ref[...] = block(1).astype(BF16)
    two_ref[...] = block(2).astype(BF16)
    three_ref[...] = block(3).astype(BF16)


def neighbour_sums(place, links, mine, other):
    row_block, width = links.shape[0], mine[0].shape[1]
    part = row_block // SIDE
    sent = jax.ShapeDtypeStruct((part, width), BF16)
    return pl.pallas_call(
        neighbour_kernel,
        out_shape=(jax.ShapeDtypeStruct((part, width), F32), sent, sent, sent),
        in_specs=[SMEM_SPEC] + [VMEM_SPEC] * (1 + 2 * SIDE),
        out_specs=(VMEM_SPEC,) * 4,
        scratch_shapes=[
            pltpu.VMEM((links.shape[1], width), BF16),
            pltpu.VMEM((row_block, width), F32),
        ],
        name="neighbours",
        compiler_params=pltpu.CompilerParams(vmem_limit_bytes=16 << 20),
    )(place, *near_core(links, *mine, *other))


def shifted(value, first, second, swap=0):
    pairs = []
    for y in range(SIDE):
        for z in range(SIDE):
            for c in range(CORES):
                dy, dz = (first, second) if c == 0 else (second, first)
                to = ((y + dy) % SIDE * SIDE + (z + dz) % SIDE) * CORES + (c + swap) % CORES
                pairs.append(((y * SIDE + z) * CORES + c, to))
    return lax.ppermute(value, "col", pairs)


def gather_blocks(update):
    near = [update] + [shifted(update, d, 0) for d in range(1, SIDE)]
    near = jnp.concatenate(near, axis=0)
    far = [near] + [shifted(near, 0, d) for d in range(1, SIDE)]
    return far, [shifted(block, 0, 0, swap=1) for block in far]


def assemble_kernel(place_ref, *refs):
    blocks, out_hbm, store_sem = refs[:-2], refs[-2], refs[-1]
    part = blocks[0].shape[0]
    stores = []
    for d, block_ref in enumerate(blocks):
        start = pl.multiple_of((place_ref[0] + len(blocks) - d) % len(blocks) * part, part)
        store = pltpu.make_async_copy(block_ref, out_hbm.at[pl.ds(start, part), :], store_sem.at[d])
        store.start()
        stores.append(store)
    for store in stores:
        store.wait()


def assemble(place, done, moved):
    rows, width = done.shape
    return pl.pallas_call(
        assemble_kernel,
        out_shape=jax.ShapeDtypeStruct((rows * (1 + len(moved)), width), BF16),
        in_specs=[SMEM_SPEC] + [VMEM_SPEC] * (1 + len(moved)),
        out_specs=HBM_SPEC,
        scratch_shapes=[pltpu.SemaphoreType.DMA((1 + len(moved),))],
        name="assemble",
        compiler_params=pltpu.CompilerParams(vmem_limit_bytes=8 << 20),
    )(place, *near_core(done, *moved))


def ring(size, distance):
    return [(i, (i + distance) % size) for i in range(size)]


def per_device(
    node_states,
    walk_nodes,
    walk_lengths,
    adjacency,
    w_xz,
    w_bc,
    w_dt,
    decay_rate,
    w_out,
    w_up,
    w_down,
):
    node_count, width = node_states.shape
    walk_count, walk_len = walk_nodes.shape
    everyone = ("row", "col")
    owners = lax.axis_size(everyone)
    row_size = lax.axis_size("row")
    row_block = adjacency.shape[0]

    my_row = lax.axis_index("row")
    row_global = lax.axis_index("col") * row_block + jnp.arange(row_block, dtype=I32)
    col_global = my_row * adjacency.shape[1] + jnp.arange(adjacency.shape[1], dtype=I32)
    self_link = (row_global[:, None] == col_global[None, :]).astype(I32)
    links = (adjacency + self_link).astype(BF16)
    wanted, slots = route(walk_nodes, walk_lengths, node_count, owners)
    requests = lax.all_to_all(wanted, everyone, split_axis=0, concat_axis=0, tiled=True)
    picked, reqrow = pick(requests, node_states)
    arrived = lax.all_to_all(
        picked.reshape(owners, CAP, width), everyone, split_axis=0, concat_axis=0, tiled=True
    )
    arrived, links = lax.optimization_barrier((arrived, links))
    outgoing = encode(
        arrived.reshape(owners * CAP, width), slots, w_xz, w_bc, w_dt, decay_rate, w_out, walk_len
    )
    returned = lax.all_to_all(
        outgoing.reshape(owners, CAP, width), everyone, split_axis=0, concat_axis=0, tiled=True
    )
    update = update_nodes(returned.reshape(owners * CAP, width), reqrow, node_states)

    mine, other = gather_blocks(update)
    my_col = lax.axis_index("col")
    place = jnp.stack([my_row, my_col // (SIDE * CORES), my_col // CORES % SIDE, my_col % CORES]).astype(I32)
    own, *sent = neighbour_sums(place, links, mine, other)
    parts = [lax.ppermute(block, "row", ring(row_size, d)) for d, block in enumerate(sent, 1)]
    done = finish(own, parts, w_up, w_down)
    moved = [lax.ppermute(done, "row", ring(row_size, d)) for d in range(1, row_size)]
    return assemble(place, done, moved)


def solution(mesh):
    return jax.shard_map(
        per_device,
        mesh=mesh,
        in_specs=(
            P(("row", "col"), None),
            P(("row", "col"), None),
            P(("row", "col")),
            P("col", "row"),
            P(),
            P(),
            P(),
            P(),
            P(),
            P(),
            P(),
        ),
        out_specs=P("col", None),
        check_vma=False,
    )
```

```python
import functools

import jax
import jax.numpy as jnp
from jax import lax
from jax.experimental import pallas as pl
from jax.experimental.pallas import tpu as pltpu
from jax.sharding import Mesh
from jax.sharding import PartitionSpec as P

F32 = jnp.float32
BF16 = jnp.bfloat16
I32 = jnp.int32
VMEM_SPEC = pl.BlockSpec(memory_space=pltpu.VMEM)
HBM_SPEC = pl.BlockSpec(memory_space=pltpu.HBM)
SMEM_SPEC = pl.BlockSpec(memory_space=pltpu.SMEM)
CAP = 8
EPS = 1e-05
LOG2E = 1.4426950408889634
SIDE = 4
CORES = 2


def iota(shape, dim):
    return lax.broadcasted_iota(I32, shape, dim)


def mm(a, b):
    return jnp.dot(a, b, preferred_element_type=F32)


def mm_nt(a, b):
    return lax.dot_general(a, b, (((1,), (1,)), ((), ())), preferred_element_type=F32)


def near_core(*arrays):
    return [pltpu.with_memory_space_constraint(a, pltpu.VMEM) for a in arrays]


def in_hbm(*arrays):
    return [pltpu.with_memory_space_constraint(a, pltpu.HBM) for a in arrays]


def onehot(cond):
    return cond.astype(F32).astype(BF16)


def as_column(row):
    return jnp.transpose(jnp.broadcast_to(row, (8, row.shape[1])))[:, 0:1]


def route_kernel(
    nodes_hbm, lengths_hbm, wanted_ref, slots_ref, nodes_ref, lengths_ref, load_sem, *, node_count, groups
):
    load_nodes = pltpu.make_async_copy(nodes_hbm, nodes_ref, load_sem.at[0])
    load_lengths = pltpu.make_async_copy(lengths_hbm, lengths_ref, load_sem.at[1])
    load_nodes.start()
    load_lengths.start()
    load_nodes.wait()
    load_lengths.wait()
    walk_count, walk_len = nodes_ref.shape
    tok = walk_count * walk_len
    place = iota((1, walk_len), 1)
    pieces = []
    for w in range(walk_count):
        live = place < lengths_ref[w]
        pieces.append(jnp.where(live, nodes_ref[w : w + 1, :], -1))
    node_row = jnp.concatenate(pieces, axis=1)
    live_row = node_row >= 0
    owner_row = ((node_row.astype(F32) + 0.5) * (1.0 / node_count)).astype(I32)
    local_row = node_row - owner_row * node_count
    owner_row = jnp.where(live_row, owner_row, -1)
    local_row = jnp.where(live_row, local_row + 1, 0)
    owner_col = as_column(owner_row)
    local_col = as_column(local_row)
    same = owner_col == owner_row
    first_i = iota((tok, tok), 0)
    second_i = iota((tok, tok), 1)
    rank_row = jnp.sum(jnp.where(same & (first_i < second_i), 1.0, 0.0), axis=0, keepdims=True)
    rank_row = rank_row.astype(I32)
    slot_row = jnp.where(live_row, owner_row * CAP + rank_row, -1)
    slots_ref[...] = jnp.broadcast_to(slot_row, slots_ref.shape)
    slot_count = wanted_ref.shape[1]
    slot_col = as_column(slot_row)
    by_group = onehot(iota((groups, tok), 0) == jnp.where(live_row, slot_row // slot_count, -1))
    by_slot = jnp.where(iota((tok, 128), 1) == slot_col % slot_count, local_col.astype(F32), 0.0)
    wanted = mm(by_group, by_slot.astype(BF16)).astype(I32) - 1
    wanted_ref[...] = wanted[:, :slot_count]


def route(walk_nodes, walk_lengths, node_count, groups, members):
    tok = walk_nodes.shape[0] * walk_nodes.shape[1]
    return pl.pallas_call(
        functools.partial(route_kernel, node_count=node_count, groups=groups),
        out_shape=(
            jax.ShapeDtypeStruct((groups, members * CAP), I32),
            jax.ShapeDtypeStruct((8, tok), I32),
        ),
        in_specs=[HBM_SPEC, HBM_SPEC],
        out_specs=(VMEM_SPEC, VMEM_SPEC),
        scratch_shapes=[
            pltpu.VMEM(walk_nodes.shape, I32),
            pltpu.SMEM(walk_lengths.shape, I32),
            pltpu.SemaphoreType.DMA((2,)),
        ],
        name="route",
        compiler_params=pltpu.CompilerParams(vmem_limit_bytes=12 << 20),
    )(*in_hbm(walk_nodes, walk_lengths))


def pick_kernel(place_ref, requests_ref, mine_ref, other_ref, picked_ref, states_ref):
    groups, slot_count = requests_ref.shape
    members = slot_count // CAP
    node_count = mine_ref.shape[0] // SIDE
    z, core = place_ref[2], place_ref[3]
    for ref, who in ((mine_ref, core), (other_ref, 1 - core)):
        for d in range(SIDE):
            member = (z + SIDE - d) % SIDE * CORES + who
            target = pl.multiple_of(member * node_count, node_count)
            states_ref[pl.ds(target, node_count), :] = ref[d * node_count : (d + 1) * node_count, :]
    total = groups * slot_count
    per_member = groups * CAP
    source = iota((total, groups), 0) % per_member // CAP
    spread = onehot(source == iota((total, groups), 1))
    wide = mm(spread, requests_ref[...].astype(F32).astype(BF16))
    row = iota((total, slot_count), 0)
    mine = iota((total, slot_count), 1) == row // per_member * CAP + row % CAP
    col = jnp.sum(jnp.where(mine, wide, 0.0), axis=1, keepdims=True).astype(I32)
    chosen = onehot(iota((total, node_count), 1) == col)
    for m in range(members):
        states = states_ref[m * node_count : (m + 1) * node_count, :]
        found = mm(chosen[m * per_member : (m + 1) * per_member, :], states).astype(BF16)
        picked_ref[:, m * CAP : (m + 1) * CAP, :] = found.reshape(groups, CAP, found.shape[1])


def pick(place, requests, mine, other):
    groups, slot_count = requests.shape
    width = mine.shape[1]
    return pl.pallas_call(
        pick_kernel,
        out_shape=jax.ShapeDtypeStruct((groups, slot_count, width), BF16),
        in_specs=[SMEM_SPEC] + [VMEM_SPEC] * 3,
        out_specs=VMEM_SPEC,
        scratch_shapes=[pltpu.VMEM((2 * mine.shape[0], width), BF16)],
        name="pick",
        compiler_params=pltpu.CompilerParams(vmem_limit_bytes=16 << 20),
    )(place, *near_core(requests, mine, other))


def visitors_kernel(place_ref, mine_ref, other_ref, reqrow_ref):
    slot_count = mine_ref.shape[1]
    members = slot_count // CAP
    groups = mine_ref.shape[0] // SIDE
    total = groups * slot_count
    z, core = place_ref[2], place_ref[3]
    tables = jnp.concatenate([mine_ref[...], other_ref[...]], axis=0).astype(F32).astype(BF16)
    row = iota((total, tables.shape[0]), 0)
    member = row // CAP % members
    d = (z + SIDE - member // CORES) % SIDE
    other = jnp.where(member % CORES == core, 0, 1)
    wanted = (other * SIDE + d) * groups + row // slot_count
    wide = mm(onehot(iota(row.shape, 1) == wanted), tables)
    slot = (z * CORES + core) * CAP + iota((total, slot_count), 0) % CAP
    mine = iota((total, slot_count), 1) == slot
    col = jnp.sum(jnp.where(mine, wide, 0.0), axis=1, keepdims=True).astype(I32)
    reqrow_ref[...] = jnp.transpose(jnp.broadcast_to(col, (total, 8)))


def visitors(place, mine, other):
    return pl.pallas_call(
        visitors_kernel,
        out_shape=jax.ShapeDtypeStruct((8, mine.shape[0] // SIDE * mine.shape[1]), I32),
        in_specs=[SMEM_SPEC, VMEM_SPEC, VMEM_SPEC],
        out_specs=VMEM_SPEC,
        name="visitors",
        compiler_params=pltpu.CompilerParams(vmem_limit_bytes=12 << 20),
    )(place, *near_core(mine, other))


def gather_members(value):
    mine = [value] + [lax.ppermute(value, "z", ring(SIDE, d)) for d in range(1, SIDE)]
    mine = jnp.concatenate(mine, axis=0)
    return mine, lax.ppermute(mine, "core", ring(CORES, 1))


def encode_kernel(
    arrived_ref,
    slots_ref,
    w_dt_ref,
    rate_ref,
    w_xz_hbm,
    w_bc_hbm,
    w_out_hbm,
    out_ref,
    w_xz_ref,
    w_bc_ref,
    w_out_ref,
    weights_sem,
    stream_ref,
    inner_ref,
    gate_ref,
    proj_ref,
    gated_ref,
    cum_ref,
    before_ref,
    rows_ref,
    *,
    walk_len,
):
    layers, inner_width, _ = w_out_ref.shape
    heads = w_dt_ref.shape[1]
    head_width = inner_width // heads
    state_width = w_bc_ref.shape[2] // 2
    total = arrived_ref.shape[0]
    tok = slots_ref.shape[1]
    quads = inner_width // 256
    walk_pairs = tok // (2 * walk_len)

    loads = []
    for layer in range(layers):
        for q, (source, target) in enumerate(
            ((w_xz_hbm, w_xz_ref), (w_bc_hbm, w_bc_ref), (w_out_hbm, w_out_ref))
        ):
            load = pltpu.make_async_copy(source.at[layer], target.at[layer], weights_sem.at[layer, q])
            load.start()
            loads.append(load)

    slot_row = slots_ref[0:1, :]
    slot_col = as_column(slot_row)
    take = onehot(iota((tok, total), 1) == slot_col)
    stream_ref[...] = mm(take, arrived_ref[...])

    live_row = slot_row >= 0
    place = iota((heads, tok), 1) % walk_len
    spread_in = iota((6 * heads, inner_width), 0)
    spread_out = iota((6 * heads, inner_width), 1)
    same_head = spread_in % heads == spread_out // head_width
    spread_cum = onehot(same_head & (spread_in < 3 * heads))
    spread_before = onehot(same_head & (spread_in >= 3 * heads))
    lane = iota((walk_len, 128), 1)
    left = lane < walk_len
    left_row = iota((1, 128), 1) < walk_len
    t_of = iota((walk_len, 128), 0)
    s_of = lane % walk_len
    earlier = s_of < t_of
    diagonal = jnp.where(s_of == t_of, 1.0, 0.0)
    left_bf = jnp.where(left, 1.0, 0.0).astype(BF16)
    right_bf = jnp.where(left, 0.0, 1.0).astype(BF16)
    nothing = jnp.zeros((walk_len, 128), BF16)

    def split3(v):
        high = v.astype(BF16).astype(F32)
        rest = v - high
        middle = rest.astype(BF16).astype(F32)
        return [high, middle, rest - middle]

    for layer in range(layers):
        x = stream_ref[...]
        normed = (x * lax.rsqrt(jnp.mean(x * x, axis=-1, keepdims=True) + EPS)).astype(BF16)
        raw = mm_nt(w_dt_ref[layer], normed)
        step = jnp.maximum(raw, 0.0) + jnp.log1p(jnp.exp(-jnp.abs(raw)))
        rate = as_column(rate_ref[layer : layer + 1, :])
        cum = (-LOG2E * rate) * step
        shift = 1
        while shift < walk_len:
            cum = cum + jnp.where(place >= shift, pltpu.roll(cum, shift, 1), 0.0)
            shift *= 2
        before = jnp.where(place >= 1, pltpu.roll(cum, 1, 1), 0.0)
        source = jnp.where(live_row, step, 0.0)
        for q, v in enumerate((cum, before, source)):
            rows_ref[2 * q] = v
            for j in range(walk_pairs):
                rows_ref[2 * q + 1, :, 128 * j : 128 * (j + 1)] = pltpu.roll(
                    v[:, 128 * j : 128 * (j + 1)], walk_len, 1
                )
        parts = jnp.concatenate(split3(cum) + split3(before), axis=0)
        parts = jnp.transpose(parts).astype(BF16)
        cum_ref[...] = mm(parts, spread_cum)
        before_ref[...] = mm(parts, spread_before)
        loads[3 * layer].wait()
        for q in range(quads):
            cols = slice(256 * q, 256 * (q + 1))
            inner_ref[:, cols] = mm(normed, w_xz_ref[layer, :, cols]).astype(BF16)
            gate_cols = slice(inner_width + 256 * q, inner_width + 256 * (q + 1))
            half_gate = 0.5 * mm(normed, w_xz_ref[layer, :, gate_cols])
            gate_ref[:, cols] = half_gate + half_gate * jnp.tanh(half_gate)
        loads[3 * layer + 1].wait()
        proj_ref[...] = mm(normed, w_bc_ref[layer]).astype(BF16)

        def pair_body(j, carry):
            lanes = pl.ds(pl.multiple_of(j * 128, 128), 128)
            for odd in range(2):
                rows = pl.ds(pl.multiple_of((2 * j + odd) * walk_len, walk_len), walk_len)
                both = proj_ref[rows, :]
                b_in = both[:, :state_width]
                c_out = both[:, state_width:]
                scores = mm_nt(c_out, jnp.concatenate([b_in, b_in], axis=0)) * state_width ** (-0.5)
                for quad in range(quads):
                    mixes, tops, bottoms = [], [], []
                    for p in (2 * quad, 2 * quad + 1):
                        cols = slice(128 * p, 128 * (p + 1))

                        def row_of(q):
                            a = rows_ref[2 * q + odd, 2 * p : 2 * p + 1, lanes]
                            b = rows_ref[2 * q + 1 - odd, 2 * p + 1 : 2 * p + 2, lanes]
                            return jnp.where(left_row, a, b)

                        gap = jnp.where(
                            earlier, cum_ref[rows, cols] - row_of(0), row_of(1) - before_ref[rows, cols]
                        )
                        decay = jnp.exp2(gap) + diagonal
                        mixes.append((scores * decay * row_of(2)).astype(BF16))
                        inner = inner_ref[rows, cols]
                        tops.append(inner * left_bf)
                        bottoms.append(inner * right_bf)
                    blocks = jnp.concatenate(
                        [
                            jnp.concatenate([tops[0], nothing], axis=1),
                            jnp.concatenate([bottoms[0], nothing], axis=1),
                            jnp.concatenate([nothing, tops[1]], axis=1),
                            jnp.concatenate([nothing, bottoms[1]], axis=1),
                        ],
                        axis=0,
                    )
                    mixed = mm(jnp.concatenate(mixes, axis=1), blocks)
                    cols = slice(256 * quad, 256 * (quad + 1))
                    gated_ref[rows, cols] = (mixed * gate_ref[rows, cols]).astype(BF16)
            return carry

        lax.fori_loop(0, walk_pairs, pair_body, 0)
        loads[3 * layer + 2].wait()
        stream = x + mm(gated_ref[...], w_out_ref[layer])
        stream_ref[...] = stream.astype(BF16).astype(F32)

    put = onehot(iota((total, tok), 0) == slot_row)
    out_ref[...] = mm(put, stream_ref[...].astype(BF16)).astype(BF16)


def encode(arrived, slots, w_xz, w_bc, w_dt, decay_rate, w_out, walk_len):
    total, width = arrived.shape
    tok = slots.shape[1]
    inner_width = w_out.shape[1]
    heads = w_dt.shape[2]
    return pl.pallas_call(
        functools.partial(encode_kernel, walk_len=walk_len),
        out_shape=jax.ShapeDtypeStruct((total, width), BF16),
        in_specs=[VMEM_SPEC] * 4 + [HBM_SPEC] * 3,
        out_specs=VMEM_SPEC,
        scratch_shapes=[
            pltpu.VMEM(w_xz.shape, BF16),
            pltpu.VMEM(w_bc.shape, BF16),
            pltpu.VMEM(w_out.shape, BF16),
            pltpu.SemaphoreType.DMA((w_out.shape[0], 3)),
            pltpu.VMEM((tok, width), F32),
            pltpu.VMEM((tok, inner_width), BF16),
            pltpu.VMEM((tok, inner_width), F32),
            pltpu.VMEM((tok, w_bc.shape[2]), BF16),
            pltpu.VMEM((tok, inner_width), BF16),
            pltpu.VMEM((tok, inner_width), F32),
            pltpu.VMEM((tok, inner_width), F32),
            pltpu.VMEM((6, heads, tok), F32),
        ],
        name="encode",
        compiler_params=pltpu.CompilerParams(vmem_limit_bytes=40 << 20),
    )(*near_core(arrived, slots, jnp.swapaxes(w_dt, 1, 2), decay_rate), *in_hbm(w_xz, w_bc, w_out))


def update_kernel(returned_ref, reqrow_ref, states_ref, out_ref):
    node_count = states_ref.shape[0]
    total = returned_ref.shape[0]
    member = jnp.where(iota((node_count, total), 0) == reqrow_ref[0:1, :], 1.0, 0.0)
    visits = jnp.sum(member, axis=1, keepdims=True)
    summed = mm(member.astype(BF16), returned_ref[...])
    out_ref[...] = (states_ref[...].astype(F32) + summed / (1.0 + visits)).astype(BF16)


def update_nodes(returned, reqrow, node_states):
    return pl.pallas_call(
        update_kernel,
        out_shape=jax.ShapeDtypeStruct(node_states.shape, BF16),
        in_specs=[VMEM_SPEC] * 3,
        out_specs=VMEM_SPEC,
        name="update",
        compiler_params=pltpu.CompilerParams(vmem_limit_bytes=12 << 20),
    )(*near_core(returned, reqrow, node_states))


def finish_kernel(
    own_ref, one_ref, two_ref, three_ref, w_up_hbm, w_down_hbm, out_ref, w_up_ref, w_down_ref, weights_sem
):
    up = pltpu.make_async_copy(w_up_hbm, w_up_ref, weights_sem.at[0])
    down = pltpu.make_async_copy(w_down_hbm, w_down_ref, weights_sem.at[1])
    up.start()
    down.start()
    combined = (own_ref[...] + one_ref[...].astype(F32)) + (
        two_ref[...].astype(F32) + three_ref[...].astype(F32)
    )
    centred = combined - jnp.mean(combined, axis=-1, keepdims=True)
    normal = centred * lax.rsqrt(jnp.mean(centred * centred, axis=-1, keepdims=True) + EPS)
    up.wait()
    hidden = jax.nn.gelu(mm(normal.astype(BF16), w_up_ref[...])).astype(BF16)
    down.wait()
    out_ref[...] = (normal + mm(hidden, w_down_ref[...])).astype(BF16)


def finish(own, parts, w_up, w_down):
    return pl.pallas_call(
        finish_kernel,
        out_shape=jax.ShapeDtypeStruct(own.shape, BF16),
        in_specs=[VMEM_SPEC] * 4 + [HBM_SPEC] * 2,
        out_specs=VMEM_SPEC,
        scratch_shapes=[
            pltpu.VMEM(w_up.shape, BF16),
            pltpu.VMEM(w_down.shape, BF16),
            pltpu.SemaphoreType.DMA((2,)),
        ],
        name="finish",
        compiler_params=pltpu.CompilerParams(vmem_limit_bytes=12 << 20),
    )(own, *near_core(*parts), *in_hbm(w_up, w_down))


def neighbour_kernel(place_ref, links_ref, *refs):
    mine, other = refs[:SIDE], refs[SIDE : 2 * SIDE]
    own_ref, one_ref, two_ref, three_ref, piece_ref, sums_ref = refs[2 * SIDE :]
    my_row, y, z, core = place_ref[0], place_ref[1], place_ref[2], place_ref[3]
    rows = mine[0].shape[0] // SIDE
    for e in range(SIDE):
        for d in range(SIDE):
            for ref, who in ((mine[e], core), (other[e], 1 - core)):
                dy = d + who * (e - d)
                dz = e + who * (d - e)
                device = ((y + SIDE - dy) % SIDE * SIDE + (z + SIDE - dz) % SIDE) * CORES + who
                target = pl.multiple_of(device * rows, rows)
                piece_ref[pl.ds(target, rows), :] = ref[d * rows : (d + 1) * rows, :]
    sums_ref[...] = mm(links_ref[...], piece_ref[...])
    part = own_ref.shape[0]

    def block(distance):
        start = pl.multiple_of((my_row + distance) % SIDE * part, part)
        return sums_ref[pl.ds(start, part), :]

    own_ref[...] = block(0)
    one_ref[...] = block(1).astype(BF16)
    two_ref[...] = block(2).astype(BF16)
    three_ref[...] = block(3).astype(BF16)


def neighbour_sums(place, links, mine, other):
    row_block, width = links.shape[0], mine[0].shape[1]
    part = row_block // SIDE
    sent = jax.ShapeDtypeStruct((part, width), BF16)
    return pl.pallas_call(
        neighbour_kernel,
        out_shape=(jax.ShapeDtypeStruct((part, width), F32), sent, sent, sent),
        in_specs=[SMEM_SPEC] + [VMEM_SPEC] * (1 + 2 * SIDE),
        out_specs=(VMEM_SPEC,) * 4,
        scratch_shapes=[
            pltpu.VMEM((links.shape[1], width), BF16),
            pltpu.VMEM((row_block, width), F32),
        ],
        name="neighbours",
        compiler_params=pltpu.CompilerParams(vmem_limit_bytes=16 << 20),
    )(place, *near_core(links, *mine, *other))


def shifted(value, first, second, swap=0):
    pairs = []
    for y in range(SIDE):
        for z in range(SIDE):
            for c in range(CORES):
                dy, dz = (first, second) if c == 0 else (second, first)
                to = ((y + dy) % SIDE * SIDE + (z + dz) % SIDE) * CORES + (c + swap) % CORES
                pairs.append(((y * SIDE + z) * CORES + c, to))
    return lax.ppermute(value, ("y", "z", "core"), pairs)


def gather_blocks(update):
    near = [update] + [shifted(update, d, 0) for d in range(1, SIDE)]
    near = jnp.concatenate(near, axis=0)
    far = [near] + [shifted(near, 0, d) for d in range(1, SIDE)]
    return far, [shifted(block, 0, 0, swap=1) for block in far]


def assemble_kernel(place_ref, *refs):
    blocks, out_hbm, store_sem = refs[:-2], refs[-2], refs[-1]
    part = blocks[0].shape[0]
    stores = []
    for d, block_ref in enumerate(blocks):
        start = pl.multiple_of((place_ref[0] + len(blocks) - d) % len(blocks) * part, part)
        store = pltpu.make_async_copy(block_ref, out_hbm.at[pl.ds(start, part), :], store_sem.at[d])
        store.start()
        stores.append(store)
    for store in stores:
        store.wait()


def assemble(place, done, moved):
    rows, width = done.shape
    return pl.pallas_call(
        assemble_kernel,
        out_shape=jax.ShapeDtypeStruct((rows * (1 + len(moved)), width), BF16),
        in_specs=[SMEM_SPEC] + [VMEM_SPEC] * (1 + len(moved)),
        out_specs=HBM_SPEC,
        scratch_shapes=[pltpu.SemaphoreType.DMA((1 + len(moved),))],
        name="assemble",
        compiler_params=pltpu.CompilerParams(vmem_limit_bytes=8 << 20),
    )(place, *near_core(done, *moved))


def ring(size, distance):
    return [(i, (i + distance) % size) for i in range(size)]


def per_device(
    node_states,
    walk_nodes,
    walk_lengths,
    adjacency,
    w_xz,
    w_bc,
    w_dt,
    decay_rate,
    w_out,
    w_up,
    w_down,
):
    node_count, width = node_states.shape
    _, walk_len = walk_nodes.shape
    everyone = ("x", "y", "z", "core")
    owners = lax.axis_size(everyone)
    members = SIDE * CORES
    groups = owners // members
    row_block = adjacency.shape[0]
    my_x, my_y, my_z, my_core = (lax.axis_index(axis) for axis in everyone)
    place = jnp.stack([my_x, my_y, my_z, my_core]).astype(I32)

    wanted, slots = route(walk_nodes, walk_lengths, node_count, groups, members)
    row_global = ((my_y * SIDE + my_z) * CORES + my_core) * row_block + jnp.arange(row_block, dtype=I32)
    col_global = my_x * adjacency.shape[1] + jnp.arange(adjacency.shape[1], dtype=I32)
    self_link = (row_global[:, None] == col_global[None, :]).astype(I32)
    links = (adjacency + self_link).astype(BF16)
    requests = lax.all_to_all(wanted, ("x", "y"), split_axis=0, concat_axis=0, tiled=True)
    near_states = gather_members(node_states)
    requests, links = lax.optimization_barrier((requests, links))
    picked = pick(place, requests, *near_states)
    arrived = lax.all_to_all(picked, ("x", "y"), split_axis=0, concat_axis=0, tiled=True)
    outgoing = encode(
        arrived.reshape(owners * CAP, width), slots, w_xz, w_bc, w_dt, decay_rate, w_out, walk_len
    )
    outgoing, asked = lax.optimization_barrier((outgoing, requests))
    returned = lax.all_to_all(
        outgoing.reshape(owners, CAP, width), everyone, split_axis=0, concat_axis=0, tiled=True
    )
    tables = gather_members(asked)
    reqrow = visitors(place, *tables)
    update = update_nodes(returned.reshape(owners * CAP, width), reqrow, node_states)

    mine, other = gather_blocks(update)
    own, *sent = neighbour_sums(place, links, mine, other)
    parts = [lax.ppermute(block, "x", ring(SIDE, d)) for d, block in enumerate(sent, 1)]
    done = finish(own, parts, w_up, w_down)
    moved = [lax.ppermute(done, "x", ring(SIDE, d)) for d in range(1, SIDE)]
    return assemble(place, done, moved)


def solution(mesh):
    torus = Mesh(mesh.devices.reshape(SIDE, SIDE, SIDE, CORES), ("x", "y", "z", "core"))
    everyone = ("x", "y", "z", "core")
    plane = ("y", "z", "core")
    return jax.shard_map(
        per_device,
        mesh=torus,
        in_specs=(
            P(everyone, None),
            P(everyone, None),
            P(everyone),
            P(plane, "x"),
            P(),
            P(),
            P(),
            P(),
            P(),
            P(),
            P(),
        ),
        out_specs=P(plane, None),
        check_vma=False,
    )
```

```python
import functools

import jax
import jax.numpy as jnp
from jax import lax
from jax.experimental import pallas as pl
from jax.experimental.pallas import tpu as pltpu
from jax.sharding import PartitionSpec as P

F32 = jnp.float32
BF16 = jnp.bfloat16
I32 = jnp.int32
VMEM_SPEC = pl.BlockSpec(memory_space=pltpu.VMEM)
HBM_SPEC = pl.BlockSpec(memory_space=pltpu.HBM)
SMEM_SPEC = pl.BlockSpec(memory_space=pltpu.SMEM)
CAP = 8
EPS = 1e-05
LOG2E = 1.4426950408889634
SIDE = 4
CORES = 2


def iota(shape, dim):
    return lax.broadcasted_iota(I32, shape, dim)


def mm(a, b):
    return jnp.dot(a, b, preferred_element_type=F32)


def mm_nt(a, b):
    return lax.dot_general(a, b, (((1,), (1,)), ((), ())), preferred_element_type=F32)


def near_core(*arrays):
    return [pltpu.with_memory_space_constraint(a, pltpu.VMEM) for a in arrays]


def in_hbm(*arrays):
    return [pltpu.with_memory_space_constraint(a, pltpu.HBM) for a in arrays]


def onehot(cond):
    return cond.astype(F32).astype(BF16)


def as_column(row):
    return jnp.transpose(jnp.broadcast_to(row, (8, row.shape[1])))[:, 0:1]


def route_kernel(
    nodes_hbm, lengths_hbm, wanted_ref, slots_ref, nodes_ref, lengths_ref, load_sem, *, node_count, owners
):
    load_nodes = pltpu.make_async_copy(nodes_hbm, nodes_ref, load_sem.at[0])
    load_lengths = pltpu.make_async_copy(lengths_hbm, lengths_ref, load_sem.at[1])
    load_nodes.start()
    load_lengths.start()
    load_nodes.wait()
    load_lengths.wait()
    walk_count, walk_len = nodes_ref.shape
    tok = walk_count * walk_len
    place = iota((1, walk_len), 1)
    pieces = []
    for w in range(walk_count):
        live = place < lengths_ref[w]
        pieces.append(jnp.where(live, nodes_ref[w : w + 1, :], -1))
    node_row = jnp.concatenate(pieces, axis=1)
    live_row = node_row >= 0
    owner_row = ((node_row.astype(F32) + 0.5) * (1.0 / node_count)).astype(I32)
    local_row = node_row - owner_row * node_count
    owner_row = jnp.where(live_row, owner_row, -1)
    local_row = jnp.where(live_row, local_row + 1, 0)
    owner_col = as_column(owner_row)
    local_col = as_column(local_row)
    same = owner_col == owner_row
    first_i = iota((tok, tok), 0)
    second_i = iota((tok, tok), 1)
    rank_row = jnp.sum(jnp.where(same & (first_i < second_i), 1.0, 0.0), axis=0, keepdims=True)
    rank_row = rank_row.astype(I32)
    rank_col = as_column(rank_row)
    slot_row = jnp.where(live_row, owner_row * CAP + rank_row, -1)
    slots_ref[...] = jnp.broadcast_to(slot_row, slots_ref.shape)
    by_owner = onehot(iota((owners, tok), 0) == owner_row)
    by_rank = jnp.where(iota((tok, 128), 1) == rank_col, local_col.astype(F32), 0.0).astype(BF16)
    wanted = mm(by_owner, by_rank).astype(I32) - 1
    wanted_ref[...] = wanted[:, :CAP]


def route(walk_nodes, walk_lengths, node_count, owners):
    tok = walk_nodes.shape[0] * walk_nodes.shape[1]
    return pl.pallas_call(
        functools.partial(route_kernel, node_count=node_count, owners=owners),
        out_shape=(
            jax.ShapeDtypeStruct((owners, CAP), I32),
            jax.ShapeDtypeStruct((8, tok), I32),
        ),
        in_specs=[HBM_SPEC, HBM_SPEC],
        out_specs=(VMEM_SPEC, VMEM_SPEC),
        scratch_shapes=[
            pltpu.VMEM(walk_nodes.shape, I32),
            pltpu.SMEM(walk_lengths.shape, I32),
            pltpu.SemaphoreType.DMA((2,)),
        ],
        name="route",
        compiler_params=pltpu.CompilerParams(vmem_limit_bytes=12 << 20),
    )(*in_hbm(walk_nodes, walk_lengths))


def pick_kernel(requests_ref, states_ref, picked_ref, reqrow_ref):
    owners = requests_ref.shape[0]
    node_count = states_ref.shape[0]
    total = owners * CAP
    spread = onehot(iota((total, owners), 0) // CAP == iota((total, owners), 1))
    wide = mm(spread, requests_ref[...].astype(F32).astype(BF16))
    mine = iota((total, CAP), 1) == iota((total, CAP), 0) % CAP
    col = jnp.sum(jnp.where(mine, wide, 0.0), axis=1, keepdims=True).astype(I32)
    chosen = onehot(iota((total, node_count), 1) == col)
    reqrow_ref[...] = jnp.transpose(jnp.broadcast_to(col, (total, 8)))
    picked_ref[...] = mm(chosen, states_ref[...]).astype(BF16)


def pick(requests, node_states):
    total = requests.shape[0] * CAP
    return pl.pallas_call(
        pick_kernel,
        out_shape=(
            jax.ShapeDtypeStruct((total, node_states.shape[1]), BF16),
            jax.ShapeDtypeStruct((8, total), I32),
        ),
        in_specs=[VMEM_SPEC, VMEM_SPEC],
        out_specs=(VMEM_SPEC, VMEM_SPEC),
        name="pick",
        compiler_params=pltpu.CompilerParams(vmem_limit_bytes=12 << 20),
    )(*near_core(requests, node_states))


def placement_kernel(slots_ref, put_ref):
    put_ref[...] = onehot(iota(put_ref.shape, 0) == slots_ref[0:1, :])


def placement(slots, total):
    return pl.pallas_call(
        placement_kernel,
        out_shape=jax.ShapeDtypeStruct((total, slots.shape[1]), BF16),
        in_specs=[VMEM_SPEC],
        out_specs=VMEM_SPEC,
        name="placement",
        compiler_params=pltpu.CompilerParams(vmem_limit_bytes=12 << 20),
    )(*near_core(slots))


def fetch_kernel(source_hbm, target_ref):
    pltpu.sync_copy(source_hbm, target_ref)


def fetch(array):
    return pl.pallas_call(
        fetch_kernel,
        out_shape=jax.ShapeDtypeStruct(array.shape, array.dtype),
        in_specs=[HBM_SPEC],
        out_specs=VMEM_SPEC,
        name="fetch",
        compiler_params=pltpu.CompilerParams(vmem_limit_bytes=8 << 20),
    )(*in_hbm(array))


PAD = 8


def encode_kernel(
    arrived_ref,
    slots_ref,
    put_hbm,
    w_dt_hbm,
    rate_hbm,
    w_xz_hbm,
    w_bc_hbm,
    w_out_hbm,
    out_ref,
    put_ref,
    w_dt_ref,
    rate_ref,
    w_xz_ref,
    w_bc_ref,
    w_out_ref,
    small_sem,
    weights_sem,
    stream_ref,
    inner_ref,
    gate_ref,
    proj_ref,
    gated_ref,
    cum_ref,
    rows_ref,
    mix_even_ref,
    mix_odd_ref,
    *,
    walk_len,
):
    layers, inner_width, width = w_out_ref.shape
    heads = w_dt_ref.shape[1]
    head_width = inner_width // heads
    state_width = w_bc_ref.shape[2] // 2
    tok = slots_ref.shape[1]
    quads = inner_width // 256
    walks = tok // walk_len
    stride = walk_len + PAD

    load_dt = pltpu.make_async_copy(w_dt_hbm, w_dt_ref, small_sem.at[0])
    load_rate = pltpu.make_async_copy(rate_hbm, rate_ref, small_sem.at[1])
    load_dt.start()
    load_rate.start()
    loads = []
    for layer in range(layers):
        for q, (source, target) in enumerate(
            ((w_xz_hbm, w_xz_ref), (w_bc_hbm, w_bc_ref), (w_out_hbm, w_out_ref))
        ):
            load = pltpu.make_async_copy(source.at[layer], target.at[layer], weights_sem.at[layer, q])
            load.start()
            loads.append(load)
    load_put = pltpu.make_async_copy(put_hbm, put_ref, small_sem.at[2])
    load_put.start()

    total = arrived_ref.shape[0]
    take = onehot(iota((tok, total), 1) == as_column(slots_ref[0:1, :]))
    stream_ref[...] = mm(take, arrived_ref[...])
    for w in range(walks):
        cum_ref[:, w * stride : w * stride + PAD, :] = jnp.zeros((2 * quads, PAD, 128), F32)
    mix_odd_ref[...] = jnp.zeros(mix_odd_ref.shape, BF16)
    load_dt.wait()
    load_rate.wait()

    live_row = slots_ref[0:1, :] >= 0
    spread_in = iota((3 * heads, inner_width), 0)
    spread_out = iota((3 * heads, inner_width), 1)
    spread = onehot(spread_in % heads == spread_out // head_width)
    sum_in = iota((128, 256), 0)
    sum_out = iota((128, 256), 1)
    same_walk = sum_in // walk_len == sum_out % 128 // walk_len
    reach = sum_out % walk_len - jnp.where(sum_out >= 128, 1, 0)
    running = onehot(same_walk & (sum_in % walk_len <= reach))
    lane = iota((walk_len, 128), 1)
    left = lane < walk_len
    left_row = iota((1, 128), 1) < walk_len
    t_of = iota((walk_len, 128), 0)
    s_of = lane % walk_len
    earlier = s_of < t_of
    diagonal = jnp.where(s_of == t_of, 1.0, 0.0)
    left_bf = jnp.where(left, 1.0, 0.0).astype(BF16)
    right_bf = jnp.where(left, 0.0, 1.0).astype(BF16)
    nothing = jnp.zeros((walk_len, 128), BF16)

    def split3(v):
        high = v.astype(BF16).astype(F32)
        rest = v - high
        middle = rest.astype(BF16).astype(F32)
        return jnp.concatenate([high, middle, rest - middle], axis=0)

    def walk_rows(walk):
        return pl.ds(pl.multiple_of(walk * walk_len, walk_len), walk_len)

    def half_step(j, odd):
        lanes = pl.ds(pl.multiple_of(j * 128, 128), 128)
        walk = 2 * j + odd
        ahead_ref, behind_ref = (mix_odd_ref, mix_even_ref) if odd else (mix_even_ref, mix_odd_ref)
        previous = walk_rows(jnp.maximum(walk - 1, 0))
        both = proj_ref[walk_rows(walk), :]
        b_in = both[:, :state_width]
        c_out = both[:, state_width:]
        scores = mm_nt(c_out, jnp.concatenate([b_in, b_in], axis=0)) * state_width ** (-0.5)
        here = pl.ds(pl.multiple_of(walk * stride + PAD, PAD), walk_len)
        above = pl.ds(walk * stride + PAD - 1, walk_len)
        for quad in range(quads):
            apply_mix(quad, previous, behind_ref)
            for p in (2 * quad, 2 * quad + 1):

                def row_of(q):
                    a = rows_ref[2 * q + odd, 2 * p : 2 * p + 1, lanes]
                    b = rows_ref[2 * q + 1 - odd, 2 * p + 1 : 2 * p + 2, lanes]
                    return jnp.where(left_row, a, b)

                gap = jnp.where(earlier, cum_ref[p, here, :] - row_of(0), row_of(1) - cum_ref[p, above, :])
                decay = jnp.exp2(gap) + diagonal
                ahead_ref[:, 128 * p : 128 * (p + 1)] = (scores * decay * row_of(2)).astype(BF16)

    def apply_mix(quad, rows, mix_ref):
        tops, bottoms = [], []
        for p in (2 * quad, 2 * quad + 1):
            inner = inner_ref[rows, 128 * p : 128 * (p + 1)]
            tops.append(inner * left_bf)
            bottoms.append(inner * right_bf)
        blocks = jnp.concatenate(
            [
                jnp.concatenate([tops[0], nothing], axis=1),
                jnp.concatenate([bottoms[0], nothing], axis=1),
                jnp.concatenate([nothing, tops[1]], axis=1),
                jnp.concatenate([nothing, bottoms[1]], axis=1),
            ],
            axis=0,
        )
        cols = slice(256 * quad, 256 * (quad + 1))
        mixed = mm(mix_ref[:, cols], blocks)
        gated_ref[rows, cols] = (mixed * gate_ref[rows, cols]).astype(BF16)

    def walk_pair(j, carry):
        half_step(j, 0)
        half_step(j, 1)
        return carry

    for layer in range(layers):
        x = stream_ref[...]
        normed = (x * lax.rsqrt(jnp.mean(x * x, axis=-1, keepdims=True) + EPS)).astype(BF16)

        def project(q):
            cols = slice(256 * q, 256 * (q + 1))
            inner_ref[:, cols] = mm(normed, w_xz_ref[layer, :, cols]).astype(BF16)
            gate_cols = slice(inner_width + 256 * q, inner_width + 256 * (q + 1))
            half_gate = 0.5 * mm(normed, w_xz_ref[layer, :, gate_cols])
            gate_ref[:, cols] = half_gate + half_gate * jnp.tanh(half_gate)

        raw = mm_nt(w_dt_ref[layer], normed)
        loads[3 * layer].wait()
        project(0)
        step = jnp.maximum(raw, 0.0) + jnp.log1p(jnp.exp(-jnp.abs(raw)))
        rate = as_column(rate_ref[layer : layer + 1, :])
        pieces = split3((-LOG2E * rate) * step).astype(BF16)
        source = jnp.where(live_row, step, 0.0)
        project(1)
        cums = []
        for j in range(walks // 2):
            lanes = slice(128 * j, 128 * (j + 1))
            sums = mm(pieces[:, lanes], running)
            sums = sums[:heads] + (sums[heads : 2 * heads] + sums[2 * heads :])
            cums.append(sums[:, :128])
            for q, v in enumerate((sums[:, :128], sums[:, 128:], source[:, lanes])):
                rows_ref[2 * q, :, lanes] = v
                rows_ref[2 * q + 1, :, lanes] = pltpu.roll(v, walk_len, 1)
        project(2)
        columns = jnp.transpose(split3(jnp.concatenate(cums, axis=1))).astype(BF16)
        project(3)
        loads[3 * layer + 1].wait()
        proj_ref[...] = mm(normed, w_bc_ref[layer]).astype(BF16)
        for quad in range(quads):
            wide = mm(columns, spread[:, 256 * quad : 256 * (quad + 1)])
            for w in range(walks):
                block = wide[w * walk_len : (w + 1) * walk_len, :]
                rows = slice(w * stride + PAD, (w + 1) * stride)
                cum_ref[2 * quad, rows, :] = block[:, :128]
                cum_ref[2 * quad + 1, rows, :] = block[:, 128:]

        lax.fori_loop(0, walks // 2, walk_pair, 0)
        for quad in range(quads):
            apply_mix(quad, walk_rows(walks - 1), mix_odd_ref)
        loads[3 * layer + 2].wait()
        stream = x + mm(gated_ref[...], w_out_ref[layer])
        stream_ref[...] = stream.astype(BF16).astype(F32)

    load_put.wait()
    out_ref[...] = mm(put_ref[...], stream_ref[...].astype(BF16)).astype(BF16)


def encode(arrived, slots, put, w_xz, w_bc, w_dt, decay_rate, w_out, walk_len):
    total, width = arrived.shape
    tok = slots.shape[1]
    inner_width = w_out.shape[1]
    w_dt = jnp.swapaxes(w_dt, 1, 2)
    return pl.pallas_call(
        functools.partial(encode_kernel, walk_len=walk_len),
        out_shape=jax.ShapeDtypeStruct((total, width), BF16),
        in_specs=[VMEM_SPEC] * 2 + [HBM_SPEC] * 6,
        out_specs=VMEM_SPEC,
        scratch_shapes=[
            pltpu.VMEM(put.shape, BF16),
            pltpu.VMEM(w_dt.shape, BF16),
            pltpu.VMEM(decay_rate.shape, F32),
            pltpu.VMEM(w_xz.shape, BF16),
            pltpu.VMEM(w_bc.shape, BF16),
            pltpu.VMEM(w_out.shape, BF16),
            pltpu.SemaphoreType.DMA((3,)),
            pltpu.SemaphoreType.DMA((w_out.shape[0], 3)),
            pltpu.VMEM((tok, width), F32),
            pltpu.VMEM((tok, inner_width), BF16),
            pltpu.VMEM((tok, inner_width), F32),
            pltpu.VMEM((tok, w_bc.shape[2]), BF16),
            pltpu.VMEM((tok, inner_width), BF16),
            pltpu.VMEM((inner_width // 128, tok // walk_len * (walk_len + PAD), 128), F32),
            pltpu.VMEM((6, w_dt.shape[1], tok), F32),
            pltpu.VMEM((walk_len, inner_width), BF16),
            pltpu.VMEM((walk_len, inner_width), BF16),
        ],
        name="encode",
        compiler_params=pltpu.CompilerParams(vmem_limit_bytes=36 << 20),
    )(*near_core(arrived, slots), *in_hbm(put, w_dt, decay_rate, w_xz, w_bc, w_out))


def update_kernel(returned_ref, reqrow_ref, states_ref, out_ref):
    node_count = states_ref.shape[0]
    total = returned_ref.shape[0]
    member = jnp.where(iota((node_count, total), 0) == reqrow_ref[0:1, :], 1.0, 0.0)
    visits = jnp.sum(member, axis=1, keepdims=True)
    summed = mm(member.astype(BF16), returned_ref[...])
    out_ref[...] = (states_ref[...].astype(F32) + summed / (1.0 + visits)).astype(BF16)


def update_nodes(returned, reqrow, node_states):
    return pl.pallas_call(
        update_kernel,
        out_shape=jax.ShapeDtypeStruct(node_states.shape, BF16),
        in_specs=[VMEM_SPEC] * 3,
        out_specs=VMEM_SPEC,
        name="update",
        compiler_params=pltpu.CompilerParams(vmem_limit_bytes=12 << 20),
    )(*near_core(returned, reqrow, node_states))


def finish_kernel(
    own_ref, one_ref, two_ref, three_ref, w_up_hbm, w_down_hbm, out_ref, w_up_ref, w_down_ref, weights_sem
):
    up = pltpu.make_async_copy(w_up_hbm, w_up_ref, weights_sem.at[0])
    down = pltpu.make_async_copy(w_down_hbm, w_down_ref, weights_sem.at[1])
    up.start()
    down.start()
    combined = (own_ref[...] + one_ref[...].astype(F32)) + (
        two_ref[...].astype(F32) + three_ref[...].astype(F32)
    )
    centred = combined - jnp.mean(combined, axis=-1, keepdims=True)
    normal = centred * lax.rsqrt(jnp.mean(centred * centred, axis=-1, keepdims=True) + EPS)
    up.wait()
    hidden = jax.nn.gelu(mm(normal.astype(BF16), w_up_ref[...])).astype(BF16)
    down.wait()
    out_ref[...] = (normal + mm(hidden, w_down_ref[...])).astype(BF16)


def finish(own, parts, w_up, w_down):
    return pl.pallas_call(
        finish_kernel,
        out_shape=jax.ShapeDtypeStruct(own.shape, BF16),
        in_specs=[VMEM_SPEC] * 4 + [HBM_SPEC] * 2,
        out_specs=VMEM_SPEC,
        scratch_shapes=[
            pltpu.VMEM(w_up.shape, BF16),
            pltpu.VMEM(w_down.shape, BF16),
            pltpu.SemaphoreType.DMA((2,)),
        ],
        name="finish",
        compiler_params=pltpu.CompilerParams(vmem_limit_bytes=12 << 20),
    )(own, *near_core(*parts), *in_hbm(w_up, w_down))


def neighbour_kernel(place_ref, links_ref, *refs):
    mine, other = refs[:SIDE], refs[SIDE : 2 * SIDE]
    own_ref, one_ref, two_ref, three_ref, piece_ref, sums_ref = refs[2 * SIDE :]
    my_row, y, z, core = place_ref[0], place_ref[1], place_ref[2], place_ref[3]
    rows = mine[0].shape[0] // SIDE
    for e in range(SIDE):
        for d in range(SIDE):
            for ref, who in ((mine[e], core), (other[e], 1 - core)):
                dy = d + who * (e - d)
                dz = e + who * (d - e)
                device = ((y + SIDE - dy) % SIDE * SIDE + (z + SIDE - dz) % SIDE) * CORES + who
                target = pl.multiple_of(device * rows, rows)
                piece_ref[pl.ds(target, rows), :] = ref[d * rows : (d + 1) * rows, :]
    sums_ref[...] = mm(links_ref[...], piece_ref[...])
    part = own_ref.shape[0]

    def block(distance):
        start = pl.multiple_of((my_row + distance) % SIDE * part, part)
        return sums_ref[pl.ds(start, part), :]

    own_ref[...] = block(0)
    one_ref[...] = block(1).astype(BF16)
    two_ref[...] = block(2).astype(BF16)
    three_ref[...] = block(3).astype(BF16)


def neighbour_sums(place, links, mine, other):
    row_block, width = links.shape[0], mine[0].shape[1]
    part = row_block // SIDE
    sent = jax.ShapeDtypeStruct((part, width), BF16)
    return pl.pallas_call(
        neighbour_kernel,
        out_shape=(jax.ShapeDtypeStruct((part, width), F32), sent, sent, sent),
        in_specs=[SMEM_SPEC] + [VMEM_SPEC] * (1 + 2 * SIDE),
        out_specs=(VMEM_SPEC,) * 4,
        scratch_shapes=[
            pltpu.VMEM((links.shape[1], width), BF16),
            pltpu.VMEM((row_block, width), F32),
        ],
        name="neighbours",
        compiler_params=pltpu.CompilerParams(vmem_limit_bytes=16 << 20),
    )(place, *near_core(links, *mine, *other))


def shifted(value, first, second, swap=0):
    pairs = []
    for y in range(SIDE):
        for z in range(SIDE):
            for c in range(CORES):
                dy, dz = (first, second) if c == 0 else (second, first)
                to = ((y + dy) % SIDE * SIDE + (z + dz) % SIDE) * CORES + (c + swap) % CORES
                pairs.append(((y * SIDE + z) * CORES + c, to))
    return lax.ppermute(value, "col", pairs)


def gather_blocks(update):
    near = [update] + [shifted(update, d, 0) for d in range(1, SIDE)]
    near = jnp.concatenate(near, axis=0)
    far = [near] + [shifted(near, 0, d) for d in range(1, SIDE)]
    return far, [shifted(block, 0, 0, swap=1) for block in far]


def assemble_kernel(place_ref, *refs):
    blocks, out_hbm, store_sem = refs[:-2], refs[-2], refs[-1]
    part = blocks[0].shape[0]
    stores = []
    for d, block_ref in enumerate(blocks):
        start = pl.multiple_of((place_ref[0] + len(blocks) - d) % len(blocks) * part, part)
        store = pltpu.make_async_copy(block_ref, out_hbm.at[pl.ds(start, part), :], store_sem.at[d])
        store.start()
        stores.append(store)
    for store in stores:
        store.wait()


def assemble(place, done, moved):
    rows, width = done.shape
    return pl.pallas_call(
        assemble_kernel,
        out_shape=jax.ShapeDtypeStruct((rows * (1 + len(moved)), width), BF16),
        in_specs=[SMEM_SPEC] + [VMEM_SPEC] * (1 + len(moved)),
        out_specs=HBM_SPEC,
        scratch_shapes=[pltpu.SemaphoreType.DMA((1 + len(moved),))],
        name="assemble",
        compiler_params=pltpu.CompilerParams(vmem_limit_bytes=8 << 20),
    )(place, *near_core(done, *moved))


def ring(size, distance):
    return [(i, (i + distance) % size) for i in range(size)]


def per_device(
    node_states,
    walk_nodes,
    walk_lengths,
    adjacency,
    w_xz,
    w_bc,
    w_dt,
    decay_rate,
    w_out,
    w_up,
    w_down,
):
    node_count, width = node_states.shape
    walk_count, walk_len = walk_nodes.shape
    everyone = ("row", "col")
    owners = lax.axis_size(everyone)
    row_size = lax.axis_size("row")
    row_block = adjacency.shape[0]

    my_row = lax.axis_index("row")
    row_global = lax.axis_index("col") * row_block + jnp.arange(row_block, dtype=I32)
    col_global = my_row * adjacency.shape[1] + jnp.arange(adjacency.shape[1], dtype=I32)
    self_link = (row_global[:, None] == col_global[None, :]).astype(I32)
    links = (adjacency + self_link).astype(BF16)
    wanted, slots = route(walk_nodes, walk_lengths, node_count, owners)
    requests = lax.all_to_all(wanted, everyone, split_axis=0, concat_axis=0, tiled=True)
    requests, near_states = lax.optimization_barrier((requests, fetch(node_states)))
    picked, reqrow = pick(requests, near_states)
    arrived = lax.all_to_all(
        picked.reshape(owners, CAP, width), everyone, split_axis=0, concat_axis=0, tiled=True
    )
    late_slots, links = lax.optimization_barrier((slots, links))
    put = placement(late_slots, owners * CAP)
    arrived, links, put = lax.optimization_barrier((arrived, links, put))
    outgoing = encode(
        arrived.reshape(owners * CAP, width),
        slots,
        put,
        w_xz,
        w_bc,
        w_dt,
        decay_rate,
        w_out,
        walk_len,
    )
    returned = lax.all_to_all(
        outgoing.reshape(owners, CAP, width), everyone, split_axis=0, concat_axis=0, tiled=True
    )
    update = update_nodes(returned.reshape(owners * CAP, width), reqrow, near_states)

    mine, other = gather_blocks(update)
    my_col = lax.axis_index("col")
    place = jnp.stack([my_row, my_col // (SIDE * CORES), my_col // CORES % SIDE, my_col % CORES]).astype(I32)
    own, *sent = neighbour_sums(place, links, mine, other)
    parts = [lax.ppermute(block, "row", ring(row_size, d)) for d, block in enumerate(sent, 1)]
    done = finish(own, parts, w_up, w_down)
    moved = [lax.ppermute(done, "row", ring(row_size, d)) for d in range(1, row_size)]
    return assemble(place, done, moved)


def solution(mesh):
    return jax.shard_map(
        per_device,
        mesh=mesh,
        in_specs=(
            P(("row", "col"), None),
            P(("row", "col"), None),
            P(("row", "col")),
            P("col", "row"),
            P(),
            P(),
            P(),
            P(),
            P(),
            P(),
            P(),
        ),
        out_specs=P("col", None),
        check_vma=False,
    )
```

```python
import functools

import jax
import jax.numpy as jnp
from jax import lax
from jax.experimental import pallas as pl
from jax.experimental.pallas import tpu as pltpu
from jax.sharding import PartitionSpec as P

F32 = jnp.float32
BF16 = jnp.bfloat16
I32 = jnp.int32
VMEM_SPEC = pl.BlockSpec(memory_space=pltpu.VMEM)
HBM_SPEC = pl.BlockSpec(memory_space=pltpu.HBM)
SMEM_SPEC = pl.BlockSpec(memory_space=pltpu.SMEM)
CAP = 8
EPS = 1e-05
LOG2E = 1.4426950408889634
SIDE = 4
CORES = 2


def iota(shape, dim):
    return lax.broadcasted_iota(I32, shape, dim)


def mm(a, b):
    return jnp.dot(a, b, preferred_element_type=F32)


def mm_nt(a, b):
    return lax.dot_general(a, b, (((1,), (1,)), ((), ())), preferred_element_type=F32)


def near_core(*arrays):
    return [pltpu.with_memory_space_constraint(a, pltpu.VMEM) for a in arrays]


def in_hbm(*arrays):
    return [pltpu.with_memory_space_constraint(a, pltpu.HBM) for a in arrays]


def onehot(cond):
    return cond.astype(F32).astype(BF16)


def as_column(row):
    return jnp.transpose(jnp.broadcast_to(row, (8, row.shape[1])))[:, 0:1]


def route_kernel(
    nodes_hbm, lengths_hbm, wanted_ref, slots_ref, nodes_ref, lengths_ref, load_sem, *, node_count, owners
):
    load_nodes = pltpu.make_async_copy(nodes_hbm, nodes_ref, load_sem.at[0])
    load_lengths = pltpu.make_async_copy(lengths_hbm, lengths_ref, load_sem.at[1])
    load_nodes.start()
    load_lengths.start()
    load_nodes.wait()
    load_lengths.wait()
    walk_count, walk_len = nodes_ref.shape
    tok = walk_count * walk_len
    place = iota((1, walk_len), 1)
    pieces = []
    for w in range(walk_count):
        live = place < lengths_ref[w]
        pieces.append(jnp.where(live, nodes_ref[w : w + 1, :], -1))
    node_row = jnp.concatenate(pieces, axis=1)
    live_row = node_row >= 0
    owner_row = ((node_row.astype(F32) + 0.5) * (1.0 / node_count)).astype(I32)
    local_row = node_row - owner_row * node_count
    owner_row = jnp.where(live_row, owner_row, -1)
    local_row = jnp.where(live_row, local_row + 1, 0)
    owner_col = as_column(owner_row)
    local_col = as_column(local_row)
    same = owner_col == owner_row
    first_i = iota((tok, tok), 0)
    second_i = iota((tok, tok), 1)
    rank_row = jnp.sum(jnp.where(same & (first_i < second_i), 1.0, 0.0), axis=0, keepdims=True)
    rank_row = rank_row.astype(I32)
    rank_col = as_column(rank_row)
    slot_row = jnp.where(live_row, owner_row * CAP + rank_row, -1)
    slots_ref[...] = jnp.broadcast_to(slot_row, slots_ref.shape)
    by_owner = onehot(iota((owners, tok), 0) == owner_row)
    by_rank = jnp.where(iota((tok, 128), 1) == rank_col, local_col.astype(F32), 0.0).astype(BF16)
    wanted = mm(by_owner, by_rank).astype(I32) - 1
    wanted_ref[...] = wanted[:, :CAP]


def route(walk_nodes, walk_lengths, node_count, owners):
    tok = walk_nodes.shape[0] * walk_nodes.shape[1]
    return pl.pallas_call(
        functools.partial(route_kernel, node_count=node_count, owners=owners),
        out_shape=(
            jax.ShapeDtypeStruct((owners, CAP), I32),
            jax.ShapeDtypeStruct((8, tok), I32),
        ),
        in_specs=[HBM_SPEC, HBM_SPEC],
        out_specs=(VMEM_SPEC, VMEM_SPEC),
        scratch_shapes=[
            pltpu.VMEM(walk_nodes.shape, I32),
            pltpu.SMEM(walk_lengths.shape, I32),
            pltpu.SemaphoreType.DMA((2,)),
        ],
        name="route",
        compiler_params=pltpu.CompilerParams(vmem_limit_bytes=12 << 20),
    )(*in_hbm(walk_nodes, walk_lengths))


def pick_kernel(requests_ref, states_ref, picked_ref, reqrow_ref):
    owners = requests_ref.shape[0]
    node_count = states_ref.shape[0]
    total = owners * CAP
    spread = onehot(iota((total, owners), 0) // CAP == iota((total, owners), 1))
    wide = mm(spread, requests_ref[...].astype(F32).astype(BF16))
    mine = iota((total, CAP), 1) == iota((total, CAP), 0) % CAP
    col = jnp.sum(jnp.where(mine, wide, 0.0), axis=1, keepdims=True).astype(I32)
    chosen = onehot(iota((total, node_count), 1) == col)
    reqrow_ref[...] = jnp.transpose(jnp.broadcast_to(col, (total, 8)))
    picked_ref[...] = mm(chosen, states_ref[...]).astype(BF16)


def pick(requests, node_states):
    total = requests.shape[0] * CAP
    return pl.pallas_call(
        pick_kernel,
        out_shape=(
            jax.ShapeDtypeStruct((total, node_states.shape[1]), BF16),
            jax.ShapeDtypeStruct((8, total), I32),
        ),
        in_specs=[VMEM_SPEC, VMEM_SPEC],
        out_specs=(VMEM_SPEC, VMEM_SPEC),
        name="pick",
        compiler_params=pltpu.CompilerParams(vmem_limit_bytes=12 << 20),
    )(*near_core(requests, node_states))


def placement_kernel(slots_ref, put_ref):
    put_ref[...] = onehot(iota(put_ref.shape, 0) == slots_ref[0:1, :])


def placement(slots, total):
    return pl.pallas_call(
        placement_kernel,
        out_shape=jax.ShapeDtypeStruct((total, slots.shape[1]), BF16),
        in_specs=[VMEM_SPEC],
        out_specs=VMEM_SPEC,
        name="placement",
        compiler_params=pltpu.CompilerParams(vmem_limit_bytes=12 << 20),
    )(*near_core(slots))


def fetch_kernel(*refs):
    count = len(refs) // 2
    loads = [
        pltpu.make_async_copy(refs[n], refs[count + n], refs[-1].at[n]) for n in range(count)
    ]
    for load in loads:
        load.start()
    for load in loads:
        load.wait()


def fetch(*arrays):
    return pl.pallas_call(
        fetch_kernel,
        out_shape=tuple(jax.ShapeDtypeStruct(array.shape, array.dtype) for array in arrays),
        in_specs=[HBM_SPEC] * len(arrays),
        out_specs=(VMEM_SPEC,) * len(arrays),
        scratch_shapes=[pltpu.SemaphoreType.DMA((len(arrays),))],
        name="fetch",
        compiler_params=pltpu.CompilerParams(vmem_limit_bytes=8 << 20),
    )(*in_hbm(*arrays))


PAD = 8


def encode_kernel(
    arrived_ref,
    slots_ref,
    put_hbm,
    w_dt_hbm,
    rate_hbm,
    w_xz_hbm,
    w_bc_hbm,
    w_out_hbm,
    out_ref,
    put_ref,
    w_dt_ref,
    rate_ref,
    w_xz_ref,
    w_bc_ref,
    w_out_ref,
    small_sem,
    weights_sem,
    stream_ref,
    inner_ref,
    gate_ref,
    proj_ref,
    gated_ref,
    cum_ref,
    rows_ref,
    mix_even_ref,
    mix_odd_ref,
    *,
    walk_len,
):
    layers, inner_width, width = w_out_ref.shape
    heads = w_dt_ref.shape[1]
    head_width = inner_width // heads
    state_width = w_bc_ref.shape[2] // 2
    tok = slots_ref.shape[1]
    quads = inner_width // 256
    walks = tok // walk_len
    stride = walk_len + PAD

    load_dt = pltpu.make_async_copy(w_dt_hbm, w_dt_ref, small_sem.at[0])
    load_rate = pltpu.make_async_copy(rate_hbm, rate_ref, small_sem.at[1])
    load_dt.start()
    load_rate.start()
    first_loads = []
    for q in range(2 * quads):
        cols = pl.ds((q // 2 + q % 2 * quads) * 256, 256)
        load = pltpu.make_async_copy(
            w_xz_hbm.at[0, :, cols], w_xz_ref.at[0, :, cols], small_sem.at[3 + q]
        )
        load.start()
        first_loads.append(load)
    loads = []
    for layer in range(layers):
        for q, (source, target) in enumerate(
            ((w_xz_hbm, w_xz_ref), (w_bc_hbm, w_bc_ref), (w_out_hbm, w_out_ref))
        ):
            if layer == 0 and q == 0:
                loads.append(None)
                continue
            load = pltpu.make_async_copy(source.at[layer], target.at[layer], weights_sem.at[layer, q])
            load.start()
            loads.append(load)
    load_put = pltpu.make_async_copy(put_hbm, put_ref, small_sem.at[2])
    load_put.start()

    total = arrived_ref.shape[0]
    take = onehot(iota((tok, total), 1) == as_column(slots_ref[0:1, :]))
    stream_ref[...] = mm(take, arrived_ref[...])
    for w in range(walks):
        cum_ref[:, w * stride : w * stride + PAD, :] = jnp.zeros((2 * quads, PAD, 128), F32)
    mix_odd_ref[...] = jnp.zeros(mix_odd_ref.shape, BF16)
    load_dt.wait()
    load_rate.wait()

    live_row = slots_ref[0:1, :] >= 0
    spread_in = iota((3 * heads, inner_width), 0)
    spread_out = iota((3 * heads, inner_width), 1)
    spread = onehot(spread_in % heads == spread_out // head_width)
    sum_in = iota((128, 256), 0)
    sum_out = iota((128, 256), 1)
    same_walk = sum_in // walk_len == sum_out % 128 // walk_len
    reach = sum_out % walk_len - jnp.where(sum_out >= 128, 1, 0)
    running = onehot(same_walk & (sum_in % walk_len <= reach))
    lane = iota((walk_len, 128), 1)
    left = lane < walk_len
    left_row = iota((1, 128), 1) < walk_len
    t_of = iota((walk_len, 128), 0)
    s_of = lane % walk_len
    earlier = s_of < t_of
    diagonal = jnp.where(s_of == t_of, 1.0, 0.0)
    left_bf = jnp.where(left, 1.0, 0.0).astype(BF16)
    right_bf = jnp.where(left, 0.0, 1.0).astype(BF16)
    nothing = jnp.zeros((walk_len, 128), BF16)

    def split3(v):
        high = v.astype(BF16).astype(F32)
        rest = v - high
        middle = rest.astype(BF16).astype(F32)
        return jnp.concatenate([high, middle, rest - middle], axis=0)

    def walk_rows(walk):
        return pl.ds(pl.multiple_of(walk * walk_len, walk_len), walk_len)

    def half_step(j, odd):
        lanes = pl.ds(pl.multiple_of(j * 128, 128), 128)
        walk = 2 * j + odd
        ahead_ref, behind_ref = (mix_odd_ref, mix_even_ref) if odd else (mix_even_ref, mix_odd_ref)
        previous = walk_rows(jnp.maximum(walk - 1, 0))
        both = proj_ref[walk_rows(walk), :]
        b_in = both[:, :state_width]
        c_out = both[:, state_width:]
        scores = mm_nt(c_out, jnp.concatenate([b_in, b_in], axis=0)) * state_width ** (-0.5)
        here = pl.ds(pl.multiple_of(walk * stride + PAD, PAD), walk_len)
        above = pl.ds(walk * stride + PAD - 1, walk_len)
        for quad in range(quads):
            apply_mix(quad, previous, behind_ref)
            for p in (2 * quad, 2 * quad + 1):

                def row_of(q):
                    a = rows_ref[2 * q + odd, 2 * p : 2 * p + 1, lanes]
                    b = rows_ref[2 * q + 1 - odd, 2 * p + 1 : 2 * p + 2, lanes]
                    return jnp.where(left_row, a, b)

                gap = jnp.where(earlier, cum_ref[p, here, :] - row_of(0), row_of(1) - cum_ref[p, above, :])
                decay = jnp.exp2(gap) + diagonal
                ahead_ref[:, 128 * p : 128 * (p + 1)] = (scores * decay * row_of(2)).astype(BF16)

    def apply_mix(quad, rows, mix_ref):
        tops, bottoms = [], []
        for p in (2 * quad, 2 * quad + 1):
            inner = inner_ref[rows, 128 * p : 128 * (p + 1)]
            tops.append(inner * left_bf)
            bottoms.append(inner * right_bf)
        blocks = jnp.concatenate(
            [
                jnp.concatenate([tops[0], nothing], axis=1),
                jnp.concatenate([bottoms[0], nothing], axis=1),
                jnp.concatenate([nothing, tops[1]], axis=1),
                jnp.concatenate([nothing, bottoms[1]], axis=1),
            ],
            axis=0,
        )
        cols = slice(256 * quad, 256 * (quad + 1))
        mixed = mm(mix_ref[:, cols], blocks)
        gated_ref[rows, cols] = (mixed * gate_ref[rows, cols]).astype(BF16)

    def walk_pair(j, carry):
        half_step(j, 0)
        half_step(j, 1)
        return carry

    for layer in range(layers):
        x = stream_ref[...]
        normed = (x * lax.rsqrt(jnp.mean(x * x, axis=-1, keepdims=True) + EPS)).astype(BF16)

        def project(q):
            cols = slice(256 * q, 256 * (q + 1))
            if layer == 0:
                first_loads[2 * q].wait()
                first_loads[2 * q + 1].wait()
            inner_ref[:, cols] = mm(normed, w_xz_ref[layer, :, cols]).astype(BF16)
            gate_cols = slice(inner_width + 256 * q, inner_width + 256 * (q + 1))
            half_gate = 0.5 * mm(normed, w_xz_ref[layer, :, gate_cols])
            gate_ref[:, cols] = half_gate + half_gate * jnp.tanh(half_gate)

        raw = mm_nt(w_dt_ref[layer], normed)
        if layer > 0:
            loads[3 * layer].wait()
        project(0)
        step = jnp.maximum(raw, 0.0) + jnp.log1p(jnp.exp(-jnp.abs(raw)))
        rate = as_column(rate_ref[layer : layer + 1, :])
        pieces = split3((-LOG2E * rate) * step).astype(BF16)
        source = jnp.where(live_row, step, 0.0)
        project(1)
        cums = []
        for j in range(walks // 2):
            lanes = slice(128 * j, 128 * (j + 1))
            sums = mm(pieces[:, lanes], running)
            sums = sums[:heads] + (sums[heads : 2 * heads] + sums[2 * heads :])
            cums.append(sums[:, :128])
            for q, v in enumerate((sums[:, :128], sums[:, 128:], source[:, lanes])):
                rows_ref[2 * q, :, lanes] = v
                rows_ref[2 * q + 1, :, lanes] = pltpu.roll(v, walk_len, 1)
        project(2)
        columns = jnp.transpose(split3(jnp.concatenate(cums, axis=1))).astype(BF16)
        project(3)
        loads[3 * layer + 1].wait()
        proj_ref[...] = mm(normed, w_bc_ref[layer]).astype(BF16)
        for quad in range(quads):
            wide = mm(columns, spread[:, 256 * quad : 256 * (quad + 1)])
            for w in range(walks):
                block = wide[w * walk_len : (w + 1) * walk_len, :]
                rows = slice(w * stride + PAD, (w + 1) * stride)
                cum_ref[2 * quad, rows, :] = block[:, :128]
                cum_ref[2 * quad + 1, rows, :] = block[:, 128:]

        lax.fori_loop(0, walks // 2, walk_pair, 0)
        for quad in range(quads):
            apply_mix(quad, walk_rows(walks - 1), mix_odd_ref)
        loads[3 * layer + 2].wait()
        stream = x + mm(gated_ref[...], w_out_ref[layer])
        stream_ref[...] = stream.astype(BF16).astype(F32)

    load_put.wait()
    out_ref[...] = mm(put_ref[...], stream_ref[...].astype(BF16)).astype(BF16)


def encode(arrived, slots, put, w_xz, w_bc, w_dt, decay_rate, w_out, walk_len):
    total, width = arrived.shape
    tok = slots.shape[1]
    inner_width = w_out.shape[1]
    w_dt = jnp.swapaxes(w_dt, 1, 2)
    return pl.pallas_call(
        functools.partial(encode_kernel, walk_len=walk_len),
        out_shape=jax.ShapeDtypeStruct((total, width), BF16),
        in_specs=[VMEM_SPEC] * 2 + [HBM_SPEC] * 6,
        out_specs=VMEM_SPEC,
        scratch_shapes=[
            pltpu.VMEM(put.shape, BF16),
            pltpu.VMEM(w_dt.shape, BF16),
            pltpu.VMEM(decay_rate.shape, F32),
            pltpu.VMEM(w_xz.shape, BF16),
            pltpu.VMEM(w_bc.shape, BF16),
            pltpu.VMEM(w_out.shape, BF16),
            pltpu.SemaphoreType.DMA((3 + inner_width // 128,)),
            pltpu.SemaphoreType.DMA((w_out.shape[0], 3)),
            pltpu.VMEM((tok, width), F32),
            pltpu.VMEM((tok, inner_width), BF16),
            pltpu.VMEM((tok, inner_width), F32),
            pltpu.VMEM((tok, w_bc.shape[2]), BF16),
            pltpu.VMEM((tok, inner_width), BF16),
            pltpu.VMEM((inner_width // 128, tok // walk_len * (walk_len + PAD), 128), F32),
            pltpu.VMEM((6, w_dt.shape[1], tok), F32),
            pltpu.VMEM((walk_len, inner_width), BF16),
            pltpu.VMEM((walk_len, inner_width), BF16),
        ],
        name="encode",
        compiler_params=pltpu.CompilerParams(vmem_limit_bytes=36 << 20),
    )(*near_core(arrived, slots), *in_hbm(put, w_dt, decay_rate, w_xz, w_bc, w_out))


def links_kernel(place_ref, adjacency_hbm, links_ref, block_ref, load_sem):
    rows, cols = links_ref.shape
    chunks = load_sem.shape[0]
    size = rows // chunks
    loads = []
    for n in range(chunks):
        part = pl.ds(n * size, size)
        load = pltpu.make_async_copy(adjacency_hbm.at[part, :], block_ref.at[part, :], load_sem.at[n])
        load.start()
        loads.append(load)
    my_row, y, z, core = place_ref[0], place_ref[1], place_ref[2], place_ref[3]
    first_row = ((y * SIDE + z) * CORES + core) * rows
    offset = first_row - my_row * cols
    for n in range(chunks):
        loads[n].wait()
        diagonal = iota((size, cols), 1) - iota((size, cols), 0) == offset + n * size
        block = block_ref[n * size : (n + 1) * size, :] + diagonal.astype(I32)
        links_ref[n * size : (n + 1) * size, :] = block.astype(F32).astype(BF16)


def make_links(place, adjacency):
    chunks = 6
    return pl.pallas_call(
        links_kernel,
        out_shape=jax.ShapeDtypeStruct(adjacency.shape, BF16),
        in_specs=[SMEM_SPEC, HBM_SPEC],
        out_specs=VMEM_SPEC,
        scratch_shapes=[pltpu.VMEM(adjacency.shape, I32), pltpu.SemaphoreType.DMA((chunks,))],
        name="links",
        compiler_params=pltpu.CompilerParams(vmem_limit_bytes=16 << 20),
    )(place, *in_hbm(adjacency))


def update_kernel(returned_ref, reqrow_ref, states_ref, out_ref):
    node_count = states_ref.shape[0]
    total = returned_ref.shape[0]
    member = jnp.where(iota((node_count, total), 0) == reqrow_ref[0:1, :], 1.0, 0.0)
    visits = jnp.sum(member, axis=1, keepdims=True)
    summed = mm(member.astype(BF16), returned_ref[...])
    out_ref[...] = (states_ref[...].astype(F32) + summed / (1.0 + visits)).astype(BF16)


def update_nodes(returned, reqrow, node_states):
    return pl.pallas_call(
        update_kernel,
        out_shape=jax.ShapeDtypeStruct(node_states.shape, BF16),
        in_specs=[VMEM_SPEC] * 3,
        out_specs=VMEM_SPEC,
        name="update",
        compiler_params=pltpu.CompilerParams(vmem_limit_bytes=12 << 20),
    )(*near_core(returned, reqrow, node_states))


def finish_kernel(own_ref, one_ref, two_ref, three_ref, w_up_ref, w_down_ref, out_ref):
    combined = (own_ref[...] + one_ref[...].astype(F32)) + (
        two_ref[...].astype(F32) + three_ref[...].astype(F32)
    )
    centred = combined - jnp.mean(combined, axis=-1, keepdims=True)
    normal = centred * lax.rsqrt(jnp.mean(centred * centred, axis=-1, keepdims=True) + EPS)
    hidden = jax.nn.gelu(mm(normal.astype(BF16), w_up_ref[...])).astype(BF16)
    out_ref[...] = (normal + mm(hidden, w_down_ref[...])).astype(BF16)


def finish(own, parts, w_up, w_down):
    return pl.pallas_call(
        finish_kernel,
        out_shape=jax.ShapeDtypeStruct(own.shape, BF16),
        in_specs=[VMEM_SPEC] * 6,
        out_specs=VMEM_SPEC,
        name="finish",
        compiler_params=pltpu.CompilerParams(vmem_limit_bytes=12 << 20),
    )(own, *near_core(*parts, w_up, w_down))


def neighbour_kernel(place_ref, links_ref, *refs):
    mine, other = refs[:SIDE], refs[SIDE : 2 * SIDE]
    own_ref, one_ref, two_ref, three_ref, piece_ref, sums_ref = refs[2 * SIDE :]
    my_row, y, z, core = place_ref[0], place_ref[1], place_ref[2], place_ref[3]
    rows = mine[0].shape[0] // SIDE
    for e in range(SIDE):
        for d in range(SIDE):
            for ref, who in ((mine[e], core), (other[e], 1 - core)):
                dy = d + who * (e - d)
                dz = e + who * (d - e)
                device = ((y + SIDE - dy) % SIDE * SIDE + (z + SIDE - dz) % SIDE) * CORES + who
                target = pl.multiple_of(device * rows, rows)
                piece_ref[pl.ds(target, rows), :] = ref[d * rows : (d + 1) * rows, :]
    sums_ref[...] = mm(links_ref[...], piece_ref[...])
    part = own_ref.shape[0]

    def block(distance):
        start = pl.multiple_of((my_row + distance) % SIDE * part, part)
        return sums_ref[pl.ds(start, part), :]

    own_ref[...] = block(0)
    one_ref[...] = block(1).astype(BF16)
    two_ref[...] = block(2).astype(BF16)
    three_ref[...] = block(3).astype(BF16)


def neighbour_sums(place, links, mine, other):
    row_block, width = links.shape[0], mine[0].shape[1]
    part = row_block // SIDE
    sent = jax.ShapeDtypeStruct((part, width), BF16)
    return pl.pallas_call(
        neighbour_kernel,
        out_shape=(jax.ShapeDtypeStruct((part, width), F32), sent, sent, sent),
        in_specs=[SMEM_SPEC] + [VMEM_SPEC] * (1 + 2 * SIDE),
        out_specs=(VMEM_SPEC,) * 4,
        scratch_shapes=[
            pltpu.VMEM((links.shape[1], width), BF16),
            pltpu.VMEM((row_block, width), F32),
        ],
        name="neighbours",
        compiler_params=pltpu.CompilerParams(vmem_limit_bytes=16 << 20),
    )(place, *near_core(links, *mine, *other))


def shifted(value, first, second, swap=0):
    pairs = []
    for y in range(SIDE):
        for z in range(SIDE):
            for c in range(CORES):
                dy, dz = (first, second) if c == 0 else (second, first)
                to = ((y + dy) % SIDE * SIDE + (z + dz) % SIDE) * CORES + (c + swap) % CORES
                pairs.append(((y * SIDE + z) * CORES + c, to))
    return lax.ppermute(value, "col", pairs)


def gather_blocks(update):
    near = [update] + [shifted(update, d, 0) for d in range(1, SIDE)]
    near = jnp.concatenate(near, axis=0)
    far = [near] + [shifted(near, 0, d) for d in range(1, SIDE)]
    return far, [shifted(block, 0, 0, swap=1) for block in far]


def assemble_kernel(place_ref, *refs):
    blocks, out_hbm, store_sem = refs[:-2], refs[-2], refs[-1]
    part = blocks[0].shape[0]
    stores = []
    for d, block_ref in enumerate(blocks):
        start = pl.multiple_of((place_ref[0] + len(blocks) - d) % len(blocks) * part, part)
        store = pltpu.make_async_copy(block_ref, out_hbm.at[pl.ds(start, part), :], store_sem.at[d])
        store.start()
        stores.append(store)
    for store in stores:
        store.wait()


def assemble(place, done, moved):
    rows, width = done.shape
    return pl.pallas_call(
        assemble_kernel,
        out_shape=jax.ShapeDtypeStruct((rows * (1 + len(moved)), width), BF16),
        in_specs=[SMEM_SPEC] + [VMEM_SPEC] * (1 + len(moved)),
        out_specs=HBM_SPEC,
        scratch_shapes=[pltpu.SemaphoreType.DMA((1 + len(moved),))],
        name="assemble",
        compiler_params=pltpu.CompilerParams(vmem_limit_bytes=8 << 20),
    )(place, *near_core(done, *moved))


def ring(size, distance):
    return [(i, (i + distance) % size) for i in range(size)]


def per_device(
    node_states,
    walk_nodes,
    walk_lengths,
    adjacency,
    w_xz,
    w_bc,
    w_dt,
    decay_rate,
    w_out,
    w_up,
    w_down,
):
    node_count, width = node_states.shape
    walk_count, walk_len = walk_nodes.shape
    everyone = ("row", "col")
    owners = lax.axis_size(everyone)
    row_size = lax.axis_size("row")
    row_block = adjacency.shape[0]

    my_row = lax.axis_index("row")
    my_col = lax.axis_index("col")
    place = jnp.stack([my_row, my_col // (SIDE * CORES), my_col // CORES % SIDE, my_col % CORES]).astype(I32)
    wanted, slots = route(walk_nodes, walk_lengths, node_count, owners)
    requests = lax.all_to_all(wanted, everyone, split_axis=0, concat_axis=0, tiled=True)
    requests, near_states, place = lax.optimization_barrier((requests, fetch(node_states)[0], place))
    picked, reqrow = pick(requests, near_states)
    arrived = lax.all_to_all(
        picked.reshape(owners, CAP, width), everyone, split_axis=0, concat_axis=0, tiled=True
    )
    links = make_links(place, adjacency)
    put = placement(slots, owners * CAP)
    arrived, links, put = lax.optimization_barrier((arrived, links, put))
    outgoing = encode(
        arrived.reshape(owners * CAP, width),
        slots,
        put,
        w_xz,
        w_bc,
        w_dt,
        decay_rate,
        w_out,
        walk_len,
    )
    returned = lax.all_to_all(
        outgoing.reshape(owners, CAP, width), everyone, split_axis=0, concat_axis=0, tiled=True
    )
    update = update_nodes(returned.reshape(owners * CAP, width), reqrow, near_states)

    mine, other = gather_blocks(update)
    own, *sent = neighbour_sums(place, links, mine, other)
    parts = [lax.ppermute(block, "row", ring(row_size, d)) for d, block in enumerate(sent, 1)]
    own, w_up, w_down = lax.optimization_barrier((own, w_up, w_down))
    done = finish(own, parts, *fetch(w_up, w_down))
    moved = [lax.ppermute(done, "row", ring(row_size, d)) for d in range(1, row_size)]
    return assemble(place, done, moved)


def solution(mesh):
    return jax.shard_map(
        per_device,
        mesh=mesh,
        in_specs=(
            P(("row", "col"), None),
            P(("row", "col"), None),
            P(("row", "col")),
            P("col", "row"),
            P(),
            P(),
            P(),
            P(),
            P(),
            P(),
            P(),
        ),
        out_specs=P("col", None),
        check_vma=False,
    )
```

```python
import functools

import jax
import jax.numpy as jnp
from jax import lax
from jax.experimental import pallas as pl
from jax.experimental.pallas import tpu as pltpu
from jax.sharding import PartitionSpec as P

F32 = jnp.float32
BF16 = jnp.bfloat16
I32 = jnp.int32
VMEM_SPEC = pl.BlockSpec(memory_space=pltpu.VMEM)
HBM_SPEC = pl.BlockSpec(memory_space=pltpu.HBM)
SMEM_SPEC = pl.BlockSpec(memory_space=pltpu.SMEM)
CAP = 8
EPS = 1e-05
LOG2E = 1.4426950408889634
SIDE = 4
CORES = 2


def iota(shape, dim):
    return lax.broadcasted_iota(I32, shape, dim)


def mm(a, b):
    return jnp.dot(a, b, preferred_element_type=F32)


def mm_nt(a, b):
    return lax.dot_general(a, b, (((1,), (1,)), ((), ())), preferred_element_type=F32)


def near_core(*arrays):
    return [pltpu.with_memory_space_constraint(a, pltpu.VMEM) for a in arrays]


def in_hbm(*arrays):
    return [pltpu.with_memory_space_constraint(a, pltpu.HBM) for a in arrays]


def onehot(cond):
    return cond.astype(F32).astype(BF16)


def as_column(row):
    return jnp.transpose(jnp.broadcast_to(row, (8, row.shape[1])))[:, 0:1]


def route_kernel(
    nodes_hbm, lengths_hbm, wanted_ref, slots_ref, nodes_ref, lengths_ref, load_sem, *, node_count, owners
):
    load_nodes = pltpu.make_async_copy(nodes_hbm, nodes_ref, load_sem.at[0])
    load_lengths = pltpu.make_async_copy(lengths_hbm, lengths_ref, load_sem.at[1])
    load_nodes.start()
    load_lengths.start()
    load_nodes.wait()
    load_lengths.wait()
    walk_count, walk_len = nodes_ref.shape
    tok = walk_count * walk_len
    place = iota((1, walk_len), 1)
    pieces = []
    for w in range(walk_count):
        live = place < lengths_ref[w]
        pieces.append(jnp.where(live, nodes_ref[w : w + 1, :], -1))
    node_row = jnp.concatenate(pieces, axis=1)
    live_row = node_row >= 0
    owner_row = ((node_row.astype(F32) + 0.5) * (1.0 / node_count)).astype(I32)
    local_row = node_row - owner_row * node_count
    owner_row = jnp.where(live_row, owner_row, -1)
    local_row = jnp.where(live_row, local_row + 1, 0)
    owner_col = as_column(owner_row)
    local_col = as_column(local_row)
    same = owner_col == owner_row
    first_i = iota((tok, tok), 0)
    second_i = iota((tok, tok), 1)
    rank_row = jnp.sum(jnp.where(same & (first_i < second_i), 1.0, 0.0), axis=0, keepdims=True)
    rank_row = rank_row.astype(I32)
    rank_col = as_column(rank_row)
    slot_row = jnp.where(live_row, owner_row * CAP + rank_row, -1)
    slots_ref[...] = jnp.broadcast_to(slot_row, slots_ref.shape)
    by_owner = onehot(iota((owners, tok), 0) == owner_row)
    by_rank = jnp.where(iota((tok, 128), 1) == rank_col, local_col.astype(F32), 0.0).astype(BF16)
    wanted = mm(by_owner, by_rank).astype(I32) - 1
    wanted_ref[...] = wanted[:, :CAP]


def route(walk_nodes, walk_lengths, node_count, owners):
    tok = walk_nodes.shape[0] * walk_nodes.shape[1]
    return pl.pallas_call(
        functools.partial(route_kernel, node_count=node_count, owners=owners),
        out_shape=(
            jax.ShapeDtypeStruct((owners, CAP), I32),
            jax.ShapeDtypeStruct((8, tok), I32),
        ),
        in_specs=[HBM_SPEC, HBM_SPEC],
        out_specs=(VMEM_SPEC, VMEM_SPEC),
        scratch_shapes=[
            pltpu.VMEM(walk_nodes.shape, I32),
            pltpu.SMEM(walk_lengths.shape, I32),
            pltpu.SemaphoreType.DMA((2,)),
        ],
        name="route",
        compiler_params=pltpu.CompilerParams(vmem_limit_bytes=12 << 20),
    )(*in_hbm(walk_nodes, walk_lengths))


def pick_kernel(requests_ref, states_ref, picked_ref, reqrow_ref):
    owners = requests_ref.shape[0]
    node_count = states_ref.shape[0]
    total = owners * CAP
    spread = onehot(iota((total, owners), 0) // CAP == iota((total, owners), 1))
    wide = mm(spread, requests_ref[...].astype(F32).astype(BF16))
    mine = iota((total, CAP), 1) == iota((total, CAP), 0) % CAP
    col = jnp.sum(jnp.where(mine, wide, 0.0), axis=1, keepdims=True).astype(I32)
    chosen = onehot(iota((total, node_count), 1) == col)
    reqrow_ref[...] = jnp.transpose(jnp.broadcast_to(col, (total, 8)))
    picked_ref[...] = mm(chosen, states_ref[...]).astype(BF16)


def pick(requests, node_states):
    total = requests.shape[0] * CAP
    return pl.pallas_call(
        pick_kernel,
        out_shape=(
            jax.ShapeDtypeStruct((total, node_states.shape[1]), BF16),
            jax.ShapeDtypeStruct((8, total), I32),
        ),
        in_specs=[VMEM_SPEC, VMEM_SPEC],
        out_specs=(VMEM_SPEC, VMEM_SPEC),
        name="pick",
        compiler_params=pltpu.CompilerParams(vmem_limit_bytes=12 << 20),
    )(*near_core(requests, node_states))


def placement_kernel(slots_ref, put_ref):
    put_ref[...] = onehot(iota(put_ref.shape, 0) == slots_ref[0:1, :])


def placement(slots, total):
    return pl.pallas_call(
        placement_kernel,
        out_shape=jax.ShapeDtypeStruct((total, slots.shape[1]), BF16),
        in_specs=[VMEM_SPEC],
        out_specs=VMEM_SPEC,
        name="placement",
        compiler_params=pltpu.CompilerParams(vmem_limit_bytes=12 << 20),
    )(*near_core(slots))


def fetch_kernel(*refs):
    count = len(refs) // 2
    loads = [
        pltpu.make_async_copy(refs[n], refs[count + n], refs[-1].at[n]) for n in range(count)
    ]
    for load in loads:
        load.start()
    for load in loads:
        load.wait()


def fetch(*arrays):
    return pl.pallas_call(
        fetch_kernel,
        out_shape=tuple(jax.ShapeDtypeStruct(array.shape, array.dtype) for array in arrays),
        in_specs=[HBM_SPEC] * len(arrays),
        out_specs=(VMEM_SPEC,) * len(arrays),
        scratch_shapes=[pltpu.SemaphoreType.DMA((len(arrays),))],
        name="fetch",
        compiler_params=pltpu.CompilerParams(vmem_limit_bytes=8 << 20),
    )(*in_hbm(*arrays))


PAD = 8


def encode_kernel(
    arrived_ref,
    slots_ref,
    put_hbm,
    w_dt_hbm,
    rate_hbm,
    w_xz_hbm,
    w_bc_hbm,
    w_out_hbm,
    out_ref,
    put_ref,
    w_dt_ref,
    rate_ref,
    w_xz_ref,
    w_bc_ref,
    w_out_ref,
    small_sem,
    weights_sem,
    stream_ref,
    inner_left_ref,
    inner_right_ref,
    gate_ref,
    scores_ref,
    gated_ref,
    cum_ref,
    rows_ref,
    mix_even_ref,
    mix_odd_ref,
    *,
    walk_len,
):
    layers, inner_width, width = w_out_ref.shape
    heads = w_dt_ref.shape[1]
    head_width = inner_width // heads
    state_width = w_bc_ref.shape[2] // 2
    tok = slots_ref.shape[1]
    quads = inner_width // 256
    walks = tok // walk_len
    stride = walk_len + PAD

    load_dt = pltpu.make_async_copy(w_dt_hbm, w_dt_ref, small_sem.at[0])
    load_rate = pltpu.make_async_copy(rate_hbm, rate_ref, small_sem.at[1])
    load_dt.start()
    load_rate.start()
    first_loads = []
    for q in range(2 * quads):
        cols = pl.ds((q // 2 + q % 2 * quads) * 256, 256)
        load = pltpu.make_async_copy(
            w_xz_hbm.at[0, :, cols], w_xz_ref.at[0, :, cols], small_sem.at[3 + q]
        )
        load.start()
        first_loads.append(load)
    loads = []
    for layer in range(layers):
        for q, (source, target) in enumerate(
            ((w_xz_hbm, w_xz_ref), (w_bc_hbm, w_bc_ref), (w_out_hbm, w_out_ref))
        ):
            if layer == 0 and q == 0:
                loads.append(None)
                continue
            load = pltpu.make_async_copy(source.at[layer], target.at[layer], weights_sem.at[layer, q])
            load.start()
            loads.append(load)
    load_put = pltpu.make_async_copy(put_hbm, put_ref, small_sem.at[2])
    load_put.start()

    total = arrived_ref.shape[0]
    take = onehot(iota((tok, total), 1) == as_column(slots_ref[0:1, :]))
    stream_ref[...] = mm(take, arrived_ref[...])
    for w in range(walks):
        cum_ref[:, w * stride : w * stride + PAD, :] = jnp.zeros((2 * quads, PAD, 128), F32)
    mix_odd_ref[...] = jnp.zeros(mix_odd_ref.shape, BF16)
    load_dt.wait()
    load_rate.wait()

    live_row = slots_ref[0:1, :] >= 0
    spread_in = iota((3 * heads, inner_width), 0)
    spread_out = iota((3 * heads, inner_width), 1)
    spread = onehot(spread_in % heads == spread_out // head_width)
    sum_in = iota((128, 256), 0)
    sum_out = iota((128, 256), 1)
    same_walk = sum_in // walk_len == sum_out % 128 // walk_len
    reach = sum_out % walk_len - jnp.where(sum_out >= 128, 1, 0)
    running = onehot(same_walk & (sum_in % walk_len <= reach))
    lane = iota((walk_len, 128), 1)
    left_row = iota((1, 128), 1) < walk_len
    t_of = iota((walk_len, 128), 0)
    s_of = lane % walk_len
    earlier = s_of < t_of
    weight = jnp.where(s_of == t_of, 2.0, 1.0) * state_width ** (-0.5)
    left_cols = iota((1, 256), 1) % 128 < walk_len
    nothing = jnp.zeros((walk_len, 128), BF16)

    def split3(v):
        high = v.astype(BF16).astype(F32)
        rest = v - high
        middle = rest.astype(BF16).astype(F32)
        return jnp.concatenate([high, middle, rest - middle], axis=0)

    def walk_rows(walk):
        return pl.ds(walk * walk_len, walk_len)

    def half_step(j, odd):
        lanes = pl.ds(j * 128, 128)
        walk = 2 * j + odd
        ahead_ref, behind_ref = (mix_odd_ref, mix_even_ref) if odd else (mix_even_ref, mix_odd_ref)
        previous = walk_rows(max(walk - 1, 0))
        scores = scores_ref[walk_rows(walk), :]
        here = pl.ds(walk * stride + PAD, walk_len)
        above = pl.ds(walk * stride + PAD - 1, walk_len)
        for quad in range(quads):
            if walk > 0:
                apply_mix(quad, previous, behind_ref)
            for p in (2 * quad, 2 * quad + 1):

                def row_of(q):
                    a = rows_ref[2 * q + odd, 2 * p : 2 * p + 1, lanes]
                    b = rows_ref[2 * q + 1 - odd, 2 * p + 1 : 2 * p + 2, lanes]
                    return jnp.where(left_row, a, b)

                gap = jnp.where(earlier, cum_ref[p, here, :] - row_of(0), row_of(1) - cum_ref[p, above, :])
                mix = scores * jnp.exp2(gap) * row_of(2)
                ahead_ref[:, 128 * p : 128 * (p + 1)] = mix.astype(BF16)

    def apply_mix(quad, rows, mix_ref):
        tops, bottoms = [], []
        for p in (2 * quad, 2 * quad + 1):
            tops.append(inner_left_ref[rows, 128 * p : 128 * (p + 1)])
            bottoms.append(inner_right_ref[rows, 128 * p : 128 * (p + 1)])
        blocks = jnp.concatenate(
            [
                jnp.concatenate([tops[0], nothing], axis=1),
                jnp.concatenate([bottoms[0], nothing], axis=1),
                jnp.concatenate([nothing, tops[1]], axis=1),
                jnp.concatenate([nothing, bottoms[1]], axis=1),
            ],
            axis=0,
        )
        cols = slice(256 * quad, 256 * (quad + 1))
        mixed = mm(mix_ref[:, cols], blocks)
        gated_ref[rows, cols] = (mixed * gate_ref[rows, cols]).astype(BF16)

    def walk_pair(j, carry):
        half_step(j, 0)
        half_step(j, 1)
        return carry

    for layer in range(layers):
        x = stream_ref[...]
        normed = (x * lax.rsqrt(jnp.mean(x * x, axis=-1, keepdims=True) + EPS)).astype(BF16)

        def project(q):
            cols = slice(256 * q, 256 * (q + 1))
            if layer == 0 and q < 2:
                for load in first_loads[2 * q : 2 if q == 0 else None]:
                    load.wait()
            inner = mm(normed, w_xz_ref[layer, :, cols])
            inner_left_ref[:, cols] = jnp.where(left_cols, inner, 0.0).astype(BF16)
            inner_right_ref[:, cols] = jnp.where(left_cols, 0.0, inner).astype(BF16)
            gate_cols = slice(inner_width + 256 * q, inner_width + 256 * (q + 1))
            half_gate = 0.5 * mm(normed, w_xz_ref[layer, :, gate_cols])
            gate_ref[:, cols] = half_gate + half_gate * jnp.tanh(half_gate)

        raw = mm_nt(w_dt_ref[layer], normed)
        if layer > 0:
            loads[3 * layer].wait()
        project(0)
        step = jnp.maximum(raw, 0.0) + jnp.log1p(jnp.exp(-jnp.abs(raw)))
        rate = as_column(rate_ref[layer : layer + 1, :])
        pieces = split3((-LOG2E * rate) * step).astype(BF16)
        source = jnp.where(live_row, step, 0.0)
        project(1)
        cums = []
        for j in range(walks // 2):
            lanes = slice(128 * j, 128 * (j + 1))
            sums = mm(pieces[:, lanes], running)
            sums = sums[:heads] + (sums[heads : 2 * heads] + sums[2 * heads :])
            cums.append(sums[:, :128])
            for q, v in enumerate((sums[:, :128], sums[:, 128:], source[:, lanes])):
                rows_ref[2 * q, :, lanes] = v
                rows_ref[2 * q + 1, :, lanes] = pltpu.roll(v, walk_len, 1)
        project(2)
        columns = jnp.transpose(split3(jnp.concatenate(cums, axis=1))).astype(BF16)
        project(3)
        loads[3 * layer + 1].wait()
        proj = mm(normed, w_bc_ref[layer]).astype(BF16)
        for w in range(walks):
            b_in = proj[w * walk_len : (w + 1) * walk_len, :state_width]
            c_out = proj[w * walk_len : (w + 1) * walk_len, state_width:]
            scores = mm_nt(c_out, jnp.concatenate([b_in, b_in], axis=0))
            scores_ref[w * walk_len : (w + 1) * walk_len, :] = scores * weight
        for quad in range(quads):
            wide = mm(columns, spread[:, 256 * quad : 256 * (quad + 1)])
            for w in range(walks):
                block = wide[w * walk_len : (w + 1) * walk_len, :]
                rows = slice(w * stride + PAD, (w + 1) * stride)
                cum_ref[2 * quad, rows, :] = block[:, :128]
                cum_ref[2 * quad + 1, rows, :] = block[:, 128:]

        for j in range(walks // 2):
            walk_pair(j, 0)
        for quad in range(quads):
            apply_mix(quad, walk_rows(walks - 1), mix_odd_ref)
        loads[3 * layer + 2].wait()
        stream = x + mm(gated_ref[...], w_out_ref[layer])
        stream_ref[...] = stream.astype(BF16).astype(F32)

    load_put.wait()
    out_ref[...] = mm(put_ref[...], stream_ref[...].astype(BF16)).astype(BF16)


def encode(arrived, slots, put, w_xz, w_bc, w_dt, decay_rate, w_out, walk_len):
    total, width = arrived.shape
    tok = slots.shape[1]
    inner_width = w_out.shape[1]
    w_dt = jnp.swapaxes(w_dt, 1, 2)
    return pl.pallas_call(
        functools.partial(encode_kernel, walk_len=walk_len),
        out_shape=jax.ShapeDtypeStruct((total, width), BF16),
        in_specs=[VMEM_SPEC] * 2 + [HBM_SPEC] * 6,
        out_specs=VMEM_SPEC,
        scratch_shapes=[
            pltpu.VMEM(put.shape, BF16),
            pltpu.VMEM(w_dt.shape, BF16),
            pltpu.VMEM(decay_rate.shape, F32),
            pltpu.VMEM(w_xz.shape, BF16),
            pltpu.VMEM(w_bc.shape, BF16),
            pltpu.VMEM(w_out.shape, BF16),
            pltpu.SemaphoreType.DMA((3 + inner_width // 128,)),
            pltpu.SemaphoreType.DMA((w_out.shape[0], 3)),
            pltpu.VMEM((tok, width), F32),
            pltpu.VMEM((tok, inner_width), BF16),
            pltpu.VMEM((tok, inner_width), BF16),
            pltpu.VMEM((tok, inner_width), F32),
            pltpu.VMEM((tok, 128), F32),
            pltpu.VMEM((tok, inner_width), BF16),
            pltpu.VMEM((inner_width // 128, tok // walk_len * (walk_len + PAD), 128), F32),
            pltpu.VMEM((6, w_dt.shape[1], tok), F32),
            pltpu.VMEM((walk_len, inner_width), BF16),
            pltpu.VMEM((walk_len, inner_width), BF16),
        ],
        name="encode",
        compiler_params=pltpu.CompilerParams(vmem_limit_bytes=36 << 20),
    )(*near_core(arrived, slots), *in_hbm(put, w_dt, decay_rate, w_xz, w_bc, w_out))


def links_kernel(place_ref, adjacency_hbm, links_ref, block_ref, load_sem):
    rows, cols = links_ref.shape
    chunks = load_sem.shape[0]
    size = rows // chunks
    loads = []
    for n in range(chunks):
        part = pl.ds(n * size, size)
        load = pltpu.make_async_copy(adjacency_hbm.at[part, :], block_ref.at[part, :], load_sem.at[n])
        load.start()
        loads.append(load)
    my_row, y, z, core = place_ref[0], place_ref[1], place_ref[2], place_ref[3]
    first_row = ((y * SIDE + z) * CORES + core) * rows
    offset = first_row - my_row * cols
    for n in range(chunks):
        loads[n].wait()
        diagonal = iota((size, cols), 1) - iota((size, cols), 0) == offset + n * size
        block = block_ref[n * size : (n + 1) * size, :] + diagonal.astype(I32)
        links_ref[n * size : (n + 1) * size, :] = block.astype(F32).astype(BF16)


def make_links(place, adjacency):
    chunks = 6
    return pl.pallas_call(
        links_kernel,
        out_shape=jax.ShapeDtypeStruct(adjacency.shape, BF16),
        in_specs=[SMEM_SPEC, HBM_SPEC],
        out_specs=VMEM_SPEC,
        scratch_shapes=[pltpu.VMEM(adjacency.shape, I32), pltpu.SemaphoreType.DMA((chunks,))],
        name="links",
        compiler_params=pltpu.CompilerParams(vmem_limit_bytes=16 << 20),
    )(place, *in_hbm(adjacency))


def update_kernel(returned_ref, reqrow_ref, states_ref, out_ref):
    node_count = states_ref.shape[0]
    total = returned_ref.shape[0]
    member = jnp.where(iota((node_count, total), 0) == reqrow_ref[0:1, :], 1.0, 0.0)
    visits = jnp.sum(member, axis=1, keepdims=True)
    summed = mm(member.astype(BF16), returned_ref[...])
    out_ref[...] = (states_ref[...].astype(F32) + summed / (1.0 + visits)).astype(BF16)


def update_nodes(returned, reqrow, node_states):
    return pl.pallas_call(
        update_kernel,
        out_shape=jax.ShapeDtypeStruct(node_states.shape, BF16),
        in_specs=[VMEM_SPEC] * 3,
        out_specs=VMEM_SPEC,
        name="update",
        compiler_params=pltpu.CompilerParams(vmem_limit_bytes=12 << 20),
    )(*near_core(returned, reqrow, node_states))


def finish_kernel(own_ref, one_ref, two_ref, three_ref, w_up_ref, w_down_ref, out_ref):
    combined = (own_ref[...] + one_ref[...].astype(F32)) + (
        two_ref[...].astype(F32) + three_ref[...].astype(F32)
    )
    centred = combined - jnp.mean(combined, axis=-1, keepdims=True)
    normal = centred * lax.rsqrt(jnp.mean(centred * centred, axis=-1, keepdims=True) + EPS)
    hidden = jax.nn.gelu(mm(normal.astype(BF16), w_up_ref[...])).astype(BF16)
    out_ref[...] = (normal + mm(hidden, w_down_ref[...])).astype(BF16)


def finish(own, parts, w_up, w_down):
    return pl.pallas_call(
        finish_kernel,
        out_shape=jax.ShapeDtypeStruct(own.shape, BF16),
        in_specs=[VMEM_SPEC] * 6,
        out_specs=VMEM_SPEC,
        name="finish",
        compiler_params=pltpu.CompilerParams(vmem_limit_bytes=12 << 20),
    )(own, *near_core(*parts, w_up, w_down))


def neighbour_kernel(place_ref, links_ref, *refs):
    mine, other = refs[:SIDE], refs[SIDE : 2 * SIDE]
    own_ref, one_ref, two_ref, three_ref, piece_ref, sums_ref = refs[2 * SIDE :]
    my_row, y, z, core = place_ref[0], place_ref[1], place_ref[2], place_ref[3]
    rows = mine[0].shape[0] // SIDE
    for e in range(SIDE):
        for d in range(SIDE):
            for ref, who in ((mine[e], core), (other[e], 1 - core)):
                dy = d + who * (e - d)
                dz = e + who * (d - e)
                device = ((y + SIDE - dy) % SIDE * SIDE + (z + SIDE - dz) % SIDE) * CORES + who
                target = pl.multiple_of(device * rows, rows)
                piece_ref[pl.ds(target, rows), :] = ref[d * rows : (d + 1) * rows, :]
    sums_ref[...] = mm(links_ref[...], piece_ref[...])
    part = own_ref.shape[0]

    def block(distance):
        start = pl.multiple_of((my_row + distance) % SIDE * part, part)
        return sums_ref[pl.ds(start, part), :]

    own_ref[...] = block(0)
    one_ref[...] = block(1).astype(BF16)
    two_ref[...] = block(2).astype(BF16)
    three_ref[...] = block(3).astype(BF16)


def neighbour_sums(place, links, mine, other):
    row_block, width = links.shape[0], mine[0].shape[1]
    part = row_block // SIDE
    sent = jax.ShapeDtypeStruct((part, width), BF16)
    return pl.pallas_call(
        neighbour_kernel,
        out_shape=(jax.ShapeDtypeStruct((part, width), F32), sent, sent, sent),
        in_specs=[SMEM_SPEC] + [VMEM_SPEC] * (1 + 2 * SIDE),
        out_specs=(VMEM_SPEC,) * 4,
        scratch_shapes=[
            pltpu.VMEM((links.shape[1], width), BF16),
            pltpu.VMEM((row_block, width), F32),
        ],
        name="neighbours",
        compiler_params=pltpu.CompilerParams(vmem_limit_bytes=16 << 20),
    )(place, *near_core(links, *mine, *other))


def shifted(value, first, second, swap=0):
    pairs = []
    for y in range(SIDE):
        for z in range(SIDE):
            for c in range(CORES):
                dy, dz = (first, second) if c == 0 else (second, first)
                to = ((y + dy) % SIDE * SIDE + (z + dz) % SIDE) * CORES + (c + swap) % CORES
                pairs.append(((y * SIDE + z) * CORES + c, to))
    return lax.ppermute(value, "col", pairs)


def gather_blocks(update):
    near = [update] + [shifted(update, d, 0) for d in range(1, SIDE)]
    near = jnp.concatenate(near, axis=0)
    far = [near] + [shifted(near, 0, d) for d in range(1, SIDE)]
    return far, [shifted(block, 0, 0, swap=1) for block in far]


def assemble_kernel(place_ref, *refs):
    blocks, out_hbm, store_sem = refs[:-2], refs[-2], refs[-1]
    part = blocks[0].shape[0]
    stores = []
    for d, block_ref in enumerate(blocks):
        start = pl.multiple_of((place_ref[0] + len(blocks) - d) % len(blocks) * part, part)
        store = pltpu.make_async_copy(block_ref, out_hbm.at[pl.ds(start, part), :], store_sem.at[d])
        store.start()
        stores.append(store)
    for store in stores:
        store.wait()


def assemble(place, done, moved):
    rows, width = done.shape
    return pl.pallas_call(
        assemble_kernel,
        out_shape=jax.ShapeDtypeStruct((rows * (1 + len(moved)), width), BF16),
        in_specs=[SMEM_SPEC] + [VMEM_SPEC] * (1 + len(moved)),
        out_specs=HBM_SPEC,
        scratch_shapes=[pltpu.SemaphoreType.DMA((1 + len(moved),))],
        name="assemble",
        compiler_params=pltpu.CompilerParams(vmem_limit_bytes=8 << 20),
    )(place, *near_core(done, *moved))


def ring(size, distance):
    return [(i, (i + distance) % size) for i in range(size)]


def per_device(
    node_states,
    walk_nodes,
    walk_lengths,
    adjacency,
    w_xz,
    w_bc,
    w_dt,
    decay_rate,
    w_out,
    w_up,
    w_down,
):
    node_count, width = node_states.shape
    walk_count, walk_len = walk_nodes.shape
    everyone = ("row", "col")
    owners = lax.axis_size(everyone)
    row_size = lax.axis_size("row")
    row_block = adjacency.shape[0]

    my_row = lax.axis_index("row")
    my_col = lax.axis_index("col")
    place = jnp.stack([my_row, my_col // (SIDE * CORES), my_col // CORES % SIDE, my_col % CORES]).astype(I32)
    wanted, slots = route(walk_nodes, walk_lengths, node_count, owners)
    requests = lax.all_to_all(wanted, everyone, split_axis=0, concat_axis=0, tiled=True)
    requests, near_states, place = lax.optimization_barrier((requests, fetch(node_states)[0], place))
    picked, reqrow = pick(requests, near_states)
    arrived = lax.all_to_all(
        picked.reshape(owners, CAP, width), everyone, split_axis=0, concat_axis=0, tiled=True
    )
    links = make_links(place, adjacency)
    put = placement(slots, owners * CAP)
    arrived, links, put = lax.optimization_barrier((arrived, links, put))
    outgoing = encode(
        arrived.reshape(owners * CAP, width),
        slots,
        put,
        w_xz,
        w_bc,
        w_dt,
        decay_rate,
        w_out,
        walk_len,
    )
    returned = lax.all_to_all(
        outgoing.reshape(owners, CAP, width), everyone, split_axis=0, concat_axis=0, tiled=True
    )
    update = update_nodes(returned.reshape(owners * CAP, width), reqrow, near_states)

    mine, other = gather_blocks(update)
    own, *sent = neighbour_sums(place, links, mine, other)
    parts = [lax.ppermute(block, "row", ring(row_size, d)) for d, block in enumerate(sent, 1)]
    own, w_up, w_down = lax.optimization_barrier((own, w_up, w_down))
    done = finish(own, parts, *fetch(w_up, w_down))
    moved = [lax.ppermute(done, "row", ring(row_size, d)) for d in range(1, row_size)]
    return assemble(place, done, moved)


def solution(mesh):
    return jax.shard_map(
        per_device,
        mesh=mesh,
        in_specs=(
            P(("row", "col"), None),
            P(("row", "col"), None),
            P(("row", "col")),
            P("col", "row"),
            P(),
            P(),
            P(),
            P(),
            P(),
            P(),
            P(),
        ),
        out_specs=P("col", None),
        check_vma=False,
    )
```

```python
import functools

import jax
import jax.numpy as jnp
from jax import lax
from jax.experimental import pallas as pl
from jax.experimental.pallas import tpu as pltpu
from jax.sharding import PartitionSpec as P

F32 = jnp.float32
BF16 = jnp.bfloat16
I32 = jnp.int32
VMEM_SPEC = pl.BlockSpec(memory_space=pltpu.VMEM)
HBM_SPEC = pl.BlockSpec(memory_space=pltpu.HBM)
SMEM_SPEC = pl.BlockSpec(memory_space=pltpu.SMEM)
CAP = 8
EPS = 1e-05
LOG2E = 1.4426950408889634
SIDE = 4
CORES = 2


def iota(shape, dim):
    return lax.broadcasted_iota(I32, shape, dim)


def mm(a, b):
    return jnp.dot(a, b, preferred_element_type=F32)


def mm_nt(a, b):
    return lax.dot_general(a, b, (((1,), (1,)), ((), ())), preferred_element_type=F32)


def near_core(*arrays):
    return [pltpu.with_memory_space_constraint(a, pltpu.VMEM) for a in arrays]


def in_hbm(*arrays):
    return [pltpu.with_memory_space_constraint(a, pltpu.HBM) for a in arrays]


def onehot(cond):
    return cond.astype(F32).astype(BF16)


def as_column(row):
    return jnp.transpose(jnp.broadcast_to(row, (8, row.shape[1])))[:, 0:1]


def route_kernel(
    nodes_hbm, lengths_hbm, wanted_ref, slots_ref, nodes_ref, lengths_ref, load_sem, *, node_count, owners
):
    load_nodes = pltpu.make_async_copy(nodes_hbm, nodes_ref, load_sem.at[0])
    load_lengths = pltpu.make_async_copy(lengths_hbm, lengths_ref, load_sem.at[1])
    load_nodes.start()
    load_lengths.start()
    load_nodes.wait()
    load_lengths.wait()
    walk_count, walk_len = nodes_ref.shape
    tok = walk_count * walk_len
    place = iota((1, walk_len), 1)
    pieces = []
    for w in range(walk_count):
        live = place < lengths_ref[w]
        pieces.append(jnp.where(live, nodes_ref[w : w + 1, :], -1))
    node_row = jnp.concatenate(pieces, axis=1)
    live_row = node_row >= 0
    owner_row = ((node_row.astype(F32) + 0.5) * (1.0 / node_count)).astype(I32)
    local_row = node_row - owner_row * node_count
    owner_row = jnp.where(live_row, owner_row, -1)
    local_row = jnp.where(live_row, local_row + 1, 0)
    owner_col = as_column(owner_row)
    local_col = as_column(local_row)
    same = owner_col == owner_row
    first_i = iota((tok, tok), 0)
    second_i = iota((tok, tok), 1)
    rank_row = jnp.sum(jnp.where(same & (first_i < second_i), 1.0, 0.0), axis=0, keepdims=True)
    rank_row = rank_row.astype(I32)
    rank_col = as_column(rank_row)
    slot_row = jnp.where(live_row, owner_row * CAP + rank_row, -1)
    slots_ref[...] = jnp.broadcast_to(slot_row, slots_ref.shape)
    by_owner = onehot(iota((owners, tok), 0) == owner_row)
    by_rank = jnp.where(iota((tok, 128), 1) == rank_col, local_col.astype(F32), 0.0).astype(BF16)
    wanted = mm(by_owner, by_rank).astype(I32) - 1
    wanted_ref[...] = wanted[:, :CAP]


def route(walk_nodes, walk_lengths, node_count, owners):
    tok = walk_nodes.shape[0] * walk_nodes.shape[1]
    return pl.pallas_call(
        functools.partial(route_kernel, node_count=node_count, owners=owners),
        out_shape=(
            jax.ShapeDtypeStruct((owners, CAP), I32),
            jax.ShapeDtypeStruct((8, tok), I32),
        ),
        in_specs=[HBM_SPEC, HBM_SPEC],
        out_specs=(VMEM_SPEC, VMEM_SPEC),
        scratch_shapes=[
            pltpu.VMEM(walk_nodes.shape, I32),
            pltpu.SMEM(walk_lengths.shape, I32),
            pltpu.SemaphoreType.DMA((2,)),
        ],
        name="route",
        compiler_params=pltpu.CompilerParams(vmem_limit_bytes=12 << 20),
    )(*in_hbm(walk_nodes, walk_lengths))


def pick_kernel(requests_ref, states_ref, picked_ref, reqrow_ref):
    owners = requests_ref.shape[0]
    node_count = states_ref.shape[0]
    total = owners * CAP
    spread = onehot(iota((total, owners), 0) // CAP == iota((total, owners), 1))
    wide = mm(spread, requests_ref[...].astype(F32).astype(BF16))
    mine = iota((total, CAP), 1) == iota((total, CAP), 0) % CAP
    col = jnp.sum(jnp.where(mine, wide, 0.0), axis=1, keepdims=True).astype(I32)
    chosen = onehot(iota((total, node_count), 1) == col)
    reqrow_ref[...] = jnp.transpose(jnp.broadcast_to(col, (total, 8)))
    picked_ref[...] = mm(chosen, states_ref[...]).astype(BF16)


def pick(requests, node_states):
    total = requests.shape[0] * CAP
    return pl.pallas_call(
        pick_kernel,
        out_shape=(
            jax.ShapeDtypeStruct((total, node_states.shape[1]), BF16),
            jax.ShapeDtypeStruct((8, total), I32),
        ),
        in_specs=[VMEM_SPEC, VMEM_SPEC],
        out_specs=(VMEM_SPEC, VMEM_SPEC),
        name="pick",
        compiler_params=pltpu.CompilerParams(vmem_limit_bytes=12 << 20),
    )(*near_core(requests, node_states))


def placement_kernel(slots_ref, put_ref):
    put_ref[...] = onehot(iota(put_ref.shape, 0) == slots_ref[0:1, :])


def placement(slots, total):
    return pl.pallas_call(
        placement_kernel,
        out_shape=jax.ShapeDtypeStruct((total, slots.shape[1]), BF16),
        in_specs=[VMEM_SPEC],
        out_specs=VMEM_SPEC,
        name="placement",
        compiler_params=pltpu.CompilerParams(vmem_limit_bytes=12 << 20),
    )(*near_core(slots))


def fetch_kernel(*refs):
    count = len(refs) // 2
    loads = [
        pltpu.make_async_copy(refs[n], refs[count + n], refs[-1].at[n]) for n in range(count)
    ]
    for load in loads:
        load.start()
    for load in loads:
        load.wait()


def fetch(*arrays):
    return pl.pallas_call(
        fetch_kernel,
        out_shape=tuple(jax.ShapeDtypeStruct(array.shape, array.dtype) for array in arrays),
        in_specs=[HBM_SPEC] * len(arrays),
        out_specs=(VMEM_SPEC,) * len(arrays),
        scratch_shapes=[pltpu.SemaphoreType.DMA((len(arrays),))],
        name="fetch",
        compiler_params=pltpu.CompilerParams(vmem_limit_bytes=8 << 20),
    )(*in_hbm(*arrays))


PAD = 8


def encode_kernel(
    arrived_ref,
    slots_ref,
    put_hbm,
    w_dt_hbm,
    rate_hbm,
    w_xz_hbm,
    w_bc_hbm,
    w_out_hbm,
    out_ref,
    put_ref,
    w_dt_ref,
    rate_ref,
    w_xz_ref,
    w_bc_ref,
    w_out_ref,
    small_sem,
    weights_sem,
    stream_ref,
    inner_left_ref,
    inner_right_ref,
    gate_ref,
    scores_ref,
    gated_ref,
    cum_ref,
    rows_ref,
    *,
    walk_len,
):
    layers, inner_width, width = w_out_ref.shape
    heads = w_dt_ref.shape[1]
    head_width = inner_width // heads
    state_width = w_bc_ref.shape[2] // 2
    tok = slots_ref.shape[1]
    quads = inner_width // 256
    walks = tok // walk_len
    stride = walk_len + PAD

    load_dt = pltpu.make_async_copy(w_dt_hbm, w_dt_ref, small_sem.at[0])
    load_rate = pltpu.make_async_copy(rate_hbm, rate_ref, small_sem.at[1])
    load_dt.start()
    load_rate.start()
    first_loads = []
    for q in range(2 * quads):
        cols = pl.ds((q // 2 + q % 2 * quads) * 256, 256)
        load = pltpu.make_async_copy(
            w_xz_hbm.at[0, :, cols], w_xz_ref.at[0, :, cols], small_sem.at[3 + q]
        )
        load.start()
        first_loads.append(load)
    loads = []
    for layer in range(layers):
        for q, (source, target) in enumerate(
            ((w_xz_hbm, w_xz_ref), (w_bc_hbm, w_bc_ref), (w_out_hbm, w_out_ref))
        ):
            if layer == 0 and q == 0:
                loads.append(None)
                continue
            load = pltpu.make_async_copy(source.at[layer], target.at[layer], weights_sem.at[layer, q])
            load.start()
            loads.append(load)
    load_put = pltpu.make_async_copy(put_hbm, put_ref, small_sem.at[2])
    load_put.start()

    total = arrived_ref.shape[0]
    take = onehot(iota((tok, total), 1) == as_column(slots_ref[0:1, :]))
    stream_ref[...] = mm(take, arrived_ref[...])
    for w in range(walks):
        cum_ref[:, w * stride : w * stride + PAD, :] = jnp.zeros((2 * quads, PAD, 128), F32)
    load_dt.wait()
    load_rate.wait()

    live_row = slots_ref[0:1, :] >= 0
    spread_in = iota((3 * heads, inner_width), 0)
    spread_out = iota((3 * heads, inner_width), 1)
    spread = onehot(spread_in % heads == spread_out // head_width)
    sum_in = iota((128, 256), 0)
    sum_out = iota((128, 256), 1)
    same_walk = sum_in // walk_len == sum_out % 128 // walk_len
    reach = sum_out % walk_len - jnp.where(sum_out >= 128, 1, 0)
    running = onehot(same_walk & (sum_in % walk_len <= reach))
    lane = iota((walk_len, 128), 1)
    left_row = iota((1, 128), 1) < walk_len
    t_of = iota((walk_len, 128), 0)
    s_of = lane % walk_len
    earlier = s_of < t_of
    weight = jnp.where(s_of == t_of, 2.0, 1.0) * state_width ** (-0.5)
    left_cols = iota((1, 256), 1) % 128 < walk_len
    nothing = jnp.zeros((walk_len, 128), BF16)

    def split3(v):
        high = v.astype(BF16).astype(F32)
        rest = v - high
        middle = rest.astype(BF16).astype(F32)
        return jnp.concatenate([high, middle, rest - middle], axis=0)

    def walk_rows(walk):
        return pl.ds(walk * walk_len, walk_len)

    def half_step(j, odd):
        lanes = pl.ds(j * 128, 128)
        walk = 2 * j + odd
        scores = scores_ref[walk_rows(walk), :]
        here = pl.ds(walk * stride + PAD, walk_len)
        above = pl.ds(walk * stride + PAD - 1, walk_len)
        for quad in range(quads):
            mixes = []
            for p in (2 * quad, 2 * quad + 1):

                def row_of(q):
                    a = rows_ref[2 * q + odd, 2 * p : 2 * p + 1, lanes]
                    b = rows_ref[2 * q + 1 - odd, 2 * p + 1 : 2 * p + 2, lanes]
                    return jnp.where(left_row, a, b)

                gap = jnp.where(earlier, cum_ref[p, here, :] - row_of(0), row_of(1) - cum_ref[p, above, :])
                mix = scores * jnp.exp2(gap) * row_of(2)
                mixes.append(mix.astype(BF16))
            apply_mix(quad, walk_rows(walk), jnp.concatenate(mixes, axis=1))

    def apply_mix(quad, rows, mix):
        tops, bottoms = [], []
        for p in (2 * quad, 2 * quad + 1):
            tops.append(inner_left_ref[rows, 128 * p : 128 * (p + 1)])
            bottoms.append(inner_right_ref[rows, 128 * p : 128 * (p + 1)])
        blocks = jnp.concatenate(
            [
                jnp.concatenate([tops[0], nothing], axis=1),
                jnp.concatenate([bottoms[0], nothing], axis=1),
                jnp.concatenate([nothing, tops[1]], axis=1),
                jnp.concatenate([nothing, bottoms[1]], axis=1),
            ],
            axis=0,
        )
        cols = slice(256 * quad, 256 * (quad + 1))
        mixed = mm(mix, blocks)
        gated_ref[rows, cols] = (mixed * gate_ref[rows, cols]).astype(BF16)

    def walk_pair(j, carry):
        half_step(j, 0)
        half_step(j, 1)
        return carry

    for layer in range(layers):
        x = stream_ref[...]
        normed = (x * lax.rsqrt(jnp.mean(x * x, axis=-1, keepdims=True) + EPS)).astype(BF16)

        def project(q):
            cols = slice(256 * q, 256 * (q + 1))
            if layer == 0 and q < 2:
                for load in first_loads[2 * q : 2 if q == 0 else None]:
                    load.wait()
            inner = mm(normed, w_xz_ref[layer, :, cols])
            inner_left_ref[:, cols] = jnp.where(left_cols, inner, 0.0).astype(BF16)
            inner_right_ref[:, cols] = jnp.where(left_cols, 0.0, inner).astype(BF16)
            gate_cols = slice(inner_width + 256 * q, inner_width + 256 * (q + 1))
            half_gate = 0.5 * mm(normed, w_xz_ref[layer, :, gate_cols])
            gate_ref[:, cols] = half_gate + half_gate * jnp.tanh(half_gate)

        raw = mm_nt(w_dt_ref[layer], normed)
        if layer > 0:
            loads[3 * layer].wait()
        project(0)
        step = jnp.maximum(raw, 0.0) + jnp.log1p(jnp.exp(-jnp.abs(raw)))
        rate = as_column(rate_ref[layer : layer + 1, :])
        pieces = split3((-LOG2E * rate) * step).astype(BF16)
        source = jnp.where(live_row, step, 0.0)
        project(1)
        cums = []
        for j in range(walks // 2):
            lanes = slice(128 * j, 128 * (j + 1))
            sums = mm(pieces[:, lanes], running)
            sums = sums[:heads] + (sums[heads : 2 * heads] + sums[2 * heads :])
            cums.append(sums[:, :128])
            for q, v in enumerate((sums[:, :128], sums[:, 128:], source[:, lanes])):
                rows_ref[2 * q, :, lanes] = v
                rows_ref[2 * q + 1, :, lanes] = pltpu.roll(v, walk_len, 1)
        project(2)
        columns = jnp.transpose(split3(jnp.concatenate(cums, axis=1))).astype(BF16)
        project(3)
        loads[3 * layer + 1].wait()
        proj = mm(normed, w_bc_ref[layer]).astype(BF16)
        for w in range(walks):
            b_in = proj[w * walk_len : (w + 1) * walk_len, :state_width]
            c_out = proj[w * walk_len : (w + 1) * walk_len, state_width:]
            scores = mm_nt(c_out, jnp.concatenate([b_in, b_in], axis=0))
            scores_ref[w * walk_len : (w + 1) * walk_len, :] = scores * weight
        for quad in range(quads):
            wide = mm(columns, spread[:, 256 * quad : 256 * (quad + 1)])
            for w in range(walks):
                block = wide[w * walk_len : (w + 1) * walk_len, :]
                rows = slice(w * stride + PAD, (w + 1) * stride)
                cum_ref[2 * quad, rows, :] = block[:, :128]
                cum_ref[2 * quad + 1, rows, :] = block[:, 128:]

        for j in range(walks // 2):
            walk_pair(j, 0)
        loads[3 * layer + 2].wait()
        stream = x + mm(gated_ref[...], w_out_ref[layer])
        stream_ref[...] = stream.astype(BF16).astype(F32)

    load_put.wait()
    out_ref[...] = mm(put_ref[...], stream_ref[...].astype(BF16)).astype(BF16)


def encode(arrived, slots, put, w_xz, w_bc, w_dt, decay_rate, w_out, walk_len):
    total, width = arrived.shape
    tok = slots.shape[1]
    inner_width = w_out.shape[1]
    w_dt = jnp.swapaxes(w_dt, 1, 2)
    return pl.pallas_call(
        functools.partial(encode_kernel, walk_len=walk_len),
        out_shape=jax.ShapeDtypeStruct((total, width), BF16),
        in_specs=[VMEM_SPEC] * 2 + [HBM_SPEC] * 6,
        out_specs=VMEM_SPEC,
        scratch_shapes=[
            pltpu.VMEM(put.shape, BF16),
            pltpu.VMEM(w_dt.shape, BF16),
            pltpu.VMEM(decay_rate.shape, F32),
            pltpu.VMEM(w_xz.shape, BF16),
            pltpu.VMEM(w_bc.shape, BF16),
            pltpu.VMEM(w_out.shape, BF16),
            pltpu.SemaphoreType.DMA((3 + inner_width // 128,)),
            pltpu.SemaphoreType.DMA((w_out.shape[0], 3)),
            pltpu.VMEM((tok, width), F32),
            pltpu.VMEM((tok, inner_width), BF16),
            pltpu.VMEM((tok, inner_width), BF16),
            pltpu.VMEM((tok, inner_width), F32),
            pltpu.VMEM((tok, 128), F32),
            pltpu.VMEM((tok, inner_width), BF16),
            pltpu.VMEM((inner_width // 128, tok // walk_len * (walk_len + PAD), 128), F32),
            pltpu.VMEM((6, w_dt.shape[1], tok), F32),
        ],
        name="encode",
        compiler_params=pltpu.CompilerParams(
            vmem_limit_bytes=36 << 20
        ),
    )(*near_core(arrived, slots), *in_hbm(put, w_dt, decay_rate, w_xz, w_bc, w_out))


def links_kernel(place_ref, adjacency_hbm, links_ref, block_ref, load_sem):
    rows, cols = links_ref.shape
    chunks = load_sem.shape[0]
    size = rows // chunks
    loads = []
    for n in range(chunks):
        part = pl.ds(n * size, size)
        load = pltpu.make_async_copy(adjacency_hbm.at[part, :], block_ref.at[part, :], load_sem.at[n])
        load.start()
        loads.append(load)
    my_row, y, z, core = place_ref[0], place_ref[1], place_ref[2], place_ref[3]
    first_row = ((y * SIDE + z) * CORES + core) * rows
    offset = first_row - my_row * cols
    for n in range(chunks):
        loads[n].wait()
        diagonal = iota((size, cols), 1) - iota((size, cols), 0) == offset + n * size
        block = block_ref[n * size : (n + 1) * size, :] + diagonal.astype(I32)
        links_ref[n * size : (n + 1) * size, :] = block.astype(F32).astype(BF16)


def make_links(place, adjacency):
    chunks = 6
    return pl.pallas_call(
        links_kernel,
        out_shape=jax.ShapeDtypeStruct(adjacency.shape, BF16),
        in_specs=[SMEM_SPEC, HBM_SPEC],
        out_specs=VMEM_SPEC,
        scratch_shapes=[pltpu.VMEM(adjacency.shape, I32), pltpu.SemaphoreType.DMA((chunks,))],
        name="links",
        compiler_params=pltpu.CompilerParams(vmem_limit_bytes=16 << 20),
    )(place, *in_hbm(adjacency))


def update_kernel(returned_ref, reqrow_ref, states_ref, out_ref):
    node_count = states_ref.shape[0]
    total = returned_ref.shape[0]
    member = jnp.where(iota((node_count, total), 0) == reqrow_ref[0:1, :], 1.0, 0.0)
    visits = jnp.sum(member, axis=1, keepdims=True)
    summed = mm(member.astype(BF16), returned_ref[...])
    out_ref[...] = (states_ref[...].astype(F32) + summed / (1.0 + visits)).astype(BF16)


def update_nodes(returned, reqrow, node_states):
    return pl.pallas_call(
        update_kernel,
        out_shape=jax.ShapeDtypeStruct(node_states.shape, BF16),
        in_specs=[VMEM_SPEC] * 3,
        out_specs=VMEM_SPEC,
        name="update",
        compiler_params=pltpu.CompilerParams(vmem_limit_bytes=12 << 20),
    )(*near_core(returned, reqrow, node_states))


def finish_kernel(own_ref, one_ref, two_ref, three_ref, w_up_ref, w_down_ref, out_ref):
    combined = (own_ref[...] + one_ref[...].astype(F32)) + (
        two_ref[...].astype(F32) + three_ref[...].astype(F32)
    )
    centred = combined - jnp.mean(combined, axis=-1, keepdims=True)
    normal = centred * lax.rsqrt(jnp.mean(centred * centred, axis=-1, keepdims=True) + EPS)
    hidden = jax.nn.gelu(mm(normal.astype(BF16), w_up_ref[...])).astype(BF16)
    out_ref[...] = (normal + mm(hidden, w_down_ref[...])).astype(BF16)


def finish(own, parts, w_up, w_down):
    return pl.pallas_call(
        finish_kernel,
        out_shape=jax.ShapeDtypeStruct(own.shape, BF16),
        in_specs=[VMEM_SPEC] * 6,
        out_specs=VMEM_SPEC,
        name="finish",
        compiler_params=pltpu.CompilerParams(vmem_limit_bytes=12 << 20),
    )(own, *near_core(*parts, w_up, w_down))


def neighbour_kernel(place_ref, links_ref, *refs):
    mine, other = refs[:SIDE], refs[SIDE : 2 * SIDE]
    own_ref, one_ref, two_ref, three_ref, piece_ref, sums_ref = refs[2 * SIDE :]
    my_row, y, z, core = place_ref[0], place_ref[1], place_ref[2], place_ref[3]
    rows = mine[0].shape[0] // SIDE
    for e in range(SIDE):
        for d in range(SIDE):
            for ref, who in ((mine[e], core), (other[e], 1 - core)):
                dy = d + who * (e - d)
                dz = e + who * (d - e)
                device = ((y + SIDE - dy) % SIDE * SIDE + (z + SIDE - dz) % SIDE) * CORES + who
                target = pl.multiple_of(device * rows, rows)
                piece_ref[pl.ds(target, rows), :] = ref[d * rows : (d + 1) * rows, :]
    sums_ref[...] = mm(links_ref[...], piece_ref[...])
    part = own_ref.shape[0]

    def block(distance):
        start = pl.multiple_of((my_row + distance) % SIDE * part, part)
        return sums_ref[pl.ds(start, part), :]

    own_ref[...] = block(0)
    one_ref[...] = block(1).astype(BF16)
    two_ref[...] = block(2).astype(BF16)
    three_ref[...] = block(3).astype(BF16)


def neighbour_sums(place, links, mine, other):
    row_block, width = links.shape[0], mine[0].shape[1]
    part = row_block // SIDE
    sent = jax.ShapeDtypeStruct((part, width), BF16)
    return pl.pallas_call(
        neighbour_kernel,
        out_shape=(jax.ShapeDtypeStruct((part, width), F32), sent, sent, sent),
        in_specs=[SMEM_SPEC] + [VMEM_SPEC] * (1 + 2 * SIDE),
        out_specs=(VMEM_SPEC,) * 4,
        scratch_shapes=[
            pltpu.VMEM((links.shape[1], width), BF16),
            pltpu.VMEM((row_block, width), F32),
        ],
        name="neighbours",
        compiler_params=pltpu.CompilerParams(vmem_limit_bytes=16 << 20),
    )(place, *near_core(links, *mine, *other))


def shifted(value, first, second, swap=0):
    pairs = []
    for y in range(SIDE):
        for z in range(SIDE):
            for c in range(CORES):
                dy, dz = (first, second) if c == 0 else (second, first)
                to = ((y + dy) % SIDE * SIDE + (z + dz) % SIDE) * CORES + (c + swap) % CORES
                pairs.append(((y * SIDE + z) * CORES + c, to))
    return lax.ppermute(value, "col", pairs)


def gather_blocks(update):
    near = [update] + [shifted(update, d, 0) for d in range(1, SIDE)]
    near = jnp.concatenate(near, axis=0)
    far = [near] + [shifted(near, 0, d) for d in range(1, SIDE)]
    return far, [shifted(block, 0, 0, swap=1) for block in far]


def assemble_kernel(place_ref, *refs):
    blocks, out_hbm, store_sem = refs[:-2], refs[-2], refs[-1]
    part = blocks[0].shape[0]
    stores = []
    for d, block_ref in enumerate(blocks):
        start = pl.multiple_of((place_ref[0] + len(blocks) - d) % len(blocks) * part, part)
        store = pltpu.make_async_copy(block_ref, out_hbm.at[pl.ds(start, part), :], store_sem.at[d])
        store.start()
        stores.append(store)
    for store in stores:
        store.wait()


def assemble(place, done, moved):
    rows, width = done.shape
    return pl.pallas_call(
        assemble_kernel,
        out_shape=jax.ShapeDtypeStruct((rows * (1 + len(moved)), width), BF16),
        in_specs=[SMEM_SPEC] + [VMEM_SPEC] * (1 + len(moved)),
        out_specs=HBM_SPEC,
        scratch_shapes=[pltpu.SemaphoreType.DMA((1 + len(moved),))],
        name="assemble",
        compiler_params=pltpu.CompilerParams(vmem_limit_bytes=8 << 20),
    )(place, *near_core(done, *moved))


def ring(size, distance):
    return [(i, (i + distance) % size) for i in range(size)]


def per_device(
    node_states,
    walk_nodes,
    walk_lengths,
    adjacency,
    w_xz,
    w_bc,
    w_dt,
    decay_rate,
    w_out,
    w_up,
    w_down,
):
    node_count, width = node_states.shape
    walk_count, walk_len = walk_nodes.shape
    everyone = ("row", "col")
    owners = lax.axis_size(everyone)
    row_size = lax.axis_size("row")
    row_block = adjacency.shape[0]

    my_row = lax.axis_index("row")
    my_col = lax.axis_index("col")
    place = jnp.stack([my_row, my_col // (SIDE * CORES), my_col // CORES % SIDE, my_col % CORES]).astype(I32)
    wanted, slots = route(walk_nodes, walk_lengths, node_count, owners)
    requests = lax.all_to_all(wanted, everyone, split_axis=0, concat_axis=0, tiled=True)
    requests, near_states, place = lax.optimization_barrier((requests, fetch(node_states)[0], place))
    picked, reqrow = pick(requests, near_states)
    arrived = lax.all_to_all(
        picked.reshape(owners, CAP, width), everyone, split_axis=0, concat_axis=0, tiled=True
    )
    links = make_links(place, adjacency)
    put = placement(slots, owners * CAP)
    arrived, links, put = lax.optimization_barrier((arrived, links, put))
    outgoing = encode(
        arrived.reshape(owners * CAP, width),
        slots,
        put,
        w_xz,
        w_bc,
        w_dt,
        decay_rate,
        w_out,
        walk_len,
    )
    returned = lax.all_to_all(
        outgoing.reshape(owners, CAP, width), everyone, split_axis=0, concat_axis=0, tiled=True
    )
    update = update_nodes(returned.reshape(owners * CAP, width), reqrow, near_states)

    mine, other = gather_blocks(update)
    own, *sent = neighbour_sums(place, links, mine, other)
    parts = [lax.ppermute(block, "row", ring(row_size, d)) for d, block in enumerate(sent, 1)]
    own, w_up, w_down = lax.optimization_barrier((own, w_up, w_down))
    done = finish(own, parts, *fetch(w_up, w_down))
    moved = [lax.ppermute(done, "row", ring(row_size, d)) for d in range(1, row_size)]
    return assemble(place, done, moved)


def solution(mesh):
    return jax.shard_map(
        per_device,
        mesh=mesh,
        in_specs=(
            P(("row", "col"), None),
            P(("row", "col"), None),
            P(("row", "col")),
            P("col", "row"),
            P(),
            P(),
            P(),
            P(),
            P(),
            P(),
            P(),
        ),
        out_specs=P("col", None),
        check_vma=False,
    )
```

```python
import functools

import jax
import jax.numpy as jnp
from jax import lax
from jax.experimental import pallas as pl
from jax.experimental.pallas import tpu as pltpu
from jax.sharding import PartitionSpec as P

F32 = jnp.float32
BF16 = jnp.bfloat16
I32 = jnp.int32
VMEM_SPEC = pl.BlockSpec(memory_space=pltpu.VMEM)
HBM_SPEC = pl.BlockSpec(memory_space=pltpu.HBM)
SMEM_SPEC = pl.BlockSpec(memory_space=pltpu.SMEM)
CAP = 8
EPS = 1e-05
LOG2E = 1.4426950408889634
SIDE = 4
CORES = 2


def iota(shape, dim):
    return lax.broadcasted_iota(I32, shape, dim)


def mm(a, b):
    return jnp.dot(a, b, preferred_element_type=F32)


def mm_nt(a, b):
    return lax.dot_general(a, b, (((1,), (1,)), ((), ())), preferred_element_type=F32)


def near_core(*arrays):
    return [pltpu.with_memory_space_constraint(a, pltpu.VMEM) for a in arrays]


def in_hbm(*arrays):
    return [pltpu.with_memory_space_constraint(a, pltpu.HBM) for a in arrays]


def onehot(cond):
    return cond.astype(F32).astype(BF16)


def as_column(row):
    return jnp.transpose(jnp.broadcast_to(row, (8, row.shape[1])))[:, 0:1]


def route_kernel(
    nodes_hbm, lengths_hbm, wanted_ref, slots_ref, nodes_ref, lengths_ref, load_sem, *, node_count, owners
):
    load_nodes = pltpu.make_async_copy(nodes_hbm, nodes_ref, load_sem.at[0])
    load_lengths = pltpu.make_async_copy(lengths_hbm, lengths_ref, load_sem.at[1])
    load_nodes.start()
    load_lengths.start()
    load_nodes.wait()
    load_lengths.wait()
    walk_count, walk_len = nodes_ref.shape
    tok = walk_count * walk_len
    place = iota((1, walk_len), 1)
    pieces = []
    for w in range(walk_count):
        live = place < lengths_ref[w]
        pieces.append(jnp.where(live, nodes_ref[w : w + 1, :], -1))
    node_row = jnp.concatenate(pieces, axis=1)
    live_row = node_row >= 0
    owner_row = ((node_row.astype(F32) + 0.5) * (1.0 / node_count)).astype(I32)
    local_row = node_row - owner_row * node_count
    owner_row = jnp.where(live_row, owner_row, -1)
    local_row = jnp.where(live_row, local_row + 1, 0)
    owner_col = as_column(owner_row)
    local_col = as_column(local_row)
    same = owner_col == owner_row
    first_i = iota((tok, tok), 0)
    second_i = iota((tok, tok), 1)
    rank_row = jnp.sum(jnp.where(same & (first_i < second_i), 1.0, 0.0), axis=0, keepdims=True)
    rank_row = rank_row.astype(I32)
    rank_col = as_column(rank_row)
    slot_row = jnp.where(live_row, owner_row * CAP + rank_row, -1)
    slots_ref[...] = jnp.broadcast_to(slot_row, slots_ref.shape)
    by_owner = onehot(iota((owners, tok), 0) == owner_row)
    by_rank = jnp.where(iota((tok, 128), 1) == rank_col, local_col.astype(F32), 0.0).astype(BF16)
    wanted = mm(by_owner, by_rank).astype(I32) - 1
    wanted_ref[...] = wanted[:, :CAP]


def route(walk_nodes, walk_lengths, node_count, owners):
    tok = walk_nodes.shape[0] * walk_nodes.shape[1]
    return pl.pallas_call(
        functools.partial(route_kernel, node_count=node_count, owners=owners),
        out_shape=(
            jax.ShapeDtypeStruct((owners, CAP), I32),
            jax.ShapeDtypeStruct((8, tok), I32),
        ),
        in_specs=[HBM_SPEC, HBM_SPEC],
        out_specs=(VMEM_SPEC, VMEM_SPEC),
        scratch_shapes=[
            pltpu.VMEM(walk_nodes.shape, I32),
            pltpu.SMEM(walk_lengths.shape, I32),
            pltpu.SemaphoreType.DMA((2,)),
        ],
        name="route",
        compiler_params=pltpu.CompilerParams(vmem_limit_bytes=12 << 20),
    )(*in_hbm(walk_nodes, walk_lengths))


def pick_kernel(requests_ref, states_ref, picked_hbm, reqrow_ref, picked_ref, store_sem):
    owners = requests_ref.shape[0]
    node_count = states_ref.shape[0]
    total = owners * CAP
    spread = onehot(iota((total, owners), 0) // CAP == iota((total, owners), 1))
    wide = mm(spread, requests_ref[...].astype(F32).astype(BF16))
    mine = iota((total, CAP), 1) == iota((total, CAP), 0) % CAP
    col = jnp.sum(jnp.where(mine, wide, 0.0), axis=1, keepdims=True).astype(I32)
    chunks = store_sem.shape[0]
    size = total // chunks
    stores = []
    for n in range(chunks):
        chosen = onehot(iota((size, node_count), 1) == col[n * size : (n + 1) * size])
        picked_ref[n * size : (n + 1) * size, :] = mm(chosen, states_ref[...]).astype(BF16)
        part = pl.ds(n * size, size)
        store = pltpu.make_async_copy(picked_ref.at[part, :], picked_hbm.at[part, :], store_sem.at[n])
        store.start()
        stores.append(store)
    reqrow_ref[...] = jnp.transpose(jnp.broadcast_to(col, (total, 8)))
    for store in stores:
        store.wait()


def pick(requests, node_states):
    total = requests.shape[0] * CAP
    return pl.pallas_call(
        pick_kernel,
        out_shape=(
            jax.ShapeDtypeStruct((total, node_states.shape[1]), BF16),
            jax.ShapeDtypeStruct((8, total), I32),
        ),
        in_specs=[VMEM_SPEC, VMEM_SPEC],
        out_specs=(HBM_SPEC, VMEM_SPEC),
        scratch_shapes=[
            pltpu.VMEM((total, node_states.shape[1]), BF16),
            pltpu.SemaphoreType.DMA((4,)),
        ],
        name="pick",
        compiler_params=pltpu.CompilerParams(vmem_limit_bytes=12 << 20),
    )(*near_core(requests, node_states))


def placement_kernel(slots_ref, put_ref):
    put_ref[...] = onehot(iota(put_ref.shape, 0) == slots_ref[0:1, :])


def placement(slots, total):
    return pl.pallas_call(
        placement_kernel,
        out_shape=jax.ShapeDtypeStruct((total, slots.shape[1]), BF16),
        in_specs=[VMEM_SPEC],
        out_specs=VMEM_SPEC,
        name="placement",
        compiler_params=pltpu.CompilerParams(vmem_limit_bytes=12 << 20),
    )(*near_core(slots))


def fetch_kernel(*refs):
    count = len(refs) // 2
    loads = [
        pltpu.make_async_copy(refs[n], refs[count + n], refs[-1].at[n]) for n in range(count)
    ]
    for load in loads:
        load.start()
    for load in loads:
        load.wait()


def fetch(*arrays):
    return pl.pallas_call(
        fetch_kernel,
        out_shape=tuple(jax.ShapeDtypeStruct(array.shape, array.dtype) for array in arrays),
        in_specs=[HBM_SPEC] * len(arrays),
        out_specs=(VMEM_SPEC,) * len(arrays),
        scratch_shapes=[pltpu.SemaphoreType.DMA((len(arrays),))],
        name="fetch",
        compiler_params=pltpu.CompilerParams(vmem_limit_bytes=8 << 20),
    )(*in_hbm(*arrays))


PAD = 8


def encode_kernel(
    arrived_ref,
    slots_ref,
    put_hbm,
    w_dt_hbm,
    rate_hbm,
    w_xz_hbm,
    w_bc_hbm,
    w_out_hbm,
    out_ref,
    put_ref,
    w_dt_ref,
    rate_ref,
    w_xz_ref,
    w_bc_ref,
    w_out_ref,
    small_sem,
    weights_sem,
    stream_ref,
    inner_left_ref,
    inner_right_ref,
    gate_ref,
    scores_ref,
    gated_ref,
    cum_ref,
    rows_ref,
    *,
    walk_len,
):
    layers, inner_width, width = w_out_ref.shape
    heads = w_dt_ref.shape[1]
    head_width = inner_width // heads
    state_width = w_bc_ref.shape[2] // 2
    tok = slots_ref.shape[1]
    quads = inner_width // 256
    walks = tok // walk_len
    stride = walk_len + PAD

    load_dt = pltpu.make_async_copy(w_dt_hbm, w_dt_ref, small_sem.at[0])
    load_rate = pltpu.make_async_copy(rate_hbm, rate_ref, small_sem.at[1])
    load_dt.start()
    load_rate.start()
    first_loads = []
    for q in range(2 * quads):
        cols = pl.ds((q // 2 + q % 2 * quads) * 256, 256)
        load = pltpu.make_async_copy(
            w_xz_hbm.at[0, :, cols], w_xz_ref.at[0, :, cols], small_sem.at[3 + q]
        )
        load.start()
        first_loads.append(load)
    loads = []
    for layer in range(layers):
        for q, (source, target) in enumerate(
            ((w_xz_hbm, w_xz_ref), (w_bc_hbm, w_bc_ref), (w_out_hbm, w_out_ref))
        ):
            if layer == 0 and q == 0:
                loads.append(None)
                continue
            load = pltpu.make_async_copy(source.at[layer], target.at[layer], weights_sem.at[layer, q])
            load.start()
            loads.append(load)
    load_put = pltpu.make_async_copy(put_hbm, put_ref, small_sem.at[2])
    load_put.start()

    total = arrived_ref.shape[0]
    take = onehot(iota((tok, total), 1) == as_column(slots_ref[0:1, :]))
    stream_ref[...] = mm(take, arrived_ref[...])
    for w in range(walks):
        cum_ref[:, w * stride : w * stride + PAD, :] = jnp.zeros((2 * quads, PAD, 128), F32)
    load_dt.wait()
    load_rate.wait()

    live_row = slots_ref[0:1, :] >= 0
    spread_in = iota((3 * heads, inner_width), 0)
    spread_out = iota((3 * heads, inner_width), 1)
    spread = onehot(spread_in % heads == spread_out // head_width)
    sum_in = iota((128, 256), 0)
    sum_out = iota((128, 256), 1)
    same_walk = sum_in // walk_len == sum_out % 128 // walk_len
    reach = sum_out % walk_len - jnp.where(sum_out >= 128, 1, 0)
    running = onehot(same_walk & (sum_in % walk_len <= reach))
    lane = iota((walk_len, 128), 1)
    left_row = iota((1, 128), 1) < walk_len
    t_of = iota((walk_len, 128), 0)
    s_of = lane % walk_len
    earlier = s_of < t_of
    weight = jnp.where(s_of == t_of, 2.0, 1.0) * state_width ** (-0.5)
    left_cols = iota((1, 256), 1) % 128 < walk_len
    nothing = jnp.zeros((walk_len, 128), BF16)

    def split3(v):
        high = v.astype(BF16).astype(F32)
        rest = v - high
        middle = rest.astype(BF16).astype(F32)
        return jnp.concatenate([high, middle, rest - middle], axis=0)

    def walk_rows(walk):
        return pl.ds(walk * walk_len, walk_len)

    def half_step(j, odd):
        lanes = pl.ds(j * 128, 128)
        walk = 2 * j + odd
        scores = scores_ref[walk_rows(walk), :]
        here = pl.ds(walk * stride + PAD, walk_len)
        above = pl.ds(walk * stride + PAD - 1, walk_len)
        for quad in range(quads):
            mixes = []
            for p in (2 * quad, 2 * quad + 1):

                def row_of(q):
                    a = rows_ref[2 * q + odd, 2 * p : 2 * p + 1, lanes]
                    b = rows_ref[2 * q + 1 - odd, 2 * p + 1 : 2 * p + 2, lanes]
                    return jnp.where(left_row, a, b)

                gap = jnp.where(earlier, cum_ref[p, here, :] - row_of(0), row_of(1) - cum_ref[p, above, :])
                mix = scores * jnp.exp2(gap) * row_of(2)
                mixes.append(mix.astype(BF16))
            apply_mix(quad, walk_rows(walk), jnp.concatenate(mixes, axis=1))

    def apply_mix(quad, rows, mix):
        tops, bottoms = [], []
        for p in (2 * quad, 2 * quad + 1):
            tops.append(inner_left_ref[rows, 128 * p : 128 * (p + 1)])
            bottoms.append(inner_right_ref[rows, 128 * p : 128 * (p + 1)])
        blocks = jnp.concatenate(
            [
                jnp.concatenate([tops[0], nothing], axis=1),
                jnp.concatenate([bottoms[0], nothing], axis=1),
                jnp.concatenate([nothing, tops[1]], axis=1),
                jnp.concatenate([nothing, bottoms[1]], axis=1),
            ],
            axis=0,
        )
        cols = slice(256 * quad, 256 * (quad + 1))
        mixed = mm(mix, blocks)
        gated_ref[rows, cols] = (mixed * gate_ref[rows, cols]).astype(BF16)

    def walk_pair(j, carry):
        half_step(j, 0)
        half_step(j, 1)
        return carry

    for layer in range(layers):
        x = stream_ref[...]
        normed = (x * lax.rsqrt(jnp.mean(x * x, axis=-1, keepdims=True) + EPS)).astype(BF16)

        def project(q):
            cols = slice(256 * q, 256 * (q + 1))
            if layer == 0 and q < 2:
                for load in first_loads[2 * q : 2 if q == 0 else None]:
                    load.wait()
            inner = mm(normed, w_xz_ref[layer, :, cols])
            inner_left_ref[:, cols] = jnp.where(left_cols, inner, 0.0).astype(BF16)
            inner_right_ref[:, cols] = jnp.where(left_cols, 0.0, inner).astype(BF16)
            gate_cols = slice(inner_width + 256 * q, inner_width + 256 * (q + 1))
            half_gate = 0.5 * mm(normed, w_xz_ref[layer, :, gate_cols])
            gate_ref[:, cols] = half_gate + half_gate * jnp.tanh(half_gate)

        raw = mm_nt(w_dt_ref[layer], normed)
        if layer > 0:
            loads[3 * layer].wait()
        project(0)
        step = jnp.maximum(raw, 0.0) + jnp.log1p(jnp.exp(-jnp.abs(raw)))
        rate = as_column(rate_ref[layer : layer + 1, :])
        pieces = split3((-LOG2E * rate) * step).astype(BF16)
        source = jnp.where(live_row, step, 0.0)
        project(1)
        cums = []
        for j in range(walks // 2):
            lanes = slice(128 * j, 128 * (j + 1))
            sums = mm(pieces[:, lanes], running)
            sums = sums[:heads] + (sums[heads : 2 * heads] + sums[2 * heads :])
            cums.append(sums[:, :128])
            for q, v in enumerate((sums[:, :128], sums[:, 128:], source[:, lanes])):
                rows_ref[2 * q, :, lanes] = v
                rows_ref[2 * q + 1, :, lanes] = pltpu.roll(v, walk_len, 1)
        project(2)
        columns = jnp.transpose(split3(jnp.concatenate(cums, axis=1))).astype(BF16)
        project(3)
        loads[3 * layer + 1].wait()
        proj = mm(normed, w_bc_ref[layer]).astype(BF16)
        for w in range(walks):
            b_in = proj[w * walk_len : (w + 1) * walk_len, :state_width]
            c_out = proj[w * walk_len : (w + 1) * walk_len, state_width:]
            scores = mm_nt(c_out, jnp.concatenate([b_in, b_in], axis=0))
            scores_ref[w * walk_len : (w + 1) * walk_len, :] = scores * weight
        for quad in range(quads):
            wide = mm(columns, spread[:, 256 * quad : 256 * (quad + 1)])
            for w in range(walks):
                block = wide[w * walk_len : (w + 1) * walk_len, :]
                rows = slice(w * stride + PAD, (w + 1) * stride)
                cum_ref[2 * quad, rows, :] = block[:, :128]
                cum_ref[2 * quad + 1, rows, :] = block[:, 128:]

        for j in range(walks // 2):
            walk_pair(j, 0)
        loads[3 * layer + 2].wait()
        stream = x + mm(gated_ref[...], w_out_ref[layer])
        stream_ref[...] = stream.astype(BF16).astype(F32)

    load_put.wait()
    out_ref[...] = mm(put_ref[...], stream_ref[...].astype(BF16)).astype(BF16)


def encode(arrived, slots, put, w_xz, w_bc, w_dt, decay_rate, w_out, walk_len):
    total, width = arrived.shape
    tok = slots.shape[1]
    inner_width = w_out.shape[1]
    w_dt = jnp.swapaxes(w_dt, 1, 2)
    return pl.pallas_call(
        functools.partial(encode_kernel, walk_len=walk_len),
        out_shape=jax.ShapeDtypeStruct((total, width), BF16),
        in_specs=[VMEM_SPEC] * 2 + [HBM_SPEC] * 6,
        out_specs=VMEM_SPEC,
        scratch_shapes=[
            pltpu.VMEM(put.shape, BF16),
            pltpu.VMEM(w_dt.shape, BF16),
            pltpu.VMEM(decay_rate.shape, F32),
            pltpu.VMEM(w_xz.shape, BF16),
            pltpu.VMEM(w_bc.shape, BF16),
            pltpu.VMEM(w_out.shape, BF16),
            pltpu.SemaphoreType.DMA((3 + inner_width // 128,)),
            pltpu.SemaphoreType.DMA((w_out.shape[0], 3)),
            pltpu.VMEM((tok, width), F32),
            pltpu.VMEM((tok, inner_width), BF16),
            pltpu.VMEM((tok, inner_width), BF16),
            pltpu.VMEM((tok, inner_width), F32),
            pltpu.VMEM((tok, 128), F32),
            pltpu.VMEM((tok, inner_width), BF16),
            pltpu.VMEM((inner_width // 128, tok // walk_len * (walk_len + PAD), 128), F32),
            pltpu.VMEM((6, w_dt.shape[1], tok), F32),
        ],
        name="encode",
        compiler_params=pltpu.CompilerParams(
            vmem_limit_bytes=36 << 20
        ),
    )(*near_core(arrived, slots), *in_hbm(put, w_dt, decay_rate, w_xz, w_bc, w_out))


def links_kernel(place_ref, adjacency_hbm, links_ref, block_ref, load_sem):
    rows, cols = links_ref.shape
    chunks = load_sem.shape[0]
    size = rows // chunks
    loads = []
    for n in range(chunks):
        part = pl.ds(n * size, size)
        load = pltpu.make_async_copy(adjacency_hbm.at[part, :], block_ref.at[part, :], load_sem.at[n])
        load.start()
        loads.append(load)
    my_row, y, z, core = place_ref[0], place_ref[1], place_ref[2], place_ref[3]
    first_row = ((y * SIDE + z) * CORES + core) * rows
    offset = first_row - my_row * cols
    for n in range(chunks):
        loads[n].wait()
        diagonal = iota((size, cols), 1) - iota((size, cols), 0) == offset + n * size
        block = block_ref[n * size : (n + 1) * size, :] + diagonal.astype(I32)
        links_ref[n * size : (n + 1) * size, :] = block.astype(F32).astype(BF16)


def make_links(place, adjacency):
    chunks = 6
    return pl.pallas_call(
        links_kernel,
        out_shape=jax.ShapeDtypeStruct(adjacency.shape, BF16),
        in_specs=[SMEM_SPEC, HBM_SPEC],
        out_specs=VMEM_SPEC,
        scratch_shapes=[pltpu.VMEM(adjacency.shape, I32), pltpu.SemaphoreType.DMA((chunks,))],
        name="links",
        compiler_params=pltpu.CompilerParams(vmem_limit_bytes=16 << 20),
    )(place, *in_hbm(adjacency))


def update_kernel(returned_ref, reqrow_ref, states_ref, out_ref):
    node_count = states_ref.shape[0]
    total = returned_ref.shape[0]
    member = jnp.where(iota((node_count, total), 0) == reqrow_ref[0:1, :], 1.0, 0.0)
    visits = jnp.sum(member, axis=1, keepdims=True)
    summed = mm(member.astype(BF16), returned_ref[...])
    out_ref[...] = (states_ref[...].astype(F32) + summed / (1.0 + visits)).astype(BF16)


def update_nodes(returned, reqrow, node_states):
    return pl.pallas_call(
        update_kernel,
        out_shape=jax.ShapeDtypeStruct(node_states.shape, BF16),
        in_specs=[VMEM_SPEC] * 3,
        out_specs=VMEM_SPEC,
        name="update",
        compiler_params=pltpu.CompilerParams(vmem_limit_bytes=12 << 20),
    )(*near_core(returned, reqrow, node_states))


def finish_kernel(own_ref, one_ref, two_ref, three_ref, w_up_ref, w_down_ref, out_ref):
    combined = (own_ref[...] + one_ref[...].astype(F32)) + (
        two_ref[...].astype(F32) + three_ref[...].astype(F32)
    )
    centred = combined - jnp.mean(combined, axis=-1, keepdims=True)
    normal = centred * lax.rsqrt(jnp.mean(centred * centred, axis=-1, keepdims=True) + EPS)
    hidden = jax.nn.gelu(mm(normal.astype(BF16), w_up_ref[...])).astype(BF16)
    out_ref[...] = (normal + mm(hidden, w_down_ref[...])).astype(BF16)


def finish(own, parts, w_up, w_down):
    return pl.pallas_call(
        finish_kernel,
        out_shape=jax.ShapeDtypeStruct(own.shape, BF16),
        in_specs=[VMEM_SPEC] * 6,
        out_specs=VMEM_SPEC,
        name="finish",
        compiler_params=pltpu.CompilerParams(vmem_limit_bytes=12 << 20),
    )(own, *near_core(*parts, w_up, w_down))


def neighbour_kernel(place_ref, links_ref, *refs):
    mine, other = refs[:SIDE], refs[SIDE : 2 * SIDE]
    own_ref, one_ref, two_ref, three_ref, piece_ref, sums_ref = refs[2 * SIDE :]
    my_row, y, z, core = place_ref[0], place_ref[1], place_ref[2], place_ref[3]
    rows = mine[0].shape[0] // SIDE
    for e in range(SIDE):
        for d in range(SIDE):
            for ref, who in ((mine[e], core), (other[e], 1 - core)):
                dy = d + who * (e - d)
                dz = e + who * (d - e)
                device = ((y + SIDE - dy) % SIDE * SIDE + (z + SIDE - dz) % SIDE) * CORES + who
                target = pl.multiple_of(device * rows, rows)
                piece_ref[pl.ds(target, rows), :] = ref[d * rows : (d + 1) * rows, :]
    sums_ref[...] = mm(links_ref[...], piece_ref[...])
    part = own_ref.shape[0]

    def block(distance):
        start = pl.multiple_of((my_row + distance) % SIDE * part, part)
        return sums_ref[pl.ds(start, part), :]

    own_ref[...] = block(0)
    one_ref[...] = block(1).astype(BF16)
    two_ref[...] = block(2).astype(BF16)
    three_ref[...] = block(3).astype(BF16)


def neighbour_sums(place, links, mine, other):
    row_block, width = links.shape[0], mine[0].shape[1]
    part = row_block // SIDE
    sent = jax.ShapeDtypeStruct((part, width), BF16)
    return pl.pallas_call(
        neighbour_kernel,
        out_shape=(jax.ShapeDtypeStruct((part, width), F32), sent, sent, sent),
        in_specs=[SMEM_SPEC] + [VMEM_SPEC] * (1 + 2 * SIDE),
        out_specs=(VMEM_SPEC,) * 4,
        scratch_shapes=[
            pltpu.VMEM((links.shape[1], width), BF16),
            pltpu.VMEM((row_block, width), F32),
        ],
        name="neighbours",
        compiler_params=pltpu.CompilerParams(vmem_limit_bytes=16 << 20),
    )(place, *near_core(links, *mine, *other))


def shifted(value, first, second, swap=0):
    pairs = []
    for y in range(SIDE):
        for z in range(SIDE):
            for c in range(CORES):
                dy, dz = (first, second) if c == 0 else (second, first)
                to = ((y + dy) % SIDE * SIDE + (z + dz) % SIDE) * CORES + (c + swap) % CORES
                pairs.append(((y * SIDE + z) * CORES + c, to))
    return lax.ppermute(value, "col", pairs)


def gather_blocks(update):
    near = [update] + [shifted(update, d, 0) for d in range(1, SIDE)]
    near = jnp.concatenate(near, axis=0)
    far = [near] + [shifted(near, 0, d) for d in range(1, SIDE)]
    return far, [shifted(block, 0, 0, swap=1) for block in far]


def assemble_kernel(place_ref, *refs):
    blocks, out_hbm, store_sem = refs[:-2], refs[-2], refs[-1]
    part = blocks[0].shape[0]
    stores = []
    for d, block_ref in enumerate(blocks):
        start = pl.multiple_of((place_ref[0] + len(blocks) - d) % len(blocks) * part, part)
        store = pltpu.make_async_copy(block_ref, out_hbm.at[pl.ds(start, part), :], store_sem.at[d])
        store.start()
        stores.append(store)
    for store in stores:
        store.wait()


def assemble(place, done, moved):
    rows, width = done.shape
    return pl.pallas_call(
        assemble_kernel,
        out_shape=jax.ShapeDtypeStruct((rows * (1 + len(moved)), width), BF16),
        in_specs=[SMEM_SPEC] + [VMEM_SPEC] * (1 + len(moved)),
        out_specs=HBM_SPEC,
        scratch_shapes=[pltpu.SemaphoreType.DMA((1 + len(moved),))],
        name="assemble",
        compiler_params=pltpu.CompilerParams(vmem_limit_bytes=8 << 20),
    )(place, *near_core(done, *moved))


def ring(size, distance):
    return [(i, (i + distance) % size) for i in range(size)]


def per_device(
    node_states,
    walk_nodes,
    walk_lengths,
    adjacency,
    w_xz,
    w_bc,
    w_dt,
    decay_rate,
    w_out,
    w_up,
    w_down,
):
    node_count, width = node_states.shape
    walk_count, walk_len = walk_nodes.shape
    everyone = ("row", "col")
    owners = lax.axis_size(everyone)
    row_size = lax.axis_size("row")
    row_block = adjacency.shape[0]

    my_row = lax.axis_index("row")
    my_col = lax.axis_index("col")
    place = jnp.stack([my_row, my_col // (SIDE * CORES), my_col // CORES % SIDE, my_col % CORES]).astype(I32)
    wanted, slots = route(walk_nodes, walk_lengths, node_count, owners)
    requests = lax.all_to_all(wanted, everyone, split_axis=0, concat_axis=0, tiled=True)
    requests, near_states, place = lax.optimization_barrier((requests, fetch(node_states)[0], place))
    picked, reqrow = pick(requests, near_states)
    arrived = lax.all_to_all(
        picked.reshape(owners, CAP, width), everyone, split_axis=0, concat_axis=0, tiled=True
    )
    links = make_links(place, adjacency)
    put = placement(slots, owners * CAP)
    arrived, links, put = lax.optimization_barrier((arrived, links, put))
    outgoing = encode(
        arrived.reshape(owners * CAP, width),
        slots,
        put,
        w_xz,
        w_bc,
        w_dt,
        decay_rate,
        w_out,
        walk_len,
    )
    returned = lax.all_to_all(
        outgoing.reshape(owners, CAP, width), everyone, split_axis=0, concat_axis=0, tiled=True
    )
    update = update_nodes(returned.reshape(owners * CAP, width), reqrow, near_states)

    mine, other = gather_blocks(update)
    own, *sent = neighbour_sums(place, links, mine, other)
    parts = [lax.ppermute(block, "row", ring(row_size, d)) for d, block in enumerate(sent, 1)]
    own, w_up, w_down = lax.optimization_barrier((own, w_up, w_down))
    done = finish(own, parts, *fetch(w_up, w_down))
    moved = [lax.ppermute(done, "row", ring(row_size, d)) for d in range(1, row_size)]
    return assemble(place, done, moved)


def solution(mesh):
    return jax.shard_map(
        per_device,
        mesh=mesh,
        in_specs=(
            P(("row", "col"), None),
            P(("row", "col"), None),
            P(("row", "col")),
            P("col", "row"),
            P(),
            P(),
            P(),
            P(),
            P(),
            P(),
            P(),
        ),
        out_specs=P("col", None),
        check_vma=False,
    )
```
